32 devices in a mesh: alpha: 8 (over z, x), beta: 4 (over y, core).
Axes of the slice: x: 2, y: 2, z: 4, core: 2. Of those that a mesh axis runs over, the one named last changes fastest.
Arguments:
- coeffs: bfloat16 [2048, 4096], P('alpha', 'beta'), may hold values from -6 to 6
- a_blocks: bfloat16 [2, 2048, 11, 128], P(None, 'alpha'), may hold values from -0.15625 to 0.15625
- a_list: int32 [2, 16, 11], replicated, may hold values from 0 to 15, as said below
- a_count: int32 [2, 16], replicated, may hold values from 4 to 11, as said below
- b_blocks: bfloat16 [2, 4096, 11, 128], P(None, 'beta'), may hold values from -0.15625 to 0.15625
- b_list: int32 [2, 32, 11], replicated, may hold values from 0 to 31, as said below
- b_count: int32 [2, 32], replicated, may hold values from 4 to 11, as said below
Outputs:
- sigma: float32 [2048, 4096], P('alpha', 'beta')
The draws below stay inside these ranges and needn't reach their ends.
Inputs may be any that keep to these rules, and one draw needn't show every extreme that they name: `a_list`: every entry, valid slot or not, is an alpha block number. For each index r of alpha and each index o of alpha, the entries of all operators in the rows of blocks r * 2 to r * 2 + 1 that lie in blocks o * 2 to o * 2 + 1 name at most 1 distinct blocks, and some pair names exactly 1. `b_list`: the same with beta, 8 and 2. `a_count`: some row has all 11 slots valid. `b_count`: some row has all 11 slots valid.
All inputs are finite; a program needn't handle non-finite values.
Results may differ from the reference program's by a relative error of at most 0.0029.
Values may be sent and summed in bfloat16 or wider, within the bound.
A program may use at most 128 MiB of HBM per device.

```python
import jax
import jax.numpy as jnp
from jax import lax

BLOCK = 128
ABLK_DEV = 2
BBLK_DEV = 8
LIST = 11
OPS = 2
NA = 2048
NB = 4096
FROM_A = 1
FROM_B = 2
N_ALPHA = 8
N_BETA = 4


def listed_blocks(key, owners, per_owner, capacity):
    score_key = jax.random.fold_in(key, 101)
    pick_key = jax.random.fold_in(key, 202)
    scores = jax.random.randint(score_key, (owners, owners, per_owner), 0, 1 << 20)
    scores = scores * per_owner + jnp.arange(per_owner, dtype=jnp.int32)
    ordering = jnp.argsort(scores, axis=-1, stable=True)[..., :capacity].astype(jnp.int32)
    allowed = ordering + (jnp.arange(owners, dtype=jnp.int32) * per_owner)[None, :, None]
    allowed = allowed.reshape(owners, owners * capacity)
    picks = jax.random.randint(pick_key, (OPS, owners, per_owner, LIST), 0, owners * capacity)
    receivers = jnp.arange(owners, dtype=jnp.int32)[None, :, None, None]
    entries = allowed[receivers, picks]
    entries = entries.at[0, 0, 0, :capacity].set(allowed[0, :capacity])
    return entries.reshape(OPS, owners * per_owner, LIST).astype(jnp.int32)


def valid_counts(key, total):
    counts = jax.random.randint(key, (OPS, total), LIST // 3 + 1, LIST + 1)
    return counts.at[0, 0].set(LIST).astype(jnp.int32)


def draw_a_list(key, part):
    return listed_blocks(jax.random.fold_in(key, 11), N_ALPHA, ABLK_DEV, FROM_A)


def draw_b_list(key, part):
    return listed_blocks(jax.random.fold_in(key, 12), N_BETA, BBLK_DEV, FROM_B)


def draw_a_count(key, part):
    return valid_counts(jax.random.fold_in(key, 21), ABLK_DEV * N_ALPHA)


def draw_b_count(key, part):
    return valid_counts(jax.random.fold_in(key, 22), BBLK_DEV * N_BETA)


def level_of(own_key, dims, cuts, low, high):
    level, own = 1.0, jax.random.fold_in(own_key, 6)
    for position, blocks in cuts:
        steps = jnp.exp(jax.random.uniform(jax.random.fold_in(own, position), (blocks,), jnp.float32, low / len(cuts), high / len(cuts)))
        level = level * jnp.repeat(steps, dims[position] // blocks).reshape([-1 if axis == position else 1 for axis in range(len(dims))])
    return level


def centred(stream_key, dims, deviation, reach, cuts=(), kind=jnp.bfloat16):
    drawn = jax.random.normal(stream_key, dims, jnp.float32) * deviation
    if len(cuts) > 0:
        drawn = level_of(stream_key, dims, cuts, -0.22, 0.18) * drawn
    return jnp.clip(drawn, min=-reach, max=reach).astype(kind)


def setup_inputs(seed: int = 0) -> dict:
    seeds = jax.random.split(jax.random.key(seed), 8)
    coeffs = centred(seeds[0], (NA, NB), 1.0, 6.0, ((0, 8), (1, 4)))
    a_blocks = centred(seeds[1], (OPS, NA, LIST, BLOCK), (LIST * BLOCK) ** -0.5, 0.15625, ((1, 8),))
    a_list = draw_a_list(jax.random.fold_in(seeds[7], 71), 0)
    a_count = draw_a_count(jax.random.fold_in(seeds[7], 71), 0)
    b_blocks = centred(seeds[4], (OPS, NB, LIST, BLOCK), (LIST * BLOCK) ** -0.5, 0.15625, ((1, 4),))
    b_list = draw_b_list(jax.random.fold_in(seeds[7], 71), 0)
    b_count = draw_b_count(jax.random.fold_in(seeds[7], 71), 0)
    return {"coeffs": coeffs, "a_blocks": a_blocks, "a_list": a_list, "a_count": a_count, "b_blocks": b_blocks, "b_list": b_list, "b_count": b_count}


def reference(coeffs, a_blocks, a_list, a_count, b_blocks, b_list, b_count):
    operators, alpha_total, list_slots, block_size = a_blocks.shape
    beta_total = coeffs.shape[1]
    alpha_nblk = alpha_total // block_size
    beta_nblk = beta_total // block_size
    slot_ids = jnp.arange(list_slots, dtype=jnp.int32)
    coeff_blocks = coeffs.reshape(alpha_nblk, block_size, beta_total)
    sigma = jnp.zeros((alpha_total, beta_total), jnp.float32)
    for k in range(operators):
        alpha_valid = slot_ids[None, :] < a_count[k][:, None]
        alpha_kept = jnp.where(alpha_valid[:, None, :, None], a_blocks[k].reshape(alpha_nblk, block_size, list_slots, block_size), jnp.zeros((), a_blocks.dtype))

        def row_block(pair):
            factor_rows, entries = pair
            picked = coeff_blocks[entries.astype(jnp.int32)].reshape(list_slots * block_size, beta_total)
            return jnp.dot(factor_rows.reshape(block_size, list_slots * block_size), picked, preferred_element_type=jnp.float32)

        inter = lax.map(row_block, (alpha_kept, a_list[k]))
        inter = inter.reshape(alpha_total, beta_total).astype(jnp.bfloat16)
        inter_cols = inter.reshape(alpha_total, beta_nblk, block_size)
        beta_valid = slot_ids[None, :] < b_count[k][:, None]
        beta_kept = jnp.where(beta_valid[:, None, :, None], b_blocks[k].reshape(beta_nblk, block_size, list_slots, block_size), jnp.zeros((), b_blocks.dtype))

        def col_block(pair):
            factor_rows, entries = pair
            picked = inter_cols[:, entries.astype(jnp.int32), :].reshape(alpha_total, list_slots * block_size)
            return jnp.dot(picked, factor_rows.reshape(block_size, list_slots * block_size).T, preferred_element_type=jnp.float32)

        partial_sigma = lax.map(col_block, (beta_kept, b_list[k]))
        sigma = sigma + jnp.transpose(partial_sigma, (1, 0, 2)).reshape(alpha_total, beta_total)
    return sigma
```

```python
import functools

import jax
import jax.numpy as jnp
from jax import lax
from jax.experimental import pallas as pl
from jax.experimental.pallas import tpu as pltpu
from jax.sharding import PartitionSpec as P

FROM_A = 1
FROM_B = 2
PAIR = 2
VMEM_LIMIT = 60 * 1024 * 1024
MESH = pl.DeviceIdType.MESH


def sigma_kernel(geometry, a_lists, a_counts, b_lists, b_counts, a_vec, b_vec, c_hbm, a_hbm, b_hbm, out_ref, cbuf, abuf, bbuf, picks, column, across, chosen,
                 adense, bdense, acc, small, local_sem, beta_send, beta_recv, column_recv, up_send, down_send, across_send, across_recv):
    na, nb, ops, slots, blk, row_blocks, col_blocks = geometry
    levels = na // PAIR
    rows = row_blocks * blk
    wide = FROM_B * blk
    a = lax.axis_index("alpha")
    c = lax.axis_index("beta")
    z = a // PAIR
    x = a % PAIR
    partner = a + 1 - 2 * x

    copies_c = [pltpu.make_async_copy(c_hbm.at[:, b * blk:(b + 1) * blk], cbuf.at[b], local_sem.at[2 + b]) for b in range(col_blocks)]
    copy_a = pltpu.make_async_copy(a_hbm, abuf, local_sem.at[0])
    copy_b = pltpu.make_async_copy(b_hbm, bbuf, local_sem.at[1])
    for copy in copies_c:
        copy.start()
    copy_a.start()
    copy_b.start()

    barrier = pltpu.get_barrier_semaphore()
    for j in range(1, nb):
        pl.semaphore_signal(barrier, inc=1, device_id={"beta": c ^ j}, device_id_type=MESH)
    pl.semaphore_signal(barrier, inc=1, device_id={"alpha": partner}, device_id_type=MESH)

    @pl.when(z < levels - 1)
    def _():
        pl.semaphore_signal(barrier, inc=1, device_id={"alpha": a + PAIR}, device_id_type=MESH)

    @pl.when(z > 0)
    def _():
        pl.semaphore_signal(barrier, inc=1, device_id={"alpha": a - PAIR}, device_id_type=MESH)

    lists = b_vec[...]
    lane = lax.broadcasted_iota(jnp.int32, (1, nb * col_blocks), 1)

    def extremes(receiver, owner):
        local = lists - owner * col_blocks
        hit = (local >= 0) & (local < col_blocks)
        rows_here = (lane >= receiver * col_blocks) & (lane < (receiver + 1) * col_blocks)
        low = jnp.min(jnp.min(jnp.where(hit, local, col_blocks), axis=0), axis=0, keepdims=True)
        high = jnp.max(jnp.max(jnp.where(hit, local, 0), axis=0), axis=0, keepdims=True)
        low = jnp.min(jnp.where(rows_here, low, col_blocks))
        high = jnp.max(jnp.where(rows_here, high, 0))
        return jnp.where(low < col_blocks, low, 0), high

    spans = [extremes(c ^ j, c) for j in range(nb)]
    for copy in copies_c:
        copy.wait()
    for j in range(nb):
        for u, block in enumerate(spans[j]):
            piece = cbuf[block]
            if j == 0:
                column[z, 0, :, u * blk:(u + 1) * blk] = piece
            else:
                picks[j - 1, :, u * blk:(u + 1) * blk] = piece

    rows_list = a_vec[...]
    row_lane = lax.broadcasted_iota(jnp.int32, (1, na * row_blocks), 1)

    def row_pick(receiver, owner):
        local = rows_list - owner * row_blocks
        hit = (local >= 0) & (local < row_blocks)
        rows_here = (row_lane >= receiver * row_blocks) & (row_lane < (receiver + 1) * row_blocks)
        high = jnp.max(jnp.max(jnp.where(hit, local, 0), axis=0), axis=0, keepdims=True)
        return jnp.max(jnp.where(rows_here, high, 0))

    for lev in range(levels):
        small[lev] = row_pick(a, lev * PAIR + x)
        small[levels + lev] = row_pick(partner, lev * PAIR + x)
    for owner in range(nb):
        small[2 * levels + owner] = extremes(c, owner)[0]

    neighbours = nb + jnp.where(z < levels - 1, 1, 0) + jnp.where(z > 0, 1, 0)
    pl.semaphore_wait(barrier, neighbours)

    def beta_copy(j):
        return pltpu.make_async_remote_copy(
            src_ref=picks.at[j - 1], dst_ref=column.at[z, j], send_sem=beta_send.at[j - 1], recv_sem=beta_recv.at[j - 1],
            device_id={"beta": c ^ j}, device_id_type=MESH)

    def up_copy(lev, j):
        return pltpu.make_async_remote_copy(
            src_ref=column.at[lev, j], dst_ref=column.at[lev, j], send_sem=up_send.at[lev, j], recv_sem=column_recv.at[lev, j],
            device_id={"alpha": a + PAIR}, device_id_type=MESH)

    def down_copy(lev, j):
        return pltpu.make_async_remote_copy(
            src_ref=column.at[lev, j], dst_ref=column.at[lev, j], send_sem=down_send.at[lev, j], recv_sem=column_recv.at[lev, j],
            device_id={"alpha": a - PAIR}, device_id_type=MESH)

    def across_copy(lev, j):
        return pltpu.make_async_remote_copy(
            src_ref=chosen.at[lev, j], dst_ref=across.at[lev, j], send_sem=across_send.at[lev, j], recv_sem=across_recv.at[lev, j],
            device_id={"alpha": partner}, device_id_type=MESH)

    def one_hot(value, place):
        gap = value - place
        return (1 - jnp.minimum(jnp.maximum(gap, -gap), 1)).astype(jnp.float32)

    def at_most(slot, count):
        return jnp.minimum(jnp.maximum(count - slot, 0), 1)

    def selected(lev, j, pick):
        total = jnp.zeros((blk, wide), jnp.float32)
        for i in range(row_blocks):
            total += column[lev, j, i * blk:(i + 1) * blk, :].astype(jnp.float32) * one_hot(pick, i)
        return total.astype(jnp.bfloat16)

    def offer(lev, j):
        chosen[lev, j] = selected(lev, j, small[levels + lev])
        across_copy(lev, j).start()

    def own_sends(j):
        @pl.when(z < levels - 1)
        def _():
            up_copy(z, j).start()

        @pl.when(z > 0)
        def _():
            down_copy(z, j).start()

        offer(z, j)

    own_sends(0)
    for j in range(1, nb):
        beta_copy(j).start()

    tall = 32

    def dense(load, codes, places, put):
        def tile(t, carry):
            here = pl.multiple_of(t * tall, tall)
            totals = [jnp.zeros((tall, blk), jnp.float32) for _ in range(places)]
            for s in range(slots):
                value = load(s, here)
                for p in range(places):
                    totals[p] += value * one_hot(codes[s], p)
            for p in range(places):
                high = totals[p].astype(jnp.bfloat16)
                put(p, here, high, (totals[p] - high.astype(jnp.float32)).astype(jnp.bfloat16))
            return carry

        lax.fori_loop(0, blk // tall, tile, 0)

    def build_a(piece):
        k = piece // row_blocks
        i = piece % row_blocks
        codes = []
        for s in range(slots):
            entry = a_lists[s, k, a * row_blocks + i]
            owner = lax.div(entry, row_blocks)
            upper = owner - 2 * lax.div(owner, 2)
            place = owner - upper + jnp.maximum(upper - x, x - upper)
            codes.append((place + 1) * at_most(s, a_counts[k, a * row_blocks + i]) - 1)

        def load(s, here):
            return abuf[k, s, pl.ds(i * blk + here, tall), :].astype(jnp.float32)

        def put(p, here, high, low):
            at = pl.ds(k * rows + i * blk + here, tall)
            side = p % PAIR
            adense[p // PAIR, 0, at, side * blk:(side + 1) * blk] = high
            adense[p // PAIR, 1, at, side * blk:(side + 1) * blk] = low

        dense(load, codes, na, put)

    def build_b(piece):
        k = piece // col_blocks
        r = piece % col_blocks
        codes = []
        for s in range(slots):
            entry = b_lists[s, k, c * col_blocks + r]
            owner = lax.div(entry, col_blocks)
            gap = entry - owner * col_blocks - small[2 * levels + owner]
            place = (owner ^ c) * FROM_B + jnp.minimum(jnp.maximum(gap, -gap), 1)
            codes.append((place + 1) * at_most(s, b_counts[k, c * col_blocks + r]) - 1)

        def load(s, here):
            return bbuf[k, s, pl.ds(r * blk + here, tall), :].astype(jnp.float32)

        def put(p, here, high, low):
            at = pl.ds(r * blk + here, tall)
            u = p % FROM_B
            bdense[p // FROM_B, 0, k, at, u * blk:(u + 1) * blk] = high
            bdense[p // FROM_B, 1, k, at, u * blk:(u + 1) * blk] = low

        dense(load, codes, nb * FROM_B, put)

    a_pieces = ops * row_blocks
    pieces = ops * col_blocks

    def build_some(first, count):
        def one(n, carry):
            @pl.when(n < pieces)
            def _():
                build_b(n)
            return carry

        lax.fori_loop(first, first + count, one, 0)

    def beta_wait(j):
        pltpu.make_async_remote_copy(
            src_ref=picks.at[j - 1], dst_ref=column.at[z, j], send_sem=beta_send.at[j - 1], recv_sem=beta_recv.at[j - 1],
            device_id={"beta": c ^ j}, device_id_type=MESH).wait_recv()

    acc[...] = jnp.zeros_like(acc)
    out_ref[...] = jnp.zeros_like(out_ref)
    copy_a.wait()

    def one_a(n, carry):
        build_a(n)
        return carry

    lax.fori_loop(0, a_pieces // 2, one_a, 0)
    built = 0
    for j in range(1, nb):
        beta_wait(j)
        own_sends(j)
        if j == 1:
            lax.fori_loop(a_pieces // 2, a_pieces, one_a, 0)
            copy_b.wait()
        build_some(built, 3)
        built += 3

    def combine(lev, j):
        across_copy(lev, j).wait_recv()
        value = jnp.concatenate([selected(lev, j, small[lev]), across[lev, j]], axis=0)
        acc[j] += (jnp.dot(adense[lev, 0], value, preferred_element_type=jnp.float32)
                   + jnp.dot(adense[lev, 1], value, preferred_element_type=jnp.float32))

    tile = min(2, col_blocks) * blk

    def finish(j):
        inters = [acc[j, k * rows:(k + 1) * rows, :].astype(jnp.bfloat16) for k in range(ops)]

        def columns(n, carry):
            here = pl.ds(pl.multiple_of(n * tile, tile), tile)
            total = out_ref[:, here]
            for k in range(ops):
                for half in range(2):
                    total += lax.dot_general(inters[k], bdense[j, half, k, here, :], (((1,), (1,)), ((), ())),
                                             preferred_element_type=jnp.float32)
            out_ref[:, here] = total
            return carry

        lax.fori_loop(0, col_blocks * blk // tile, columns, 0)

    steps = (levels - 1) * nb
    farthest = jnp.maximum(z, levels - 1 - z)

    def arrive(lev, j, below):
        pltpu.make_async_remote_copy(
            src_ref=column.at[lev, j], dst_ref=column.at[lev, j], send_sem=up_send.at[lev, j], recv_sem=column_recv.at[lev, j],
            device_id={"alpha": partner}, device_id_type=MESH).wait_recv()
        if below:
            @pl.when(z < levels - 1)
            def _():
                up_copy(lev, j).start()
        else:
            @pl.when(z > 0)
            def _():
                down_copy(lev, j).start()

        offer(lev, j)

    def step(i, carry):
        j = i % nb
        distance = i // nb + 1

        @pl.when((i < steps) & (z - distance >= 0))
        def _():
            arrive(z - distance, j, True)

        @pl.when((i < steps) & (z + distance < levels))
        def _():
            arrive(z + distance, j, False)

        @pl.when(i < nb)
        def _():
            combine(z, j)

        before = jnp.maximum(i - 1, 0)
        j_before = before % nb
        distance_before = before // nb + 1

        @pl.when((i > 0) & (z - distance_before >= 0))
        def _():
            combine(z - distance_before, j_before)

        @pl.when((i > 0) & (z + distance_before < levels))
        def _():
            combine(z + distance_before, j_before)

        done = i - 1 - (farthest - 1) * nb
        build_some(built + 2 * i, 2)

        @pl.when((done >= 0) & (done < nb))
        def _():
            finish(done)

        return carry

    lax.fori_loop(0, steps + 1, step, 0)

    for j in range(1, nb):
        beta_copy(j).wait_send()

    def drain(n, carry):
        lev = n // nb
        j = n % nb

        @pl.when((lev <= z) & (z < levels - 1))
        def _():
            up_copy(lev, j).wait_send()

        @pl.when((lev >= z) & (z > 0))
        def _():
            down_copy(lev, j).wait_send()

        across_copy(lev, j).wait_send()
        return carry

    lax.fori_loop(0, levels * nb, drain, 0)


def scratch_of(geometry, dtype):
    na, nb, ops, slots, blk, row_blocks, col_blocks = geometry
    levels = na // PAIR
    rows, cols, wide = row_blocks * blk, col_blocks * blk, FROM_B * blk
    return [
        ((col_blocks, rows, blk), dtype),
        ((ops, slots, rows, blk), dtype),
        ((ops, slots, cols, blk), dtype),
        ((nb - 1, rows, wide), dtype),
        ((levels, nb, rows, wide), dtype),
        ((levels, nb, blk, wide), dtype),
        ((levels, nb, blk, wide), dtype),
        ((levels, 2, ops * rows, PAIR * blk), dtype),
        ((nb, 2, ops, cols, wide), dtype),
        ((nb, ops * rows, wide), jnp.float32),
    ]


def scratch_bytes(geometry):
    total = 0
    for shape, dtype in scratch_of(geometry, jnp.bfloat16):
        size = jnp.dtype(dtype).itemsize
        for extent in shape:
            size *= extent
        total += size
    return total


def fused(geometry, coeffs, a_blocks, a_list, a_count, b_blocks, b_list, b_count):
    na, nb, ops, slots, blk, row_blocks, col_blocks = geometry
    levels = na // PAIR
    a_lists = jnp.transpose(a_list, (2, 0, 1))
    b_lists = jnp.transpose(b_list, (2, 0, 1))
    rows, cols = row_blocks * blk, col_blocks * blk
    dma = pltpu.SemaphoreType.DMA
    smem = pl.BlockSpec(memory_space=pltpu.SMEM)
    vmem = pl.BlockSpec(memory_space=pltpu.VMEM)
    return pl.pallas_call(
        functools.partial(sigma_kernel, geometry),
        out_shape=jax.ShapeDtypeStruct((rows, cols), jnp.float32),
        in_specs=[
            smem, smem, smem, smem, vmem, vmem,
            pl.BlockSpec(memory_space=pl.ANY),
            pl.BlockSpec(memory_space=pl.ANY),
            pl.BlockSpec(memory_space=pl.ANY),
        ],
        out_specs=pl.BlockSpec(memory_space=pltpu.VMEM),
        scratch_shapes=[pltpu.VMEM(shape, dtype) for shape, dtype in scratch_of(geometry, coeffs.dtype)] + [
            pltpu.SMEM((2 * levels + nb,), jnp.int32),
            dma((2 + col_blocks,)), dma((nb - 1,)), dma((nb - 1,)), dma((levels, nb)), dma((levels, nb)), dma((levels, nb)),
            dma((levels, nb)), dma((levels, nb)),
        ],
        compiler_params=pltpu.CompilerParams(collective_id=0, has_side_effects=True, vmem_limit_bytes=VMEM_LIMIT),
        name="sigma_build",
    )(a_lists, a_count, b_lists, b_count, a_lists, b_lists, coeffs, jnp.transpose(a_blocks, (0, 2, 1, 3)), jnp.transpose(b_blocks, (0, 2, 1, 3)))


def arrange(entries, owners, per_owner, capacity):
    operators, total, list_slots = entries.shape
    flattened = entries.reshape(operators, owners, per_owner * list_slots)
    matches = flattened[..., None] == jnp.arange(total, dtype=jnp.int32)
    present = jnp.any(matches, axis=(0, 2)).reshape(owners, owners, per_owner).astype(jnp.int32)
    ranking = jnp.cumsum(present, axis=2)
    position = jnp.arange(capacity, dtype=jnp.int32) + 1
    chosen_bits = (present[..., None] == 1) & (ranking[..., None] == position)
    local_ids = jnp.arange(per_owner, dtype=jnp.int32)[None, None, :, None]
    wanted = jnp.sum(local_ids * chosen_bits.astype(jnp.int32), axis=2)
    return (wanted, ranking)


def locate(entries, ranking_here, per_owner, capacity):
    owner = entries // per_owner
    local_id = entries % per_owner
    return owner * capacity + ranking_here[owner, local_id] - 1


def pick_columns(pool_piece, index_piece):
    return pool_piece[:, index_piece]


def plain(coeffs, a_blocks, a_list, a_count, b_blocks, b_list, b_count):
    operators, local_rows, list_slots, block_size = a_blocks.shape
    local_cols = coeffs.shape[1]
    row_blocks = local_rows // block_size
    col_blocks = local_cols // block_size
    row_capacity = FROM_A
    col_capacity = FROM_B
    alpha_size = lax.axis_size("alpha")
    beta_size = lax.axis_size("beta")
    alpha_here = lax.axis_index("alpha")
    beta_here = lax.axis_index("beta")
    slot_ids = jnp.arange(list_slots, dtype=jnp.int32)
    alpha_mine = lax.dynamic_slice_in_dim(a_list, alpha_here * row_blocks, row_blocks, 1)
    alpha_counts = lax.dynamic_slice_in_dim(a_count, alpha_here * row_blocks, row_blocks, 1)
    alpha_valid = slot_ids < alpha_counts[..., None]
    alpha_kept = jnp.where(
        alpha_valid[:, :, None, :, None],
        a_blocks.reshape(operators, row_blocks, block_size, list_slots, block_size),
        jnp.zeros((), jnp.bfloat16),
    )
    wanted, ranking = arrange(a_list, alpha_size, row_blocks, row_capacity)
    outgoing = coeffs.reshape(row_blocks, block_size, local_cols)[wanted[:, alpha_here, :]]
    incoming = lax.all_to_all(outgoing, "alpha", split_axis=0, concat_axis=0, tiled=True)
    source_index = locate(alpha_mine, ranking[alpha_here], row_blocks, row_capacity)
    chosen = incoming.reshape(alpha_size * row_capacity, block_size, local_cols)[source_index]
    inter = jnp.einsum("kbrsi,kbsic->kbrc", alpha_kept, chosen, preferred_element_type=jnp.float32)
    inter = inter.astype(jnp.bfloat16).reshape(operators, local_rows, col_blocks, block_size)
    wanted_cols, ranking_cols = arrange(b_list, beta_size, col_blocks, col_capacity)
    outgoing_cols = inter[:, :, wanted_cols[:, beta_here, :], :]
    incoming_cols = lax.all_to_all(outgoing_cols, "beta", split_axis=2, concat_axis=2, tiled=True)
    beta_mine = lax.dynamic_slice_in_dim(b_list, beta_here * col_blocks, col_blocks, 1)
    beta_counts = lax.dynamic_slice_in_dim(b_count, beta_here * col_blocks, col_blocks, 1)
    beta_valid = slot_ids < beta_counts[..., None]
    beta_kept = jnp.where(
        beta_valid[:, :, None, :, None],
        b_blocks.reshape(operators, col_blocks, block_size, list_slots, block_size),
        jnp.zeros((), jnp.bfloat16),
    )
    source_cols = locate(beta_mine, ranking_cols[beta_here], col_blocks, col_capacity)
    pooled = incoming_cols.reshape(operators, local_rows, beta_size * col_capacity, block_size)
    picked = jax.vmap(pick_columns)(pooled, source_cols)
    sigma = jnp.einsum("kabsj,kbrsj->abr", picked, beta_kept, preferred_element_type=jnp.float32)
    return sigma.reshape(local_rows, local_cols)


def on_device(coeffs, a_blocks, a_list, a_count, b_blocks, b_list, b_count):
    operators, local_rows, list_slots, block_size = a_blocks.shape
    na, nb = lax.axis_size("alpha"), lax.axis_size("beta")
    geometry = (na, nb, operators, list_slots, block_size, local_rows // block_size, coeffs.shape[1] // block_size)
    fits = scratch_bytes(geometry) < VMEM_LIMIT * 3 // 4
    shaped = FROM_A == 1 and FROM_B == 2 and na % PAIR == 0 and na > PAIR and nb & (nb - 1) == 0 and nb > 1
    build = functools.partial(fused, geometry) if fits and shaped else plain
    return build(coeffs, a_blocks, a_list, a_count, b_blocks, b_list, b_count)


def solution(mesh):
    in_specs = (
        P("alpha", "beta"),
        P(None, "alpha", None, None),
        P(),
        P(),
        P(None, "beta", None, None),
        P(),
        P(),
    )
    out_specs = P("alpha", "beta")
    return jax.shard_map(
        on_device, mesh=mesh, in_specs=in_specs, out_specs=out_specs, check_vma=False
    )
```

```python
import functools

import jax
import jax.numpy as jnp
from jax import lax
from jax.experimental import pallas as pl
from jax.experimental.pallas import tpu as pltpu
from jax.sharding import PartitionSpec as P

FROM_A = 1
FROM_B = 2
PAIR = 2
VMEM_LIMIT = 60 * 1024 * 1024
MESH = pl.DeviceIdType.MESH


def sigma_kernel(geometry, a_lists, a_counts, b_lists, b_counts, a_vec, b_vec, c_hbm, a_hbm, b_hbm, out_ref, cbuf, abuf, bbuf, picks, column, across, chosen,
                 straight, tail, adense, bdense, acc, small, local_sem, beta_send, beta_recv, column_recv, up_send, down_send, across_send, across_recv,
                 straight_send, tail_recv):
    na, nb, ops, slots, blk, row_blocks, col_blocks = geometry
    levels = na // PAIR
    rows = row_blocks * blk
    wide = FROM_B * blk
    a = lax.axis_index("alpha")
    c = lax.axis_index("beta")
    z = a // PAIR
    x = a % PAIR
    partner = a + 1 - 2 * x

    copies_c = [pltpu.make_async_copy(c_hbm.at[:, b * blk:(b + 1) * blk], cbuf.at[b], local_sem.at[2 + b]) for b in range(col_blocks)]
    copy_a = pltpu.make_async_copy(a_hbm, abuf, local_sem.at[0])
    copy_b = pltpu.make_async_copy(b_hbm, bbuf, local_sem.at[1])
    for copy in copies_c:
        copy.start()
    copy_a.start()
    copy_b.start()

    barrier = pltpu.get_barrier_semaphore()
    for j in range(1, nb):
        pl.semaphore_signal(barrier, inc=1, device_id={"beta": c ^ j}, device_id_type=MESH)
    pl.semaphore_signal(barrier, inc=1, device_id={"alpha": partner}, device_id_type=MESH)

    @pl.when(z < levels - 1)
    def _():
        pl.semaphore_signal(barrier, inc=1, device_id={"alpha": a + PAIR}, device_id_type=MESH)

    @pl.when(z > 0)
    def _():
        pl.semaphore_signal(barrier, inc=1, device_id={"alpha": a - PAIR}, device_id_type=MESH)

    lists = b_vec[...]
    lane = lax.broadcasted_iota(jnp.int32, (1, nb * col_blocks), 1)

    def extremes(receiver, owner):
        local = lists - owner * col_blocks
        hit = (local >= 0) & (local < col_blocks)
        rows_here = (lane >= receiver * col_blocks) & (lane < (receiver + 1) * col_blocks)
        low = jnp.min(jnp.min(jnp.where(hit, local, col_blocks), axis=0), axis=0, keepdims=True)
        high = jnp.max(jnp.max(jnp.where(hit, local, 0), axis=0), axis=0, keepdims=True)
        low = jnp.min(jnp.where(rows_here, low, col_blocks))
        high = jnp.max(jnp.where(rows_here, high, 0))
        return jnp.where(low < col_blocks, low, 0), high

    spans = [extremes(c ^ j, c) for j in range(nb)]
    for copy in copies_c:
        copy.wait()
    for j in range(nb):
        for u, block in enumerate(spans[j]):
            piece = cbuf[block]
            if j == 0:
                column[z, 0, :, u * blk:(u + 1) * blk] = piece
            else:
                picks[j - 1, :, u * blk:(u + 1) * blk] = piece

    rows_list = a_vec[...]
    row_lane = lax.broadcasted_iota(jnp.int32, (1, na * row_blocks), 1)

    def row_pick(receiver, owner):
        local = rows_list - owner * row_blocks
        hit = (local >= 0) & (local < row_blocks)
        rows_here = (row_lane >= receiver * row_blocks) & (row_lane < (receiver + 1) * row_blocks)
        high = jnp.max(jnp.max(jnp.where(hit, local, 0), axis=0), axis=0, keepdims=True)
        return jnp.max(jnp.where(rows_here, high, 0))

    for lev in range(levels):
        small[lev] = row_pick(a, lev * PAIR + x)
        small[levels + lev] = row_pick(partner, lev * PAIR + x)
    for owner in range(nb):
        small[2 * levels + owner] = extremes(c, owner)[0]
    far = jnp.where(z == levels - 2, levels - 1, 0)
    opposite = levels - 1 - far
    for side in range(PAIR):
        small[2 * levels + nb + side] = row_pick(far * PAIR + (x + side) % PAIR, opposite * PAIR + x)
    out_ref[...] = jnp.zeros_like(out_ref)

    neighbours = nb + jnp.where(z < levels - 1, 1, 0) + jnp.where(z > 0, 1, 0)
    pl.semaphore_wait(barrier, neighbours)

    def beta_copy(j):
        return pltpu.make_async_remote_copy(
            src_ref=picks.at[j - 1], dst_ref=column.at[z, j], send_sem=beta_send.at[j - 1], recv_sem=beta_recv.at[j - 1],
            device_id={"beta": c ^ j}, device_id_type=MESH)

    def up_copy(lev, j):
        return pltpu.make_async_remote_copy(
            src_ref=column.at[lev, j], dst_ref=column.at[lev, j], send_sem=up_send.at[lev, j], recv_sem=column_recv.at[lev, j],
            device_id={"alpha": a + PAIR}, device_id_type=MESH)

    def down_copy(lev, j):
        return pltpu.make_async_remote_copy(
            src_ref=column.at[lev, j], dst_ref=column.at[lev, j], send_sem=down_send.at[lev, j], recv_sem=column_recv.at[lev, j],
            device_id={"alpha": a - PAIR}, device_id_type=MESH)

    def across_copy(lev, j):
        return pltpu.make_async_remote_copy(
            src_ref=chosen.at[lev, j], dst_ref=across.at[lev, j], send_sem=across_send.at[lev, j], recv_sem=across_recv.at[lev, j],
            device_id={"alpha": partner}, device_id_type=MESH)

    def one_hot(value, place):
        gap = value - place
        return (1 - jnp.minimum(jnp.maximum(gap, -gap), 1)).astype(jnp.float32)

    def at_most(slot, count):
        return jnp.minimum(jnp.maximum(count - slot, 0), 1)

    def selected(lev, j, pick):
        total = jnp.zeros((blk, wide), jnp.float32)
        for i in range(row_blocks):
            total += column[lev, j, i * blk:(i + 1) * blk, :].astype(jnp.float32) * one_hot(pick, i)
        return total.astype(jnp.bfloat16)

    def offer(lev, j):
        chosen[lev, j] = selected(lev, j, small[levels + lev])
        across_copy(lev, j).start()

    def own_sends(j):
        @pl.when(z < levels - 1)
        def _():
            up_copy(z, j).start()

        @pl.when(z > 0)
        def _():
            down_copy(z, j).start()

        offer(z, j)

    own_sends(0)
    for j in range(1, nb):
        beta_copy(j).start()

    def dense(load, codes, groups, per_group, put):
        def group(g, carry):
            totals = [jnp.zeros((blk, blk), jnp.float32) for _ in range(per_group)]
            for s in range(slots):
                value = load(s)
                for p in range(per_group):
                    totals[p] += value * jnp.where(codes[s] == g * per_group + p, 1.0, 0.0)
            for p in range(per_group):
                put(g, p, totals[p])
            return carry

        lax.fori_loop(0, groups, group, 0)

    def build_a(piece):
        k = piece // row_blocks
        i = piece % row_blocks
        codes = []
        for s in range(slots):
            entry = a_lists[s, k, a * row_blocks + i]
            owner = lax.div(entry, row_blocks)
            upper = owner - 2 * lax.div(owner, 2)
            place = owner - upper + jnp.maximum(upper - x, x - upper)
            codes.append((place + 1) * at_most(s, a_counts[k, a * row_blocks + i]) - 1)

        def load(s):
            return abuf[k, s, pl.ds(i * blk, blk), :].astype(jnp.float32)

        def put(g, p, total):
            at = pl.ds(k * rows + i * blk, blk)
            high = total.astype(jnp.bfloat16)
            adense[g, at, p * blk:(p + 1) * blk] = high
            adense[g, at, (PAIR + p) * blk:(PAIR + p + 1) * blk] = (total - high.astype(jnp.float32)).astype(jnp.bfloat16)

        dense(load, codes, levels, PAIR, put)

    def build_b(piece):
        k = piece // col_blocks
        r = piece % col_blocks
        codes = []
        for s in range(slots):
            entry = b_lists[s, k, c * col_blocks + r]
            owner = lax.div(entry, col_blocks)
            gap = entry - owner * col_blocks - small[2 * levels + owner]
            place = (owner ^ c) * FROM_B + jnp.minimum(jnp.maximum(gap, -gap), 1)
            codes.append((place + 1) * at_most(s, b_counts[k, c * col_blocks + r]) - 1)

        def load(s):
            return bbuf[k, s, pl.ds(r * blk, blk), :].astype(jnp.float32)

        def put(g, p, total):
            bdense[g, k, pl.ds(r * blk, blk), p * blk:(p + 1) * blk] = total.astype(jnp.bfloat16)

        dense(load, codes, nb, FROM_B, put)

    a_pieces = ops * row_blocks
    pieces = ops * col_blocks

    def build_some(first, count):
        def one(n, carry):
            @pl.when(n < pieces)
            def _():
                build_b(n)
            return carry

        lax.fori_loop(first, first + count, one, 0)

    def beta_wait(j):
        pltpu.make_async_remote_copy(
            src_ref=picks.at[j - 1], dst_ref=column.at[z, j], send_sem=beta_send.at[j - 1], recv_sem=beta_recv.at[j - 1],
            device_id={"beta": c ^ j}, device_id_type=MESH).wait_recv()

    copy_a.wait()

    def one_a(n, carry):
        build_a(n)
        return carry

    lax.fori_loop(0, a_pieces // 2, one_a, 0)
    built = 0
    for j in range(1, nb):
        beta_wait(j)
        own_sends(j)
        if j == 1:
            lax.fori_loop(a_pieces // 2, a_pieces, one_a, 0)
            copy_b.wait()
        if j < nb - 1:
            build_some(built, 2 * j)
            built += 2 * j

    def product(lev, j, mine):
        across_copy(lev, j).wait_recv()
        other = across[lev, j]
        value = jnp.concatenate([mine, other, mine, other], axis=0)
        return jnp.dot(adense[lev], value, preferred_element_type=jnp.float32)

    def combine(lev, j):
        acc[j] += product(lev, j, selected(lev, j, small[lev]))

    tile = min(2, col_blocks) * blk

    def finish(j):
        inters = [acc[j, k * rows:(k + 1) * rows, :].astype(jnp.bfloat16) for k in range(ops)]

        def columns(n, carry):
            here = pl.ds(pl.multiple_of(n * tile, tile), tile)
            total = out_ref[:, here]
            for k in range(ops):
                total += lax.dot_general(inters[k], bdense[j, k, here, :], (((1,), (1,)), ((), ())),
                                         preferred_element_type=jnp.float32)
            out_ref[:, here] = total
            return carry

        lax.fori_loop(0, col_blocks * blk // tile, columns, 0)

    def straight_copy(j):
        return pltpu.make_async_remote_copy(
            src_ref=straight.at[0, j], dst_ref=tail.at[j], send_sem=straight_send.at[0, j], recv_sem=tail_recv.at[j],
            device_id={"alpha": far * PAIR + x}, device_id_type=MESH)

    def diagonal_copy(j):
        return pltpu.make_async_remote_copy(
            src_ref=straight.at[1, j], dst_ref=across.at[opposite, j], send_sem=straight_send.at[1, j], recv_sem=across_recv.at[opposite, j],
            device_id={"alpha": far * PAIR + 1 - x}, device_id_type=MESH)

    def arrive(lev, j, below):
        pltpu.make_async_remote_copy(
            src_ref=column.at[lev, j], dst_ref=column.at[lev, j], send_sem=up_send.at[lev, j], recv_sem=column_recv.at[lev, j],
            device_id={"alpha": partner}, device_id_type=MESH).wait_recv()
        last = (z == levels - 2) & (lev == 0) if below else (z == 1) & (lev == levels - 1)

        @pl.when(last)
        def _():
            straight[1, j] = selected(lev, j, small[2 * levels + nb + 1])
            diagonal_copy(j).start()
            straight[0, j] = selected(lev, j, small[2 * levels + nb])
            straight_copy(j).start()

        if below:
            @pl.when((z < levels - 1) & jnp.logical_not(last))
            def _():
                up_copy(lev, j).start()
        else:
            @pl.when((z > 0) & jnp.logical_not(last))
            def _():
                down_copy(lev, j).start()

        offer(lev, j)

    relayed = (levels - 2) * nb
    at_end = (z == 0) | (z == levels - 1)

    def step(i, carry):
        j = i % nb
        distance = i // nb + 1

        @pl.when((i < relayed) & (z - distance >= 0))
        def _():
            arrive(z - distance, j, True)

        @pl.when((i < relayed) & (z + distance < levels))
        def _():
            arrive(z + distance, j, False)

        @pl.when(i < nb)
        def _():
            acc[j] = product(z, j, selected(z, j, small[z]))

        before = jnp.maximum(i - 1, 0)
        j_before = before % nb
        distance_before = before // nb + 1

        @pl.when((i > 0) & (i <= relayed) & (z - distance_before >= 0))
        def _():
            combine(z - distance_before, j_before)

        @pl.when((i > 0) & (i <= relayed) & (z + distance_before < levels))
        def _():
            combine(z + distance_before, j_before)

        build_some(built + 2 * i, 2)

        @pl.when(i >= relayed)
        def _():
            @pl.when(at_end)
            def _():
                pltpu.make_async_remote_copy(
                    src_ref=straight.at[0, j], dst_ref=tail.at[j], send_sem=straight_send.at[0, j], recv_sem=tail_recv.at[j],
                    device_id={"alpha": partner}, device_id_type=MESH).wait_recv()
                lev = levels - 1 - z
                acc[j] += product(lev, j, tail[j])

            finish(j)

        return carry

    lax.fori_loop(0, relayed + nb, step, 0)

    for j in range(1, nb):
        beta_copy(j).wait_send()

    def drain(n, carry):
        lev = n // nb
        j = n % nb
        up_last = (z == levels - 2) & (lev == 0)
        down_last = (z == 1) & (lev == levels - 1)

        @pl.when((lev <= z) & (z < levels - 1) & jnp.logical_not(up_last))
        def _():
            up_copy(lev, j).wait_send()

        @pl.when((lev >= z) & (z > 0) & jnp.logical_not(down_last))
        def _():
            down_copy(lev, j).wait_send()

        @pl.when(up_last | down_last)
        def _():
            straight_copy(j).wait_send()
            diagonal_copy(j).wait_send()

        @pl.when(jnp.logical_not(at_end & (lev == levels - 1 - z)))
        def _():
            across_copy(lev, j).wait_send()

        return carry

    lax.fori_loop(0, levels * nb, drain, 0)


def scratch_of(geometry, dtype):
    na, nb, ops, slots, blk, row_blocks, col_blocks = geometry
    levels = na // PAIR
    rows, cols, wide = row_blocks * blk, col_blocks * blk, FROM_B * blk
    return [
        ((col_blocks, rows, blk), dtype),
        ((ops, slots, rows, blk), dtype),
        ((ops, slots, cols, blk), dtype),
        ((nb - 1, rows, wide), dtype),
        ((levels, nb, rows, wide), dtype),
        ((levels, nb, blk, wide), dtype),
        ((levels, nb, blk, wide), dtype),
        ((PAIR, nb, blk, wide), dtype),
        ((nb, blk, wide), dtype),
        ((levels, ops * rows, 2 * PAIR * blk), dtype),
        ((nb, ops, cols, wide), dtype),
        ((nb, ops * rows, wide), jnp.float32),
    ]


def scratch_bytes(geometry):
    total = 0
    for shape, dtype in scratch_of(geometry, jnp.bfloat16):
        size = jnp.dtype(dtype).itemsize
        for extent in shape:
            size *= extent
        total += size
    return total


def fused(geometry, coeffs, a_blocks, a_list, a_count, b_blocks, b_list, b_count):
    na, nb, ops, slots, blk, row_blocks, col_blocks = geometry
    levels = na // PAIR
    a_lists = jnp.transpose(a_list, (2, 0, 1))
    b_lists = jnp.transpose(b_list, (2, 0, 1))
    rows, cols = row_blocks * blk, col_blocks * blk
    dma = pltpu.SemaphoreType.DMA
    smem = pl.BlockSpec(memory_space=pltpu.SMEM)
    vmem = pl.BlockSpec(memory_space=pltpu.VMEM)
    return pl.pallas_call(
        functools.partial(sigma_kernel, geometry),
        out_shape=jax.ShapeDtypeStruct((rows, cols), jnp.float32),
        in_specs=[
            smem, smem, smem, smem, vmem, vmem,
            pl.BlockSpec(memory_space=pl.ANY),
            pl.BlockSpec(memory_space=pl.ANY),
            pl.BlockSpec(memory_space=pl.ANY),
        ],
        out_specs=pl.BlockSpec(memory_space=pltpu.VMEM),
        scratch_shapes=[pltpu.VMEM(shape, dtype) for shape, dtype in scratch_of(geometry, coeffs.dtype)] + [
            pltpu.SMEM((2 * levels + nb + PAIR,), jnp.int32),
            dma((2 + col_blocks,)), dma((nb - 1,)), dma((nb - 1,)), dma((levels, nb)), dma((levels, nb)), dma((levels, nb)),
            dma((levels, nb)), dma((levels, nb)), dma((PAIR, nb)), dma((nb,)),
        ],
        compiler_params=pltpu.CompilerParams(collective_id=0, has_side_effects=True, vmem_limit_bytes=VMEM_LIMIT),
        name="sigma_build",
    )(a_lists, a_count, b_lists, b_count, a_lists, b_lists, coeffs, jnp.transpose(a_blocks, (0, 2, 1, 3)), jnp.transpose(b_blocks, (0, 2, 1, 3)))


def arrange(entries, owners, per_owner, capacity):
    operators, total, list_slots = entries.shape
    flattened = entries.reshape(operators, owners, per_owner * list_slots)
    matches = flattened[..., None] == jnp.arange(total, dtype=jnp.int32)
    present = jnp.any(matches, axis=(0, 2)).reshape(owners, owners, per_owner).astype(jnp.int32)
    ranking = jnp.cumsum(present, axis=2)
    position = jnp.arange(capacity, dtype=jnp.int32) + 1
    chosen_bits = (present[..., None] == 1) & (ranking[..., None] == position)
    local_ids = jnp.arange(per_owner, dtype=jnp.int32)[None, None, :, None]
    wanted = jnp.sum(local_ids * chosen_bits.astype(jnp.int32), axis=2)
    return (wanted, ranking)


def locate(entries, ranking_here, per_owner, capacity):
    owner = entries // per_owner
    local_id = entries % per_owner
    return owner * capacity + ranking_here[owner, local_id] - 1


def pick_columns(pool_piece, index_piece):
    return pool_piece[:, index_piece]


def plain(coeffs, a_blocks, a_list, a_count, b_blocks, b_list, b_count):
    operators, local_rows, list_slots, block_size = a_blocks.shape
    local_cols = coeffs.shape[1]
    row_blocks = local_rows // block_size
    col_blocks = local_cols // block_size
    row_capacity = FROM_A
    col_capacity = FROM_B
    alpha_size = lax.axis_size("alpha")
    beta_size = lax.axis_size("beta")
    alpha_here = lax.axis_index("alpha")
    beta_here = lax.axis_index("beta")
    slot_ids = jnp.arange(list_slots, dtype=jnp.int32)
    alpha_mine = lax.dynamic_slice_in_dim(a_list, alpha_here * row_blocks, row_blocks, 1)
    alpha_counts = lax.dynamic_slice_in_dim(a_count, alpha_here * row_blocks, row_blocks, 1)
    alpha_valid = slot_ids < alpha_counts[..., None]
    alpha_kept = jnp.where(
        alpha_valid[:, :, None, :, None],
        a_blocks.reshape(operators, row_blocks, block_size, list_slots, block_size),
        jnp.zeros((), jnp.bfloat16),
    )
    wanted, ranking = arrange(a_list, alpha_size, row_blocks, row_capacity)
    outgoing = coeffs.reshape(row_blocks, block_size, local_cols)[wanted[:, alpha_here, :]]
    incoming = lax.all_to_all(outgoing, "alpha", split_axis=0, concat_axis=0, tiled=True)
    source_index = locate(alpha_mine, ranking[alpha_here], row_blocks, row_capacity)
    chosen = incoming.reshape(alpha_size * row_capacity, block_size, local_cols)[source_index]
    inter = jnp.einsum("kbrsi,kbsic->kbrc", alpha_kept, chosen, preferred_element_type=jnp.float32)
    inter = inter.astype(jnp.bfloat16).reshape(operators, local_rows, col_blocks, block_size)
    wanted_cols, ranking_cols = arrange(b_list, beta_size, col_blocks, col_capacity)
    outgoing_cols = inter[:, :, wanted_cols[:, beta_here, :], :]
    incoming_cols = lax.all_to_all(outgoing_cols, "beta", split_axis=2, concat_axis=2, tiled=True)
    beta_mine = lax.dynamic_slice_in_dim(b_list, beta_here * col_blocks, col_blocks, 1)
    beta_counts = lax.dynamic_slice_in_dim(b_count, beta_here * col_blocks, col_blocks, 1)
    beta_valid = slot_ids < beta_counts[..., None]
    beta_kept = jnp.where(
        beta_valid[:, :, None, :, None],
        b_blocks.reshape(operators, col_blocks, block_size, list_slots, block_size),
        jnp.zeros((), jnp.bfloat16),
    )
    source_cols = locate(beta_mine, ranking_cols[beta_here], col_blocks, col_capacity)
    pooled = incoming_cols.reshape(operators, local_rows, beta_size * col_capacity, block_size)
    picked = jax.vmap(pick_columns)(pooled, source_cols)
    sigma = jnp.einsum("kabsj,kbrsj->abr", picked, beta_kept, preferred_element_type=jnp.float32)
    return sigma.reshape(local_rows, local_cols)


def on_device(coeffs, a_blocks, a_list, a_count, b_blocks, b_list, b_count):
    operators, local_rows, list_slots, block_size = a_blocks.shape
    na, nb = lax.axis_size("alpha"), lax.axis_size("beta")
    geometry = (na, nb, operators, list_slots, block_size, local_rows // block_size, coeffs.shape[1] // block_size)
    fits = scratch_bytes(geometry) < VMEM_LIMIT * 3 // 4
    shaped = FROM_A == 1 and FROM_B == 2 and na % PAIR == 0 and na > 3 * PAIR and nb & (nb - 1) == 0 and nb > 1
    build = functools.partial(fused, geometry) if fits and shaped else plain
    return build(coeffs, a_blocks, a_list, a_count, b_blocks, b_list, b_count)


def solution(mesh):
    in_specs = (
        P("alpha", "beta"),
        P(None, "alpha", None, None),
        P(),
        P(),
        P(None, "beta", None, None),
        P(),
        P(),
    )
    out_specs = P("alpha", "beta")
    return jax.shard_map(
        on_device, mesh=mesh, in_specs=in_specs, out_specs=out_specs, check_vma=False
    )
```

```python
import functools

import jax
import jax.numpy as jnp
from jax import lax
from jax.experimental import pallas as pl
from jax.experimental.pallas import tpu as pltpu
from jax.sharding import PartitionSpec as P

FROM_A = 1
FROM_B = 2
PAIR = 2
VMEM_LIMIT = 60 * 1024 * 1024
KERNEL_LIMIT = 40 * 1024 * 1024
MESH = pl.DeviceIdType.MESH


def sigma_kernel(geometry, a_lists_hbm, a_counts_hbm, b_lists_hbm, b_counts_hbm, c_hbm, a_hbm, b_hbm, out_ref, a_lists, a_counts, b_lists, b_counts, a_vec, b_vec, cbuf, abuf, bbuf, picks, column, across, chosen,
                 straight, tail, adense, bdense, acc, small, table_sem, local_sem, beta_send, beta_recv, column_recv, up_send, down_send, across_send, across_recv,
                 straight_send, tail_recv):
    na, nb, ops, slots, blk, row_blocks, col_blocks = geometry
    levels = na // PAIR
    rows = row_blocks * blk
    wide = FROM_B * blk
    a = lax.axis_index("alpha")
    c = lax.axis_index("beta")
    z = a // PAIR
    x = a % PAIR
    partner = a + 1 - 2 * x

    barrier = pltpu.get_barrier_semaphore()
    for j in range(1, nb):
        pl.semaphore_signal(barrier, inc=1, device_id={"beta": c ^ j}, device_id_type=MESH)
    pl.semaphore_signal(barrier, inc=1, device_id={"alpha": partner}, device_id_type=MESH)

    @pl.when(z < levels - 1)
    def _():
        pl.semaphore_signal(barrier, inc=1, device_id={"alpha": a + PAIR}, device_id_type=MESH)

    @pl.when(z > 0)
    def _():
        pl.semaphore_signal(barrier, inc=1, device_id={"alpha": a - PAIR}, device_id_type=MESH)

    tables = [(b_lists_hbm, b_vec), (a_lists_hbm, a_vec), (a_lists_hbm, a_lists), (a_counts_hbm, a_counts), (b_lists_hbm, b_lists), (b_counts_hbm, b_counts)]
    copies_t = [pltpu.make_async_copy(source, target, table_sem.at[n]) for n, (source, target) in enumerate(tables)]
    copies_c = [pltpu.make_async_copy(c_hbm.at[:, b * blk:(b + 1) * blk], cbuf.at[b], local_sem.at[2 + b]) for b in range(col_blocks)]
    copy_a = pltpu.make_async_copy(a_hbm, abuf, local_sem.at[0])
    copy_b = pltpu.make_async_copy(b_hbm, bbuf, local_sem.at[1])
    for copy in copies_t + copies_c:
        copy.start()
    copy_a.start()
    copy_b.start()
    for copy in copies_t:
        copy.wait()

    lists = b_vec[...]
    lane = lax.broadcasted_iota(jnp.int32, (1, nb * col_blocks), 1)

    def extremes(receiver, owner):
        local = lists - owner * col_blocks
        hit = (local >= 0) & (local < col_blocks)
        rows_here = (lane >= receiver * col_blocks) & (lane < (receiver + 1) * col_blocks)
        low = jnp.min(jnp.min(jnp.where(hit, local, col_blocks), axis=0), axis=0, keepdims=True)
        high = jnp.max(jnp.max(jnp.where(hit, local, 0), axis=0), axis=0, keepdims=True)
        low = jnp.min(jnp.where(rows_here, low, col_blocks))
        high = jnp.max(jnp.where(rows_here, high, 0))
        return jnp.where(low < col_blocks, low, 0), high

    spans = [extremes(c ^ j, c) for j in range(nb)]
    for copy in copies_c:
        copy.wait()
    for j in range(nb):
        for u, block in enumerate(spans[j]):
            piece = cbuf[block]
            if j == 0:
                column[z, 0, :, u * blk:(u + 1) * blk] = piece
            else:
                picks[j - 1, :, u * blk:(u + 1) * blk] = piece

    rows_list = a_vec[...]
    row_lane = lax.broadcasted_iota(jnp.int32, (1, na * row_blocks), 1)

    def row_pick(receiver, owner):
        local = rows_list - owner * row_blocks
        hit = (local >= 0) & (local < row_blocks)
        rows_here = (row_lane >= receiver * row_blocks) & (row_lane < (receiver + 1) * row_blocks)
        high = jnp.max(jnp.max(jnp.where(hit, local, 0), axis=0), axis=0, keepdims=True)
        return jnp.max(jnp.where(rows_here, high, 0))

    for lev in range(levels):
        small[lev] = row_pick(a, lev * PAIR + x)
        small[levels + lev] = row_pick(partner, lev * PAIR + x)
    for owner in range(nb):
        small[2 * levels + owner] = extremes(c, owner)[0]
    far = jnp.where(z == levels - 2, levels - 1, 0)
    opposite = levels - 1 - far
    for side in range(PAIR):
        small[2 * levels + nb + side] = row_pick(far * PAIR + (x + side) % PAIR, opposite * PAIR + x)
    out_ref[...] = jnp.zeros_like(out_ref)

    neighbours = nb + jnp.where(z < levels - 1, 1, 0) + jnp.where(z > 0, 1, 0)
    pl.semaphore_wait(barrier, neighbours)

    def beta_copy(j):
        return pltpu.make_async_remote_copy(
            src_ref=picks.at[j - 1], dst_ref=column.at[z, j], send_sem=beta_send.at[j - 1], recv_sem=beta_recv.at[j - 1],
            device_id={"beta": c ^ j}, device_id_type=MESH)

    def up_copy(lev, j):
        return pltpu.make_async_remote_copy(
            src_ref=column.at[lev, j], dst_ref=column.at[lev, j], send_sem=up_send.at[lev, j], recv_sem=column_recv.at[lev, j],
            device_id={"alpha": a + PAIR}, device_id_type=MESH)

    def down_copy(lev, j):
        return pltpu.make_async_remote_copy(
            src_ref=column.at[lev, j], dst_ref=column.at[lev, j], send_sem=down_send.at[lev, j], recv_sem=column_recv.at[lev, j],
            device_id={"alpha": a - PAIR}, device_id_type=MESH)

    def across_copy(lev, j):
        return pltpu.make_async_remote_copy(
            src_ref=chosen.at[lev, j], dst_ref=across.at[lev, j], send_sem=across_send.at[lev, j], recv_sem=across_recv.at[lev, j],
            device_id={"alpha": partner}, device_id_type=MESH)

    def one_hot(value, place):
        gap = value - place
        return (1 - jnp.minimum(jnp.maximum(gap, -gap), 1)).astype(jnp.float32)

    def at_most(slot, count):
        return jnp.minimum(jnp.maximum(count - slot, 0), 1)

    def selected(lev, j, pick):
        total = jnp.zeros((blk, wide), jnp.float32)
        for i in range(row_blocks):
            total += column[lev, j, i * blk:(i + 1) * blk, :].astype(jnp.float32) * one_hot(pick, i)
        return total.astype(jnp.bfloat16)

    def offer(lev, j):
        chosen[lev, j] = selected(lev, j, small[levels + lev])
        across_copy(lev, j).start()

    def own_sends(j):
        @pl.when(z < levels - 1)
        def _():
            up_copy(z, j).start()

        @pl.when(z > 0)
        def _():
            down_copy(z, j).start()

        offer(z, j)

    own_sends(0)
    for j in range(1, nb):
        beta_copy(j).start()

    def dense(load, codes, groups, per_group, put):
        def group(g, carry):
            totals = [jnp.zeros((blk, blk), jnp.float32) for _ in range(per_group)]
            for s in range(slots):
                value = load(s)
                for p in range(per_group):
                    totals[p] += value * jnp.where(codes[s] == g * per_group + p, 1.0, 0.0)
            for p in range(per_group):
                put(g, p, totals[p])
            return carry

        lax.fori_loop(0, groups, group, 0)

    def build_a(piece):
        k = piece // row_blocks
        i = piece % row_blocks
        codes = []
        for s in range(slots):
            entry = a_lists[s, k, a * row_blocks + i]
            owner = lax.div(entry, row_blocks)
            upper = owner - 2 * lax.div(owner, 2)
            place = owner - upper + jnp.maximum(upper - x, x - upper)
            codes.append((place + 1) * at_most(s, a_counts[k, a * row_blocks + i]) - 1)

        def load(s):
            return abuf[k, s, pl.ds(i * blk, blk), :].astype(jnp.float32)

        def put(g, p, total):
            at = pl.ds(k * rows + i * blk, blk)
            high = total.astype(jnp.bfloat16)
            adense[g, at, p * blk:(p + 1) * blk] = high
            adense[g, at, (PAIR + p) * blk:(PAIR + p + 1) * blk] = (total - high.astype(jnp.float32)).astype(jnp.bfloat16)

        dense(load, codes, levels, PAIR, put)

    def build_b(piece):
        k = piece // col_blocks
        r = piece % col_blocks
        codes = []
        for s in range(slots):
            entry = b_lists[s, k, c * col_blocks + r]
            owner = lax.div(entry, col_blocks)
            gap = entry - owner * col_blocks - small[2 * levels + owner]
            place = (owner ^ c) * FROM_B + jnp.minimum(jnp.maximum(gap, -gap), 1)
            codes.append((place + 1) * at_most(s, b_counts[k, c * col_blocks + r]) - 1)

        def load(s):
            return bbuf[k, s, pl.ds(r * blk, blk), :].astype(jnp.float32)

        def put(g, p, total):
            bdense[g, k, pl.ds(r * blk, blk), p * blk:(p + 1) * blk] = total.astype(jnp.bfloat16)

        dense(load, codes, nb, FROM_B, put)

    a_pieces = ops * row_blocks
    pieces = ops * col_blocks

    def build_some(first, count):
        def one(n, carry):
            @pl.when(n < pieces)
            def _():
                build_b(n)
            return carry

        lax.fori_loop(first, first + count, one, 0)

    def beta_wait(j):
        pltpu.make_async_remote_copy(
            src_ref=picks.at[j - 1], dst_ref=column.at[z, j], send_sem=beta_send.at[j - 1], recv_sem=beta_recv.at[j - 1],
            device_id={"beta": c ^ j}, device_id_type=MESH).wait_recv()

    copy_a.wait()

    def one_a(n, carry):
        build_a(n)
        return carry

    lax.fori_loop(0, a_pieces // 2, one_a, 0)
    built = 0
    for j in range(1, nb):
        beta_wait(j)
        own_sends(j)
        if j == 1:
            lax.fori_loop(a_pieces // 2, a_pieces, one_a, 0)
            copy_b.wait()
        if j < nb - 1:
            build_some(built, 2 * j)
            built += 2 * j

    def product(lev, j, mine):
        across_copy(lev, j).wait_recv()
        other = across[lev, j]
        value = jnp.concatenate([mine, other, mine, other], axis=0)
        return jnp.dot(adense[lev], value, preferred_element_type=jnp.float32)

    def combine(lev, j):
        acc[j] += product(lev, j, selected(lev, j, small[lev]))

    tile = min(2, col_blocks) * blk

    def finish(j):
        inters = [acc[j, k * rows:(k + 1) * rows, :].astype(jnp.bfloat16) for k in range(ops)]

        def columns(n, carry):
            here = pl.ds(pl.multiple_of(n * tile, tile), tile)
            total = out_ref[:, here]
            for k in range(ops):
                total += lax.dot_general(inters[k], bdense[j, k, here, :], (((1,), (1,)), ((), ())),
                                         preferred_element_type=jnp.float32)
            out_ref[:, here] = total
            return carry

        lax.fori_loop(0, col_blocks * blk // tile, columns, 0)

    def straight_copy(j):
        return pltpu.make_async_remote_copy(
            src_ref=straight.at[0, j], dst_ref=tail.at[j], send_sem=straight_send.at[0, j], recv_sem=tail_recv.at[j],
            device_id={"alpha": far * PAIR + x}, device_id_type=MESH)

    def diagonal_copy(j):
        return pltpu.make_async_remote_copy(
            src_ref=straight.at[1, j], dst_ref=across.at[opposite, j], send_sem=straight_send.at[1, j], recv_sem=across_recv.at[opposite, j],
            device_id={"alpha": far * PAIR + 1 - x}, device_id_type=MESH)

    def arrive(lev, j, below):
        pltpu.make_async_remote_copy(
            src_ref=column.at[lev, j], dst_ref=column.at[lev, j], send_sem=up_send.at[lev, j], recv_sem=column_recv.at[lev, j],
            device_id={"alpha": partner}, device_id_type=MESH).wait_recv()
        last = (z == levels - 2) & (lev == 0) if below else (z == 1) & (lev == levels - 1)

        @pl.when(last)
        def _():
            straight[1, j] = selected(lev, j, small[2 * levels + nb + 1])
            diagonal_copy(j).start()
            straight[0, j] = selected(lev, j, small[2 * levels + nb])
            straight_copy(j).start()

        if below:
            @pl.when((z < levels - 1) & jnp.logical_not(last))
            def _():
                up_copy(lev, j).start()
        else:
            @pl.when((z > 0) & jnp.logical_not(last))
            def _():
                down_copy(lev, j).start()

        offer(lev, j)

    relayed = (levels - 2) * nb
    at_end = (z == 0) | (z == levels - 1)

    def step(i, carry):
        j = i % nb
        distance = i // nb + 1

        @pl.when((i < relayed) & (z - distance >= 0))
        def _():
            arrive(z - distance, j, True)

        @pl.when((i < relayed) & (z + distance < levels))
        def _():
            arrive(z + distance, j, False)

        @pl.when(i < nb)
        def _():
            acc[j] = product(z, j, selected(z, j, small[z]))

        before = jnp.maximum(i - 1, 0)
        j_before = before % nb
        distance_before = before // nb + 1

        @pl.when((i > 0) & (i <= relayed) & (z - distance_before >= 0))
        def _():
            combine(z - distance_before, j_before)

        @pl.when((i > 0) & (i <= relayed) & (z + distance_before < levels))
        def _():
            combine(z + distance_before, j_before)

        build_some(built + 2 * i, 2)

        @pl.when(i >= relayed)
        def _():
            @pl.when(at_end)
            def _():
                pltpu.make_async_remote_copy(
                    src_ref=straight.at[0, j], dst_ref=tail.at[j], send_sem=straight_send.at[0, j], recv_sem=tail_recv.at[j],
                    device_id={"alpha": partner}, device_id_type=MESH).wait_recv()
                lev = levels - 1 - z
                acc[j] += product(lev, j, tail[j])

            finish(j)

        return carry

    lax.fori_loop(0, relayed + nb, step, 0)

    for j in range(1, nb):
        beta_copy(j).wait_send()

    def drain(n, carry):
        lev = n // nb
        j = n % nb
        up_last = (z == levels - 2) & (lev == 0)
        down_last = (z == 1) & (lev == levels - 1)

        @pl.when((lev <= z) & (z < levels - 1) & jnp.logical_not(up_last))
        def _():
            up_copy(lev, j).wait_send()

        @pl.when((lev >= z) & (z > 0) & jnp.logical_not(down_last))
        def _():
            down_copy(lev, j).wait_send()

        @pl.when(up_last | down_last)
        def _():
            straight_copy(j).wait_send()
            diagonal_copy(j).wait_send()

        @pl.when(jnp.logical_not(at_end & (lev == levels - 1 - z)))
        def _():
            across_copy(lev, j).wait_send()

        return carry

    lax.fori_loop(0, levels * nb, drain, 0)


def scratch_of(geometry, dtype):
    na, nb, ops, slots, blk, row_blocks, col_blocks = geometry
    levels = na // PAIR
    rows, cols, wide = row_blocks * blk, col_blocks * blk, FROM_B * blk
    return [
        ((col_blocks, rows, blk), dtype),
        ((ops, slots, rows, blk), dtype),
        ((ops, slots, cols, blk), dtype),
        ((nb - 1, rows, wide), dtype),
        ((levels, nb, rows, wide), dtype),
        ((levels, nb, blk, wide), dtype),
        ((levels, nb, blk, wide), dtype),
        ((PAIR, nb, blk, wide), dtype),
        ((nb, blk, wide), dtype),
        ((levels, ops * rows, 2 * PAIR * blk), dtype),
        ((nb, ops, cols, wide), dtype),
        ((nb, ops * rows, wide), jnp.float32),
    ]


def scratch_bytes(geometry):
    total = 0
    for shape, dtype in scratch_of(geometry, jnp.bfloat16):
        size = jnp.dtype(dtype).itemsize
        for extent in shape:
            size *= extent
        total += size
    return total


def fused(geometry, coeffs, a_blocks, a_list, a_count, b_blocks, b_list, b_count):
    na, nb, ops, slots, blk, row_blocks, col_blocks = geometry
    levels = na // PAIR
    a_lists = jnp.transpose(a_list, (2, 0, 1))
    b_lists = jnp.transpose(b_list, (2, 0, 1))
    rows, cols = row_blocks * blk, col_blocks * blk
    dma = pltpu.SemaphoreType.DMA
    held = pl.pallas_call(
        functools.partial(sigma_kernel, geometry),
        out_shape=pltpu.VMEM((rows, cols), jnp.float32),
        in_specs=[pl.BlockSpec(memory_space=pltpu.HBM)] * 7,
        out_specs=pl.BlockSpec(memory_space=pltpu.VMEM),
        scratch_shapes=[
            pltpu.SMEM(a_lists.shape, jnp.int32), pltpu.SMEM(a_count.shape, jnp.int32), pltpu.SMEM(b_lists.shape, jnp.int32),
            pltpu.SMEM(b_count.shape, jnp.int32), pltpu.VMEM(a_lists.shape, jnp.int32), pltpu.VMEM(b_lists.shape, jnp.int32),
        ] + [pltpu.VMEM(shape, dtype) for shape, dtype in scratch_of(geometry, coeffs.dtype)] + [
            pltpu.SMEM((2 * levels + nb + PAIR,), jnp.int32),
            dma((6,)), dma((2 + col_blocks,)), dma((nb - 1,)), dma((nb - 1,)), dma((levels, nb)), dma((levels, nb)), dma((levels, nb)),
            dma((levels, nb)), dma((levels, nb)), dma((PAIR, nb)), dma((nb,)),
        ],
        compiler_params=pltpu.CompilerParams(collective_id=0, has_side_effects=True, vmem_limit_bytes=KERNEL_LIMIT),
        name="sigma_build",
    )(*[pltpu.with_memory_space_constraint(v, pltpu.HBM) for v in (a_lists, a_count, b_lists, b_count, coeffs, jnp.transpose(a_blocks, (0, 2, 1, 3)), jnp.transpose(b_blocks, (0, 2, 1, 3)))])
    return held


def arrange(entries, owners, per_owner, capacity):
    operators, total, list_slots = entries.shape
    flattened = entries.reshape(operators, owners, per_owner * list_slots)
    matches = flattened[..., None] == jnp.arange(total, dtype=jnp.int32)
    present = jnp.any(matches, axis=(0, 2)).reshape(owners, owners, per_owner).astype(jnp.int32)
    ranking = jnp.cumsum(present, axis=2)
    position = jnp.arange(capacity, dtype=jnp.int32) + 1
    chosen_bits = (present[..., None] == 1) & (ranking[..., None] == position)
    local_ids = jnp.arange(per_owner, dtype=jnp.int32)[None, None, :, None]
    wanted = jnp.sum(local_ids * chosen_bits.astype(jnp.int32), axis=2)
    return (wanted, ranking)


def locate(entries, ranking_here, per_owner, capacity):
    owner = entries // per_owner
    local_id = entries % per_owner
    return owner * capacity + ranking_here[owner, local_id] - 1


def pick_columns(pool_piece, index_piece):
    return pool_piece[:, index_piece]


def plain(coeffs, a_blocks, a_list, a_count, b_blocks, b_list, b_count):
    operators, local_rows, list_slots, block_size = a_blocks.shape
    local_cols = coeffs.shape[1]
    row_blocks = local_rows // block_size
    col_blocks = local_cols // block_size
    row_capacity = FROM_A
    col_capacity = FROM_B
    alpha_size = lax.axis_size("alpha")
    beta_size = lax.axis_size("beta")
    alpha_here = lax.axis_index("alpha")
    beta_here = lax.axis_index("beta")
    slot_ids = jnp.arange(list_slots, dtype=jnp.int32)
    alpha_mine = lax.dynamic_slice_in_dim(a_list, alpha_here * row_blocks, row_blocks, 1)
    alpha_counts = lax.dynamic_slice_in_dim(a_count, alpha_here * row_blocks, row_blocks, 1)
    alpha_valid = slot_ids < alpha_counts[..., None]
    alpha_kept = jnp.where(
        alpha_valid[:, :, None, :, None],
        a_blocks.reshape(operators, row_blocks, block_size, list_slots, block_size),
        jnp.zeros((), jnp.bfloat16),
    )
    wanted, ranking = arrange(a_list, alpha_size, row_blocks, row_capacity)
    outgoing = coeffs.reshape(row_blocks, block_size, local_cols)[wanted[:, alpha_here, :]]
    incoming = lax.all_to_all(outgoing, "alpha", split_axis=0, concat_axis=0, tiled=True)
    source_index = locate(alpha_mine, ranking[alpha_here], row_blocks, row_capacity)
    chosen = incoming.reshape(alpha_size * row_capacity, block_size, local_cols)[source_index]
    inter = jnp.einsum("kbrsi,kbsic->kbrc", alpha_kept, chosen, preferred_element_type=jnp.float32)
    inter = inter.astype(jnp.bfloat16).reshape(operators, local_rows, col_blocks, block_size)
    wanted_cols, ranking_cols = arrange(b_list, beta_size, col_blocks, col_capacity)
    outgoing_cols = inter[:, :, wanted_cols[:, beta_here, :], :]
    incoming_cols = lax.all_to_all(outgoing_cols, "beta", split_axis=2, concat_axis=2, tiled=True)
    beta_mine = lax.dynamic_slice_in_dim(b_list, beta_here * col_blocks, col_blocks, 1)
    beta_counts = lax.dynamic_slice_in_dim(b_count, beta_here * col_blocks, col_blocks, 1)
    beta_valid = slot_ids < beta_counts[..., None]
    beta_kept = jnp.where(
        beta_valid[:, :, None, :, None],
        b_blocks.reshape(operators, col_blocks, block_size, list_slots, block_size),
        jnp.zeros((), jnp.bfloat16),
    )
    source_cols = locate(beta_mine, ranking_cols[beta_here], col_blocks, col_capacity)
    pooled = incoming_cols.reshape(operators, local_rows, beta_size * col_capacity, block_size)
    picked = jax.vmap(pick_columns)(pooled, source_cols)
    sigma = jnp.einsum("kabsj,kbrsj->abr", picked, beta_kept, preferred_element_type=jnp.float32)
    return sigma.reshape(local_rows, local_cols)


def on_device(coeffs, a_blocks, a_list, a_count, b_blocks, b_list, b_count):
    operators, local_rows, list_slots, block_size = a_blocks.shape
    na, nb = lax.axis_size("alpha"), lax.axis_size("beta")
    geometry = (na, nb, operators, list_slots, block_size, local_rows // block_size, coeffs.shape[1] // block_size)
    fits = scratch_bytes(geometry) < VMEM_LIMIT * 3 // 4
    shaped = FROM_A == 1 and FROM_B == 2 and na % PAIR == 0 and na > 3 * PAIR and nb & (nb - 1) == 0 and nb > 1
    build = functools.partial(fused, geometry) if fits and shaped else plain
    return build(coeffs, a_blocks, a_list, a_count, b_blocks, b_list, b_count)


def solution(mesh):
    in_specs = (
        P("alpha", "beta"),
        P(None, "alpha", None, None),
        P(),
        P(),
        P(None, "beta", None, None),
        P(),
        P(),
    )
    out_specs = P("alpha", "beta")
    return jax.shard_map(
        on_device, mesh=mesh, in_specs=in_specs, out_specs=out_specs, check_vma=False
    )
```

```python
import functools

import jax
import jax.numpy as jnp
from jax import lax
from jax.experimental import pallas as pl
from jax.experimental.pallas import tpu as pltpu
from jax.sharding import PartitionSpec as P

FROM_A = 1
FROM_B = 2
PAIR = 2
VMEM_LIMIT = 60 * 1024 * 1024
KERNEL_LIMIT = 40 * 1024 * 1024
MESH = pl.DeviceIdType.MESH


def sigma_kernel(geometry, a_lists_hbm, a_counts_hbm, b_lists_hbm, b_counts_hbm, c_hbm, a_hbm, b_hbm, out_ref, last_ref, last_b_ref, a_lists, a_counts, b_lists, b_counts, a_vec, b_vec, cbuf, abuf, bbuf, picks, column, across, chosen,
                 straight, tail, adense, bdense, acc, small, table_sem, local_sem, beta_send, beta_recv, column_recv, up_send, down_send, across_send, across_recv,
                 straight_send, tail_recv):
    na, nb, ops, slots, blk, row_blocks, col_blocks = geometry
    levels = na // PAIR
    rows = row_blocks * blk
    wide = FROM_B * blk
    a = lax.axis_index("alpha")
    c = lax.axis_index("beta")
    z = a // PAIR
    x = a % PAIR
    partner = a + 1 - 2 * x

    barrier = pltpu.get_barrier_semaphore()
    for j in range(1, nb):
        pl.semaphore_signal(barrier, inc=1, device_id={"beta": c ^ j}, device_id_type=MESH)
    pl.semaphore_signal(barrier, inc=1, device_id={"alpha": partner}, device_id_type=MESH)

    @pl.when(z < levels - 1)
    def _():
        pl.semaphore_signal(barrier, inc=1, device_id={"alpha": a + PAIR}, device_id_type=MESH)

    @pl.when(z > 0)
    def _():
        pl.semaphore_signal(barrier, inc=1, device_id={"alpha": a - PAIR}, device_id_type=MESH)

    tables = [(b_lists_hbm, b_vec), (a_lists_hbm, a_vec), (a_lists_hbm, a_lists), (a_counts_hbm, a_counts), (b_lists_hbm, b_lists), (b_counts_hbm, b_counts)]
    copies_t = [pltpu.make_async_copy(source, target, table_sem.at[n]) for n, (source, target) in enumerate(tables)]
    copies_c = [pltpu.make_async_copy(c_hbm.at[:, b * blk:(b + 1) * blk], cbuf.at[b], local_sem.at[2 + b]) for b in range(col_blocks)]
    copy_a = pltpu.make_async_copy(a_hbm, abuf, local_sem.at[0])
    copy_b = pltpu.make_async_copy(b_hbm, bbuf, local_sem.at[1])
    for copy in copies_t + copies_c:
        copy.start()
    copy_a.start()
    copy_b.start()
    copies_t[0].wait()

    lists = b_vec[...]
    lane = lax.broadcasted_iota(jnp.int32, (1, nb * col_blocks), 1)

    def extremes(receiver, owner):
        local = lists - owner * col_blocks
        hit = (local >= 0) & (local < col_blocks)
        rows_here = (lane >= receiver * col_blocks) & (lane < (receiver + 1) * col_blocks)
        low = jnp.min(jnp.min(jnp.where(hit, local, col_blocks), axis=0), axis=0, keepdims=True)
        high = jnp.max(jnp.max(jnp.where(hit, local, 0), axis=0), axis=0, keepdims=True)
        low = jnp.min(jnp.where(rows_here, low, col_blocks))
        high = jnp.max(jnp.where(rows_here, high, 0))
        return jnp.where(low < col_blocks, low, 0), high

    spans = [extremes(c ^ j, c) for j in range(nb)]
    for copy in copies_c:
        copy.wait()
    for j in range(nb):
        for u, block in enumerate(spans[j]):
            piece = cbuf[block]
            if j == 0:
                column[z, 0, :, u * blk:(u + 1) * blk] = piece
            else:
                picks[j - 1, :, u * blk:(u + 1) * blk] = piece

    neighbours = nb + jnp.where(z < levels - 1, 1, 0) + jnp.where(z > 0, 1, 0)
    pl.semaphore_wait(barrier, neighbours)

    def beta_copy(j):
        return pltpu.make_async_remote_copy(
            src_ref=picks.at[j - 1], dst_ref=column.at[z, j], send_sem=beta_send.at[j - 1], recv_sem=beta_recv.at[j - 1],
            device_id={"beta": c ^ j}, device_id_type=MESH)

    def up_copy(lev, j):
        return pltpu.make_async_remote_copy(
            src_ref=column.at[lev, j], dst_ref=column.at[lev, j], send_sem=up_send.at[lev, j], recv_sem=column_recv.at[lev, j],
            device_id={"alpha": a + PAIR}, device_id_type=MESH)

    def down_copy(lev, j):
        return pltpu.make_async_remote_copy(
            src_ref=column.at[lev, j], dst_ref=column.at[lev, j], send_sem=down_send.at[lev, j], recv_sem=column_recv.at[lev, j],
            device_id={"alpha": a - PAIR}, device_id_type=MESH)

    def across_copy(lev, j):
        return pltpu.make_async_remote_copy(
            src_ref=chosen.at[lev, j], dst_ref=across.at[lev, j], send_sem=across_send.at[lev, j], recv_sem=across_recv.at[lev, j],
            device_id={"alpha": partner}, device_id_type=MESH)

    def one_hot(value, place):
        gap = value - place
        return (1 - jnp.minimum(jnp.maximum(gap, -gap), 1)).astype(jnp.float32)

    def at_most(slot, count):
        return jnp.minimum(jnp.maximum(count - slot, 0), 1)

    def selected(lev, j, pick):
        total = jnp.zeros((blk, wide), jnp.float32)
        for i in range(row_blocks):
            total += column[lev, j, i * blk:(i + 1) * blk, :].astype(jnp.float32) * one_hot(pick, i)
        return total.astype(jnp.bfloat16)

    def offer(lev, j):
        chosen[lev, j] = selected(lev, j, small[levels + lev])
        across_copy(lev, j).start()

    def own_relays(j):
        @pl.when(z < levels - 1)
        def _():
            up_copy(z, j).start()

        @pl.when(z > 0)
        def _():
            down_copy(z, j).start()

    own_relays(0)
    for j in range(1, nb):
        beta_copy(j).start()
    for copy in copies_t[1:]:
        copy.wait()
    rows_list = a_vec[...]
    row_lane = lax.broadcasted_iota(jnp.int32, (1, na * row_blocks), 1)

    def row_pick(receiver, owner):
        local = rows_list - owner * row_blocks
        hit = (local >= 0) & (local < row_blocks)
        rows_here = (row_lane >= receiver * row_blocks) & (row_lane < (receiver + 1) * row_blocks)
        high = jnp.max(jnp.max(jnp.where(hit, local, 0), axis=0), axis=0, keepdims=True)
        return jnp.max(jnp.where(rows_here, high, 0))

    for lev in range(levels):
        small[lev] = row_pick(a, lev * PAIR + x)
        small[levels + lev] = row_pick(partner, lev * PAIR + x)
    for owner in range(nb):
        small[2 * levels + owner] = extremes(c, owner)[0]
    far = jnp.where(z == levels - 2, levels - 1, 0)
    opposite = levels - 1 - far
    for side in range(PAIR):
        small[2 * levels + nb + side] = row_pick(far * PAIR + (x + side) % PAIR, opposite * PAIR + x)
    out_ref[...] = jnp.zeros_like(out_ref)

    offer(z, 0)

    def dense(load, codes, groups, per_group, put):
        def group(g, carry):
            totals = [jnp.zeros((blk, blk), jnp.float32) for _ in range(per_group)]
            for s in range(slots):
                value = load(s)
                for p in range(per_group):
                    totals[p] += value * jnp.where(codes[s] == g * per_group + p, 1.0, 0.0)
            for p in range(per_group):
                put(g, p, totals[p])
            return carry

        lax.fori_loop(0, groups, group, 0)

    def build_a(piece):
        k = piece // row_blocks
        i = piece % row_blocks
        codes = []
        for s in range(slots):
            entry = a_lists[s, k, a * row_blocks + i]
            owner = lax.div(entry, row_blocks)
            upper = owner - 2 * lax.div(owner, 2)
            place = owner - upper + jnp.maximum(upper - x, x - upper)
            codes.append((place + 1) * at_most(s, a_counts[k, a * row_blocks + i]) - 1)

        def load(s):
            return abuf[k, s, pl.ds(i * blk, blk), :].astype(jnp.float32)

        def put(g, p, total):
            at = pl.ds(k * rows + i * blk, blk)
            high = total.astype(jnp.bfloat16)
            adense[g, at, p * blk:(p + 1) * blk] = high
            adense[g, at, (PAIR + p) * blk:(PAIR + p + 1) * blk] = (total - high.astype(jnp.float32)).astype(jnp.bfloat16)

        dense(load, codes, levels, PAIR, put)

    def build_b(piece):
        k = piece // col_blocks
        r = piece % col_blocks
        codes = []
        for s in range(slots):
            entry = b_lists[s, k, c * col_blocks + r]
            owner = lax.div(entry, col_blocks)
            gap = entry - owner * col_blocks - small[2 * levels + owner]
            place = (owner ^ c) * FROM_B + jnp.minimum(jnp.maximum(gap, -gap), 1)
            codes.append((place + 1) * at_most(s, b_counts[k, c * col_blocks + r]) - 1)

        def load(s):
            return bbuf[k, s, pl.ds(r * blk, blk), :].astype(jnp.float32)

        def put(g, p, total):
            bdense[g, k, pl.ds(r * blk, blk), p * blk:(p + 1) * blk] = total.astype(jnp.bfloat16)

        dense(load, codes, nb, FROM_B, put)

    a_pieces = ops * row_blocks
    pieces = ops * col_blocks

    def build_some(first, count):
        def one(n, carry):
            @pl.when(n < pieces)
            def _():
                build_b(n)
            return carry

        lax.fori_loop(first, first + count, one, 0)

    def beta_wait(j):
        pltpu.make_async_remote_copy(
            src_ref=picks.at[j - 1], dst_ref=column.at[z, j], send_sem=beta_send.at[j - 1], recv_sem=beta_recv.at[j - 1],
            device_id={"beta": c ^ j}, device_id_type=MESH).wait_recv()

    copy_a.wait()

    def one_a(n, carry):
        build_a(n)
        return carry

    lax.fori_loop(0, a_pieces // 2, one_a, 0)
    built = 0
    for j in range(1, nb):
        beta_wait(j)
        own_relays(j)
        offer(z, j)
        if j == 1:
            lax.fori_loop(a_pieces // 2, a_pieces, one_a, 0)
            copy_b.wait()
        if j < nb - 1:
            build_some(built, 2 * j)
            built += 2 * j

    def product(lev, j, mine):
        across_copy(lev, j).wait_recv()
        other = across[lev, j]
        value = jnp.concatenate([mine, other, mine, other], axis=0)
        return jnp.dot(adense[lev], value, preferred_element_type=jnp.float32)

    def combine(lev, j):
        acc[j] += product(lev, j, selected(lev, j, small[lev]))

    tile = min(2, col_blocks) * blk

    def finish(j):
        inters = [acc[j, k * rows:(k + 1) * rows, :].astype(jnp.bfloat16) for k in range(ops)]

        def columns(n, carry):
            here = pl.ds(pl.multiple_of(n * tile, tile), tile)
            total = out_ref[:, here]
            for k in range(ops):
                total += lax.dot_general(inters[k], bdense[j, k, here, :], (((1,), (1,)), ((), ())),
                                         preferred_element_type=jnp.float32)
            out_ref[:, here] = total
            return carry

        lax.fori_loop(0, col_blocks * blk // tile, columns, 0)

    def straight_copy(j):
        return pltpu.make_async_remote_copy(
            src_ref=straight.at[0, j], dst_ref=tail.at[j], send_sem=straight_send.at[0, j], recv_sem=tail_recv.at[j],
            device_id={"alpha": far * PAIR + x}, device_id_type=MESH)

    def diagonal_copy(j):
        return pltpu.make_async_remote_copy(
            src_ref=straight.at[1, j], dst_ref=across.at[opposite, j], send_sem=straight_send.at[1, j], recv_sem=across_recv.at[opposite, j],
            device_id={"alpha": far * PAIR + 1 - x}, device_id_type=MESH)

    def arrive(lev, j, below):
        pltpu.make_async_remote_copy(
            src_ref=column.at[lev, j], dst_ref=column.at[lev, j], send_sem=up_send.at[lev, j], recv_sem=column_recv.at[lev, j],
            device_id={"alpha": partner}, device_id_type=MESH).wait_recv()
        last = (z == levels - 2) & (lev == 0) if below else (z == 1) & (lev == levels - 1)

        @pl.when(last)
        def _():
            straight[1, j] = selected(lev, j, small[2 * levels + nb + 1])
            diagonal_copy(j).start()
            straight[0, j] = selected(lev, j, small[2 * levels + nb])
            straight_copy(j).start()

        if below:
            @pl.when((z < levels - 1) & jnp.logical_not(last))
            def _():
                up_copy(lev, j).start()
        else:
            @pl.when((z > 0) & jnp.logical_not(last))
            def _():
                down_copy(lev, j).start()

        offer(lev, j)

    relayed = (levels - 2) * nb
    at_end = (z == 0) | (z == levels - 1)

    def step(i, carry, final=False):
        j = i % nb
        distance = i // nb + 1

        @pl.when((i < relayed) & (z - distance >= 0))
        def _():
            arrive(z - distance, j, True)

        @pl.when((i < relayed) & (z + distance < levels))
        def _():
            arrive(z + distance, j, False)

        @pl.when(i < nb)
        def _():
            acc[j] = product(z, j, selected(z, j, small[z]))

        before = jnp.maximum(i - 1, 0)
        j_before = before % nb
        distance_before = before // nb + 1

        @pl.when((i > 0) & (i <= relayed) & (z - distance_before >= 0))
        def _():
            combine(z - distance_before, j_before)

        @pl.when((i > 0) & (i <= relayed) & (z + distance_before < levels))
        def _():
            combine(z + distance_before, j_before)

        build_some(built + 2 * i, 2)

        @pl.when(i >= relayed)
        def _():
            @pl.when(at_end)
            def _():
                pltpu.make_async_remote_copy(
                    src_ref=straight.at[0, j], dst_ref=tail.at[j], send_sem=straight_send.at[0, j], recv_sem=tail_recv.at[j],
                    device_id={"alpha": partner}, device_id_type=MESH).wait_recv()
                lev = levels - 1 - z
                acc[j] += product(lev, j, tail[j])

            if final:
                for k in range(ops):
                    last_ref[k] = acc[j, k * rows:(k + 1) * rows, :].astype(jnp.bfloat16)
            else:
                finish(j)

        return carry

    lax.fori_loop(0, relayed + nb - 1, step, 0)

    def drain(n, carry):
        lev = n // nb
        j = n % nb
        up_last = (z == levels - 2) & (lev == 0)
        down_last = (z == 1) & (lev == levels - 1)

        @pl.when((lev <= z) & (z < levels - 1) & jnp.logical_not(up_last))
        def _():
            up_copy(lev, j).wait_send()

        @pl.when((lev >= z) & (z > 0) & jnp.logical_not(down_last))
        def _():
            down_copy(lev, j).wait_send()

        @pl.when(up_last | down_last)
        def _():
            straight_copy(j).wait_send()
            diagonal_copy(j).wait_send()

        @pl.when(jnp.logical_not(at_end & (lev == levels - 1 - z)))
        def _():
            across_copy(lev, j).wait_send()

        return carry

    def drain_all():
        for j in range(1, nb):
            beta_copy(j).wait_send()
        lax.fori_loop(0, levels * nb, drain, 0)

    @pl.when(at_end)
    def _():
        drain_all()

    last_b_ref[...] = bdense[nb - 1]
    step(relayed + nb - 1, 0, True)

    @pl.when(jnp.logical_not(at_end))
    def _():
        drain_all()


def close_kernel(tile, part, last, last_b, out_hbm, staged, sems):
    copies = []
    for n in range(part.shape[1] // tile):
        here = slice(n * tile, (n + 1) * tile)
        staged[n] = part[:, here] + sum(lax.dot_general(last[k], last_b[k, here, :], (((1,), (1,)), ((), ())), preferred_element_type=jnp.float32) for k in range(last.shape[0]))
        copies.append(pltpu.make_async_copy(staged.at[n], out_hbm.at[:, here], sems.at[n]))
        copies[-1].start()
    for copy in copies:
        copy.wait()


def scratch_of(geometry, dtype):
    na, nb, ops, slots, blk, row_blocks, col_blocks = geometry
    levels = na // PAIR
    rows, cols, wide = row_blocks * blk, col_blocks * blk, FROM_B * blk
    return [
        ((col_blocks, rows, blk), dtype),
        ((ops, slots, rows, blk), dtype),
        ((ops, slots, cols, blk), dtype),
        ((nb - 1, rows, wide), dtype),
        ((levels, nb, rows, wide), dtype),
        ((levels, nb, blk, wide), dtype),
        ((levels, nb, blk, wide), dtype),
        ((PAIR, nb, blk, wide), dtype),
        ((nb, blk, wide), dtype),
        ((levels, ops * rows, 2 * PAIR * blk), dtype),
        ((nb, ops, cols, wide), dtype),
        ((nb, ops * rows, wide), jnp.float32),
    ]


def scratch_bytes(geometry):
    total = 0
    for shape, dtype in scratch_of(geometry, jnp.bfloat16):
        size = jnp.dtype(dtype).itemsize
        for extent in shape:
            size *= extent
        total += size
    return total


def fused(geometry, coeffs, a_blocks, a_list, a_count, b_blocks, b_list, b_count):
    na, nb, ops, slots, blk, row_blocks, col_blocks = geometry
    levels = na // PAIR
    a_lists = jnp.transpose(a_list, (2, 0, 1))
    b_lists = jnp.transpose(b_list, (2, 0, 1))
    rows, cols = row_blocks * blk, col_blocks * blk
    dma = pltpu.SemaphoreType.DMA
    vmem = pl.BlockSpec(memory_space=pltpu.VMEM)
    held = pl.pallas_call(
        functools.partial(sigma_kernel, geometry),
        out_shape=(pltpu.VMEM((rows, cols), jnp.float32), pltpu.VMEM((ops, rows, FROM_B * blk), coeffs.dtype), pltpu.VMEM((ops, cols, FROM_B * blk), coeffs.dtype)),
        in_specs=[pl.BlockSpec(memory_space=pltpu.HBM)] * 7,
        out_specs=(vmem, vmem, vmem),
        scratch_shapes=[
            pltpu.SMEM(a_lists.shape, jnp.int32), pltpu.SMEM(a_count.shape, jnp.int32), pltpu.SMEM(b_lists.shape, jnp.int32),
            pltpu.SMEM(b_count.shape, jnp.int32), pltpu.VMEM(a_lists.shape, jnp.int32), pltpu.VMEM(b_lists.shape, jnp.int32),
        ] + [pltpu.VMEM(shape, dtype) for shape, dtype in scratch_of(geometry, coeffs.dtype)] + [
            pltpu.SMEM((2 * levels + nb + PAIR,), jnp.int32),
            dma((6,)), dma((2 + col_blocks,)), dma((nb - 1,)), dma((nb - 1,)), dma((levels, nb)), dma((levels, nb)), dma((levels, nb)),
            dma((levels, nb)), dma((levels, nb)), dma((PAIR, nb)), dma((nb,)),
        ],
        compiler_params=pltpu.CompilerParams(collective_id=0, has_side_effects=True, vmem_limit_bytes=KERNEL_LIMIT),
        name="sigma_build",
    )(*[pltpu.with_memory_space_constraint(v, pltpu.HBM) for v in (a_lists, a_count, b_lists, b_count, coeffs, jnp.transpose(a_blocks, (0, 2, 1, 3)), jnp.transpose(b_blocks, (0, 2, 1, 3)))])
    tile = min(2, cols // blk) * blk
    return pl.pallas_call(
        functools.partial(close_kernel, tile),
        out_shape=jax.ShapeDtypeStruct((rows, cols), jnp.float32),
        in_specs=[vmem, vmem, vmem],
        out_specs=pl.BlockSpec(memory_space=pltpu.HBM),
        scratch_shapes=[pltpu.VMEM((cols // tile, rows, tile), jnp.float32), dma((cols // tile,))],
        compiler_params=pltpu.CompilerParams(vmem_limit_bytes=8 * 1024 * 1024),
        name="close_sigma",
    )(*held)


def arrange(entries, owners, per_owner, capacity):
    operators, total, list_slots = entries.shape
    flattened = entries.reshape(operators, owners, per_owner * list_slots)
    matches = flattened[..., None] == jnp.arange(total, dtype=jnp.int32)
    present = jnp.any(matches, axis=(0, 2)).reshape(owners, owners, per_owner).astype(jnp.int32)
    ranking = jnp.cumsum(present, axis=2)
    position = jnp.arange(capacity, dtype=jnp.int32) + 1
    chosen_bits = (present[..., None] == 1) & (ranking[..., None] == position)
    local_ids = jnp.arange(per_owner, dtype=jnp.int32)[None, None, :, None]
    wanted = jnp.sum(local_ids * chosen_bits.astype(jnp.int32), axis=2)
    return (wanted, ranking)


def locate(entries, ranking_here, per_owner, capacity):
    owner = entries // per_owner
    local_id = entries % per_owner
    return owner * capacity + ranking_here[owner, local_id] - 1


def pick_columns(pool_piece, index_piece):
    return pool_piece[:, index_piece]


def plain(coeffs, a_blocks, a_list, a_count, b_blocks, b_list, b_count):
    operators, local_rows, list_slots, block_size = a_blocks.shape
    local_cols = coeffs.shape[1]
    row_blocks = local_rows // block_size
    col_blocks = local_cols // block_size
    row_capacity = FROM_A
    col_capacity = FROM_B
    alpha_size = lax.axis_size("alpha")
    beta_size = lax.axis_size("beta")
    alpha_here = lax.axis_index("alpha")
    beta_here = lax.axis_index("beta")
    slot_ids = jnp.arange(list_slots, dtype=jnp.int32)
    alpha_mine = lax.dynamic_slice_in_dim(a_list, alpha_here * row_blocks, row_blocks, 1)
    alpha_counts = lax.dynamic_slice_in_dim(a_count, alpha_here * row_blocks, row_blocks, 1)
    alpha_valid = slot_ids < alpha_counts[..., None]
    alpha_kept = jnp.where(
        alpha_valid[:, :, None, :, None],
        a_blocks.reshape(operators, row_blocks, block_size, list_slots, block_size),
        jnp.zeros((), jnp.bfloat16),
    )
    wanted, ranking = arrange(a_list, alpha_size, row_blocks, row_capacity)
    outgoing = coeffs.reshape(row_blocks, block_size, local_cols)[wanted[:, alpha_here, :]]
    incoming = lax.all_to_all(outgoing, "alpha", split_axis=0, concat_axis=0, tiled=True)
    source_index = locate(alpha_mine, ranking[alpha_here], row_blocks, row_capacity)
    chosen = incoming.reshape(alpha_size * row_capacity, block_size, local_cols)[source_index]
    inter = jnp.einsum("kbrsi,kbsic->kbrc", alpha_kept, chosen, preferred_element_type=jnp.float32)
    inter = inter.astype(jnp.bfloat16).reshape(operators, local_rows, col_blocks, block_size)
    wanted_cols, ranking_cols = arrange(b_list, beta_size, col_blocks, col_capacity)
    outgoing_cols = inter[:, :, wanted_cols[:, beta_here, :], :]
    incoming_cols = lax.all_to_all(outgoing_cols, "beta", split_axis=2, concat_axis=2, tiled=True)
    beta_mine = lax.dynamic_slice_in_dim(b_list, beta_here * col_blocks, col_blocks, 1)
    beta_counts = lax.dynamic_slice_in_dim(b_count, beta_here * col_blocks, col_blocks, 1)
    beta_valid = slot_ids < beta_counts[..., None]
    beta_kept = jnp.where(
        beta_valid[:, :, None, :, None],
        b_blocks.reshape(operators, col_blocks, block_size, list_slots, block_size),
        jnp.zeros((), jnp.bfloat16),
    )
    source_cols = locate(beta_mine, ranking_cols[beta_here], col_blocks, col_capacity)
    pooled = incoming_cols.reshape(operators, local_rows, beta_size * col_capacity, block_size)
    picked = jax.vmap(pick_columns)(pooled, source_cols)
    sigma = jnp.einsum("kabsj,kbrsj->abr", picked, beta_kept, preferred_element_type=jnp.float32)
    return sigma.reshape(local_rows, local_cols)


def on_device(coeffs, a_blocks, a_list, a_count, b_blocks, b_list, b_count):
    operators, local_rows, list_slots, block_size = a_blocks.shape
    na, nb = lax.axis_size("alpha"), lax.axis_size("beta")
    geometry = (na, nb, operators, list_slots, block_size, local_rows // block_size, coeffs.shape[1] // block_size)
    fits = scratch_bytes(geometry) < VMEM_LIMIT * 3 // 4
    shaped = FROM_A == 1 and FROM_B == 2 and na % PAIR == 0 and na > 3 * PAIR and nb & (nb - 1) == 0 and nb > 1
    build = functools.partial(fused, geometry) if fits and shaped else plain
    return build(coeffs, a_blocks, a_list, a_count, b_blocks, b_list, b_count)


def solution(mesh):
    in_specs = (
        P("alpha", "beta"),
        P(None, "alpha", None, None),
        P(),
        P(),
        P(None, "beta", None, None),
        P(),
        P(),
    )
    out_specs = P("alpha", "beta")
    return jax.shard_map(
        on_device, mesh=mesh, in_specs=in_specs, out_specs=out_specs, check_vma=False
    )
```

```python
import functools

import jax
import jax.numpy as jnp
from jax import lax
from jax.experimental import pallas as pl
from jax.experimental.pallas import tpu as pltpu
from jax.sharding import PartitionSpec as P

FROM_A = 1
FROM_B = 2
PAIR = 2
LAG = 3
CORES = 2
VMEM_LIMIT = 60 * 1024 * 1024
KERNEL_LIMIT = 40 * 1024 * 1024
MESH = pl.DeviceIdType.MESH


def sigma_kernel(geometry, a_lists_hbm, a_counts_hbm, b_lists_hbm, b_counts_hbm, c_hbm, a_hbm, b_hbm, out_ref, last_ref, last_b_ref, a_lists, a_counts, b_lists, b_counts, a_vec, b_vec, cbuf, abuf, bbuf, picks, column, across, chosen,
                 straight, tail, adense, bdense, acc, small, table_sem, local_sem, beta_send, beta_recv, column_recv, up_send, down_send, across_send, across_recv,
                 straight_send, tail_recv, aside_send):
    na, nb, ops, slots, blk, row_blocks, col_blocks = geometry
    levels = na // PAIR
    rows = row_blocks * blk
    wide = FROM_B * blk
    a = lax.axis_index("alpha")
    c = lax.axis_index("beta")
    z = a // PAIR
    x = a % PAIR
    partner = a + 1 - 2 * x

    barrier = pltpu.get_barrier_semaphore()
    for j in range(1, nb):
        pl.semaphore_signal(barrier, inc=1, device_id={"beta": c ^ j}, device_id_type=MESH)
    pl.semaphore_signal(barrier, inc=1, device_id={"alpha": partner}, device_id_type=MESH)

    @pl.when(z < levels - 1)
    def _():
        pl.semaphore_signal(barrier, inc=1, device_id={"alpha": a + PAIR}, device_id_type=MESH)

    @pl.when(z > 0)
    def _():
        pl.semaphore_signal(barrier, inc=1, device_id={"alpha": a - PAIR}, device_id_type=MESH)

    tables = [(b_lists_hbm, b_vec), (a_lists_hbm, a_vec), (a_lists_hbm, a_lists), (a_counts_hbm, a_counts), (b_lists_hbm, b_lists), (b_counts_hbm, b_counts)]
    copies_t = [pltpu.make_async_copy(source, target, table_sem.at[n]) for n, (source, target) in enumerate(tables)]
    copies_c = [pltpu.make_async_copy(c_hbm.at[:, b * blk:(b + 1) * blk], cbuf.at[b], local_sem.at[2 + b]) for b in range(col_blocks)]
    copy_a = pltpu.make_async_copy(a_hbm, abuf, local_sem.at[0])
    copy_b = pltpu.make_async_copy(b_hbm, bbuf, local_sem.at[1])
    for copy in copies_t + copies_c:
        copy.start()
    copy_a.start()
    copy_b.start()
    copies_t[0].wait()

    lists = b_vec[...]
    lane = lax.broadcasted_iota(jnp.int32, (1, nb * col_blocks), 1)

    def extremes(receiver, owner):
        local = lists - owner * col_blocks
        hit = (local >= 0) & (local < col_blocks)
        rows_here = (lane >= receiver * col_blocks) & (lane < (receiver + 1) * col_blocks)
        low = jnp.min(jnp.min(jnp.where(hit, local, col_blocks), axis=0), axis=0, keepdims=True)
        high = jnp.max(jnp.max(jnp.where(hit, local, 0), axis=0), axis=0, keepdims=True)
        low = jnp.min(jnp.where(rows_here, low, col_blocks))
        high = jnp.max(jnp.where(rows_here, high, 0))
        return jnp.where(low < col_blocks, low, 0), high

    spans = [extremes(c ^ j, c) for j in range(nb)]
    for copy in copies_c:
        copy.wait()
    for j in range(nb):
        for u, block in enumerate(spans[j]):
            piece = cbuf[block]
            if j == 0:
                column[z, 0, :, u * blk:(u + 1) * blk] = piece
            else:
                picks[j - 1, :, u * blk:(u + 1) * blk] = piece

    neighbours = nb + jnp.where(z < levels - 1, 1, 0) + jnp.where(z > 0, 1, 0)
    pl.semaphore_wait(barrier, neighbours)

    def beta_copy(j):
        return pltpu.make_async_remote_copy(
            src_ref=picks.at[j - 1], dst_ref=column.at[z, j], send_sem=beta_send.at[j - 1], recv_sem=beta_recv.at[j - 1],
            device_id={"beta": c ^ j}, device_id_type=MESH)

    def up_copy(lev, j):
        return pltpu.make_async_remote_copy(
            src_ref=column.at[lev, j], dst_ref=column.at[lev, j], send_sem=up_send.at[lev, j], recv_sem=column_recv.at[lev, j],
            device_id={"alpha": a + PAIR}, device_id_type=MESH)

    def down_copy(lev, j):
        return pltpu.make_async_remote_copy(
            src_ref=column.at[lev, j], dst_ref=column.at[lev, j], send_sem=down_send.at[lev, j], recv_sem=column_recv.at[lev, j],
            device_id={"alpha": a - PAIR}, device_id_type=MESH)

    def across_copy(lev, j):
        return pltpu.make_async_remote_copy(
            src_ref=chosen.at[lev, j], dst_ref=across.at[lev, j], send_sem=across_send.at[lev, j], recv_sem=across_recv.at[lev, j],
            device_id={"alpha": partner}, device_id_type=MESH)

    def one_hot(value, place):
        gap = value - place
        return (1 - jnp.minimum(jnp.maximum(gap, -gap), 1)).astype(jnp.float32)

    def at_most(slot, count):
        return jnp.minimum(jnp.maximum(count - slot, 0), 1)

    def selected(lev, j, pick):
        total = jnp.zeros((blk, wide), jnp.float32)
        for i in range(row_blocks):
            total += column[lev, j, i * blk:(i + 1) * blk, :].astype(jnp.float32) * one_hot(pick, i)
        return total.astype(jnp.bfloat16)

    def offer(lev, j):
        chosen[lev, j] = selected(lev, j, small[levels + lev])
        across_copy(lev, j).start()

    def own_relays(j):
        @pl.when(z < levels - 1)
        def _():
            up_copy(z, j).start()

        @pl.when(z > 0)
        def _():
            down_copy(z, j).start()

    own_relays(0)
    for j in range(1, nb):
        beta_copy(j).start()
    for copy in copies_t[1:]:
        copy.wait()
    rows_list = a_vec[...]
    row_lane = lax.broadcasted_iota(jnp.int32, (1, na * row_blocks), 1)

    def row_pick(receiver, owner):
        local = rows_list - owner * row_blocks
        hit = (local >= 0) & (local < row_blocks)
        rows_here = (row_lane >= receiver * row_blocks) & (row_lane < (receiver + 1) * row_blocks)
        high = jnp.max(jnp.max(jnp.where(hit, local, 0), axis=0), axis=0, keepdims=True)
        return jnp.max(jnp.where(rows_here, high, 0))

    for lev in range(levels):
        small[lev] = row_pick(a, lev * PAIR + x)
        small[levels + lev] = row_pick(partner, lev * PAIR + x)
    for owner in range(nb):
        small[2 * levels + owner] = extremes(c, owner)[0]
    far = jnp.where(z == levels - 2, levels - 1, 0)
    opposite = levels - 1 - far
    for side in range(PAIR):
        small[2 * levels + nb + side] = row_pick(far * PAIR + (x + side) % PAIR, opposite * PAIR + x)
    out_ref[...] = jnp.zeros_like(out_ref)

    offer(z, 0)

    def dense(load, codes, groups, per_group, put):
        def group(g, carry):
            totals = [jnp.zeros((blk, blk), jnp.float32) for _ in range(per_group)]
            for s in range(slots):
                value = load(s)
                for p in range(per_group):
                    totals[p] += value * jnp.where(codes[s] == g * per_group + p, 1.0, 0.0)
            for p in range(per_group):
                put(g, p, totals[p])
            return carry

        lax.fori_loop(0, groups, group, 0)

    def build_a(piece):
        k = piece // row_blocks
        i = piece % row_blocks
        codes = []
        for s in range(slots):
            entry = a_lists[s, k, a * row_blocks + i]
            owner = lax.div(entry, row_blocks)
            upper = owner - 2 * lax.div(owner, 2)
            place = owner - upper + jnp.maximum(upper - x, x - upper)
            codes.append((place + 1) * at_most(s, a_counts[k, a * row_blocks + i]) - 1)

        def load(s):
            return abuf[k, s, pl.ds(i * blk, blk), :].astype(jnp.float32)

        def put(g, p, total):
            at = pl.ds(k * rows + i * blk, blk)
            high = total.astype(jnp.bfloat16)
            adense[g, at, p * blk:(p + 1) * blk] = high
            adense[g, at, (PAIR + p) * blk:(PAIR + p + 1) * blk] = (total - high.astype(jnp.float32)).astype(jnp.bfloat16)

        dense(load, codes, levels, PAIR, put)

    def build_b(piece):
        k = piece // col_blocks
        r = piece % col_blocks
        codes = []
        for s in range(slots):
            entry = b_lists[s, k, c * col_blocks + r]
            owner = lax.div(entry, col_blocks)
            gap = entry - owner * col_blocks - small[2 * levels + owner]
            place = (owner ^ c) * FROM_B + jnp.minimum(jnp.maximum(gap, -gap), 1)
            codes.append((place + 1) * at_most(s, b_counts[k, c * col_blocks + r]) - 1)

        def load(s):
            return bbuf[k, s, pl.ds(r * blk, blk), :].astype(jnp.float32)

        def put(g, p, total):
            bdense[g, k, pl.ds(r * blk, blk), p * blk:(p + 1) * blk] = total.astype(jnp.bfloat16)

        dense(load, codes, nb, FROM_B, put)

    a_pieces = ops * row_blocks
    pieces = ops * col_blocks

    def build_some(first, count):
        def one(n, carry):
            @pl.when(n < pieces)
            def _():
                build_b(n)
            return carry

        lax.fori_loop(first, first + count, one, 0)

    def beta_wait(j):
        pltpu.make_async_remote_copy(
            src_ref=picks.at[j - 1], dst_ref=column.at[z, j], send_sem=beta_send.at[j - 1], recv_sem=beta_recv.at[j - 1],
            device_id={"beta": c ^ j}, device_id_type=MESH).wait_recv()

    copy_a.wait()

    def one_a(n, carry):
        build_a(n)
        return carry

    lax.fori_loop(0, a_pieces // 2, one_a, 0)
    built = 0
    for j in range(1, nb):
        beta_wait(j)
        own_relays(j)
        offer(z, j)
        if j == 1:
            lax.fori_loop(a_pieces // 2, a_pieces, one_a, 0)
            copy_b.wait()
        if j < nb - 1:
            build_some(built, 2 * j)
            built += 2 * j

    def product(lev, j, mine):
        across_copy(lev, j).wait_recv()
        other = across[lev, j]
        value = jnp.concatenate([mine, other, mine, other], axis=0)
        return jnp.dot(adense[lev], value, preferred_element_type=jnp.float32)

    def combine(lev, j):
        acc[j] += product(lev, j, selected(lev, j, small[lev]))

    tile = min(2, col_blocks) * blk

    def finish(j):
        inters = [acc[j, k * rows:(k + 1) * rows, :].astype(jnp.bfloat16) for k in range(ops)]

        def columns(n, carry):
            here = pl.ds(pl.multiple_of(n * tile, tile), tile)
            total = out_ref[:, here]
            for k in range(ops):
                total += lax.dot_general(inters[k], bdense[j, k, here, :], (((1,), (1,)), ((), ())),
                                         preferred_element_type=jnp.float32)
            out_ref[:, here] = total
            return carry

        lax.fori_loop(0, col_blocks * blk // tile, columns, 0)

    def straight_copy(j):
        return pltpu.make_async_remote_copy(
            src_ref=straight.at[0, j], dst_ref=tail.at[j], send_sem=straight_send.at[0, j], recv_sem=tail_recv.at[j],
            device_id={"alpha": far * PAIR + x}, device_id_type=MESH)

    def diagonal_copy(j):
        return pltpu.make_async_remote_copy(
            src_ref=straight.at[1, j], dst_ref=across.at[opposite, j], send_sem=straight_send.at[1, j], recv_sem=across_recv.at[opposite, j],
            device_id={"alpha": far * PAIR + 1 - x}, device_id_type=MESH)

    lightened = (z == 1) & (c < CORES)
    forwards = (z == 1) & (c >= CORES) & (c < 2 * CORES)
    beside = jnp.where(c < CORES, c + CORES, jnp.where(c < 2 * CORES, c - CORES, c))

    def aside_copy():
        return pltpu.make_async_remote_copy(
            src_ref=straight.at[1 - x, 0], dst_ref=tail.at[0], send_sem=aside_send.at[0], recv_sem=tail_recv.at[0],
            device_id={"beta": beside}, device_id_type=MESH)

    def forward_crossing():
        return pltpu.make_async_remote_copy(
            src_ref=tail.at[0], dst_ref=across.at[levels - 1, 0], send_sem=aside_send.at[1], recv_sem=across_recv.at[levels - 1, 0],
            device_id={"alpha": a - 1, "beta": beside}, device_id_type=MESH)

    def forward_direct():
        return pltpu.make_async_remote_copy(
            src_ref=tail.at[0], dst_ref=tail.at[0], send_sem=aside_send.at[1], recv_sem=tail_recv.at[0],
            device_id={"alpha": a - PAIR, "beta": beside}, device_id_type=MESH)

    def arrive(lev, j, below):
        pltpu.make_async_remote_copy(
            src_ref=column.at[lev, j], dst_ref=column.at[lev, j], send_sem=up_send.at[lev, j], recv_sem=column_recv.at[lev, j],
            device_id={"alpha": partner}, device_id_type=MESH).wait_recv()
        last = (z == levels - 2) & (lev == 0) if below else (z == 1) & (lev == levels - 1)

        @pl.when(last)
        def _():
            straight[1, j] = selected(lev, j, small[2 * levels + nb + 1])
            straight[0, j] = selected(lev, j, small[2 * levels + nb])
            if below:
                diagonal_copy(j).start()
                straight_copy(j).start()
            else:
                turned = lightened & (j == 0)

                @pl.when(turned)
                def _():
                    aside_copy().start()

                @pl.when(jnp.logical_not(turned & (x == 0)))
                def _():
                    diagonal_copy(j).start()

                @pl.when(jnp.logical_not(turned & (x == 1)))
                def _():
                    straight_copy(j).start()

        if below:
            @pl.when((z < levels - 1) & jnp.logical_not(last))
            def _():
                up_copy(lev, j).start()
        else:
            @pl.when((z > 0) & jnp.logical_not(last))
            def _():
                down_copy(lev, j).start()

        offer(lev, j)

    relayed = (levels - 2) * nb
    at_end = (z == 0) | (z == levels - 1)

    def step(i, carry, final=False):
        j = i % nb
        distance = i // nb + 1

        @pl.when((i == relayed - nb + 1) & forwards)
        def _():
            aside_copy().wait_recv()

            @pl.when(x == 0)
            def _():
                forward_crossing().start()

            @pl.when(x == 1)
            def _():
                forward_direct().start()

        @pl.when((i < relayed) & (z - distance >= 0))
        def _():
            arrive(z - distance, j, True)

        @pl.when((i < relayed) & (z + distance < levels))
        def _():
            arrive(z + distance, j, False)

        own = jnp.maximum(i - 1, 0) % nb

        @pl.when((i > 0) & (i <= nb))
        def _():
            acc[own] = product(z, own, selected(z, own, small[z]))

        before = jnp.maximum(i - LAG, 0)
        j_before = before % nb
        distance_before = before // nb + 1

        @pl.when((i >= LAG) & (i < relayed + LAG) & (z - distance_before >= 0))
        def _():
            combine(z - distance_before, j_before)

        @pl.when((i >= LAG) & (i < relayed + LAG) & (z + distance_before < levels))
        def _():
            combine(z + distance_before, j_before)

        build_some(built + 2 * i, 2)


        early = i - (relayed + LAG - nb)

        @pl.when((early >= 0) & (early < nb - 1) & jnp.logical_not(at_end))
        def _():
            finish(early)

        @pl.when(i >= relayed)
        def _():
            @pl.when(at_end)
            def _():
                pltpu.make_async_remote_copy(
                    src_ref=straight.at[0, j], dst_ref=tail.at[j], send_sem=straight_send.at[0, j], recv_sem=tail_recv.at[j],
                    device_id={"alpha": partner}, device_id_type=MESH).wait_recv()
                lev = levels - 1 - z
                total = acc[j] + product(lev, j, tail[j])
                if final:
                    for k in range(ops):
                        last_ref[k] = total[k * rows:(k + 1) * rows].astype(jnp.bfloat16)
                else:
                    acc[j] = total

            if final:
                @pl.when(jnp.logical_not(at_end))
                def _():
                    for k in range(ops):
                        last_ref[k] = acc[j, k * rows:(k + 1) * rows, :].astype(jnp.bfloat16)
            else:
                @pl.when(at_end)
                def _():
                    finish(j)

        return carry

    lax.fori_loop(0, relayed + nb - 1, step, 0)

    def drain(n, carry):
        lev = n // nb
        j = n % nb
        up_last = (z == levels - 2) & (lev == 0)
        down_last = (z == 1) & (lev == levels - 1)

        @pl.when((lev <= z) & (z < levels - 1) & jnp.logical_not(up_last))
        def _():
            up_copy(lev, j).wait_send()

        @pl.when((lev >= z) & (z > 0) & jnp.logical_not(down_last))
        def _():
            down_copy(lev, j).wait_send()

        @pl.when(up_last | down_last)
        def _():
            turned = lightened & (j == 0)

            @pl.when(turned)
            def _():
                aside_copy().wait_send()

            @pl.when(jnp.logical_not(turned & (x == 1)))
            def _():
                straight_copy(j).wait_send()

            @pl.when(jnp.logical_not(turned & (x == 0)))
            def _():
                diagonal_copy(j).wait_send()

            @pl.when(forwards & (j == 0))
            def _():
                forward_direct().wait_send()

        @pl.when(jnp.logical_not(at_end & (lev == levels - 1 - z)))
        def _():
            across_copy(lev, j).wait_send()

        return carry

    def drain_all():
        for j in range(1, nb):
            beta_copy(j).wait_send()
        lax.fori_loop(0, levels * nb, drain, 0)

    @pl.when(at_end)
    def _():
        drain_all()

    last_b_ref[...] = bdense[nb - 1]
    step(relayed + nb - 1, 0, True)

    @pl.when(jnp.logical_not(at_end))
    def _():
        drain_all()


def close_kernel(tile, part, last, last_b, out_hbm, staged, sems):
    copies = []
    for n in range(part.shape[1] // tile):
        here = slice(n * tile, (n + 1) * tile)
        staged[n] = part[:, here] + sum(lax.dot_general(last[k], last_b[k, here, :], (((1,), (1,)), ((), ())), preferred_element_type=jnp.float32) for k in range(last.shape[0]))
        copies.append(pltpu.make_async_copy(staged.at[n], out_hbm.at[:, here], sems.at[n]))
        copies[-1].start()
    for copy in copies:
        copy.wait()


def scratch_of(geometry, dtype):
    na, nb, ops, slots, blk, row_blocks, col_blocks = geometry
    levels = na // PAIR
    rows, cols, wide = row_blocks * blk, col_blocks * blk, FROM_B * blk
    return [
        ((col_blocks, rows, blk), dtype),
        ((ops, slots, rows, blk), dtype),
        ((ops, slots, cols, blk), dtype),
        ((nb - 1, rows, wide), dtype),
        ((levels, nb, rows, wide), dtype),
        ((levels, nb, blk, wide), dtype),
        ((levels, nb, blk, wide), dtype),
        ((PAIR, nb, blk, wide), dtype),
        ((nb, blk, wide), dtype),
        ((levels, ops * rows, 2 * PAIR * blk), dtype),
        ((nb, ops, cols, wide), dtype),
        ((nb, ops * rows, wide), jnp.float32),
    ]


def scratch_bytes(geometry):
    total = 0
    for shape, dtype in scratch_of(geometry, jnp.bfloat16):
        size = jnp.dtype(dtype).itemsize
        for extent in shape:
            size *= extent
        total += size
    return total


def fused(geometry, coeffs, a_blocks, a_list, a_count, b_blocks, b_list, b_count):
    na, nb, ops, slots, blk, row_blocks, col_blocks = geometry
    levels = na // PAIR
    a_lists = jnp.transpose(a_list, (2, 0, 1))
    b_lists = jnp.transpose(b_list, (2, 0, 1))
    rows, cols = row_blocks * blk, col_blocks * blk
    dma = pltpu.SemaphoreType.DMA
    vmem = pl.BlockSpec(memory_space=pltpu.VMEM)
    held = pl.pallas_call(
        functools.partial(sigma_kernel, geometry),
        out_shape=(pltpu.VMEM((rows, cols), jnp.float32), pltpu.VMEM((ops, rows, FROM_B * blk), coeffs.dtype), pltpu.VMEM((ops, cols, FROM_B * blk), coeffs.dtype)),
        in_specs=[pl.BlockSpec(memory_space=pltpu.HBM)] * 7,
        out_specs=(vmem, vmem, vmem),
        scratch_shapes=[
            pltpu.SMEM(a_lists.shape, jnp.int32), pltpu.SMEM(a_count.shape, jnp.int32), pltpu.SMEM(b_lists.shape, jnp.int32),
            pltpu.SMEM(b_count.shape, jnp.int32), pltpu.VMEM(a_lists.shape, jnp.int32), pltpu.VMEM(b_lists.shape, jnp.int32),
        ] + [pltpu.VMEM(shape, dtype) for shape, dtype in scratch_of(geometry, coeffs.dtype)] + [
            pltpu.SMEM((2 * levels + nb + PAIR,), jnp.int32),
            dma((6,)), dma((2 + col_blocks,)), dma((nb - 1,)), dma((nb - 1,)), dma((levels, nb)), dma((levels, nb)), dma((levels, nb)),
            dma((levels, nb)), dma((levels, nb)), dma((PAIR, nb)), dma((nb,)), dma((2,)),
        ],
        compiler_params=pltpu.CompilerParams(collective_id=0, has_side_effects=True, vmem_limit_bytes=KERNEL_LIMIT),
        name="sigma_build",
    )(*[pltpu.with_memory_space_constraint(v, pltpu.HBM) for v in (a_lists, a_count, b_lists, b_count, coeffs, jnp.transpose(a_blocks, (0, 2, 1, 3)), jnp.transpose(b_blocks, (0, 2, 1, 3)))])
    tile = cols // 2
    return pl.pallas_call(
        functools.partial(close_kernel, tile),
        out_shape=jax.ShapeDtypeStruct((rows, cols), jnp.float32),
        in_specs=[vmem, vmem, vmem],
        out_specs=pl.BlockSpec(memory_space=pltpu.HBM),
        scratch_shapes=[pltpu.VMEM((cols // tile, rows, tile), jnp.float32), dma((cols // tile,))],
        compiler_params=pltpu.CompilerParams(vmem_limit_bytes=8 * 1024 * 1024),
        name="close_sigma",
    )(*held)


def arrange(entries, owners, per_owner, capacity):
    operators, total, list_slots = entries.shape
    flattened = entries.reshape(operators, owners, per_owner * list_slots)
    matches = flattened[..., None] == jnp.arange(total, dtype=jnp.int32)
    present = jnp.any(matches, axis=(0, 2)).reshape(owners, owners, per_owner).astype(jnp.int32)
    ranking = jnp.cumsum(present, axis=2)
    position = jnp.arange(capacity, dtype=jnp.int32) + 1
    chosen_bits = (present[..., None] == 1) & (ranking[..., None] == position)
    local_ids = jnp.arange(per_owner, dtype=jnp.int32)[None, None, :, None]
    wanted = jnp.sum(local_ids * chosen_bits.astype(jnp.int32), axis=2)
    return (wanted, ranking)


def locate(entries, ranking_here, per_owner, capacity):
    owner = entries // per_owner
    local_id = entries % per_owner
    return owner * capacity + ranking_here[owner, local_id] - 1


def pick_columns(pool_piece, index_piece):
    return pool_piece[:, index_piece]


def plain(coeffs, a_blocks, a_list, a_count, b_blocks, b_list, b_count):
    operators, local_rows, list_slots, block_size = a_blocks.shape
    local_cols = coeffs.shape[1]
    row_blocks = local_rows // block_size
    col_blocks = local_cols // block_size
    row_capacity = FROM_A
    col_capacity = FROM_B
    alpha_size = lax.axis_size("alpha")
    beta_size = lax.axis_size("beta")
    alpha_here = lax.axis_index("alpha")
    beta_here = lax.axis_index("beta")
    slot_ids = jnp.arange(list_slots, dtype=jnp.int32)
    alpha_mine = lax.dynamic_slice_in_dim(a_list, alpha_here * row_blocks, row_blocks, 1)
    alpha_counts = lax.dynamic_slice_in_dim(a_count, alpha_here * row_blocks, row_blocks, 1)
    alpha_valid = slot_ids < alpha_counts[..., None]
    alpha_kept = jnp.where(
        alpha_valid[:, :, None, :, None],
        a_blocks.reshape(operators, row_blocks, block_size, list_slots, block_size),
        jnp.zeros((), jnp.bfloat16),
    )
    wanted, ranking = arrange(a_list, alpha_size, row_blocks, row_capacity)
    outgoing = coeffs.reshape(row_blocks, block_size, local_cols)[wanted[:, alpha_here, :]]
    incoming = lax.all_to_all(outgoing, "alpha", split_axis=0, concat_axis=0, tiled=True)
    source_index = locate(alpha_mine, ranking[alpha_here], row_blocks, row_capacity)
    chosen = incoming.reshape(alpha_size * row_capacity, block_size, local_cols)[source_index]
    inter = jnp.einsum("kbrsi,kbsic->kbrc", alpha_kept, chosen, preferred_element_type=jnp.float32)
    inter = inter.astype(jnp.bfloat16).reshape(operators, local_rows, col_blocks, block_size)
    wanted_cols, ranking_cols = arrange(b_list, beta_size, col_blocks, col_capacity)
    outgoing_cols = inter[:, :, wanted_cols[:, beta_here, :], :]
    incoming_cols = lax.all_to_all(outgoing_cols, "beta", split_axis=2, concat_axis=2, tiled=True)
    beta_mine = lax.dynamic_slice_in_dim(b_list, beta_here * col_blocks, col_blocks, 1)
    beta_counts = lax.dynamic_slice_in_dim(b_count, beta_here * col_blocks, col_blocks, 1)
    beta_valid = slot_ids < beta_counts[..., None]
    beta_kept = jnp.where(
        beta_valid[:, :, None, :, None],
        b_blocks.reshape(operators, col_blocks, block_size, list_slots, block_size),
        jnp.zeros((), jnp.bfloat16),
    )
    source_cols = locate(beta_mine, ranking_cols[beta_here], col_blocks, col_capacity)
    pooled = incoming_cols.reshape(operators, local_rows, beta_size * col_capacity, block_size)
    picked = jax.vmap(pick_columns)(pooled, source_cols)
    sigma = jnp.einsum("kabsj,kbrsj->abr", picked, beta_kept, preferred_element_type=jnp.float32)
    return sigma.reshape(local_rows, local_cols)


def on_device(coeffs, a_blocks, a_list, a_count, b_blocks, b_list, b_count):
    operators, local_rows, list_slots, block_size = a_blocks.shape
    na, nb = lax.axis_size("alpha"), lax.axis_size("beta")
    geometry = (na, nb, operators, list_slots, block_size, local_rows // block_size, coeffs.shape[1] // block_size)
    fits = scratch_bytes(geometry) < VMEM_LIMIT * 3 // 4
    shaped = FROM_A == 1 and FROM_B == 2 and na % PAIR == 0 and na > 3 * PAIR and nb & (nb - 1) == 0 and nb >= 2 * CORES
    build = functools.partial(fused, geometry) if fits and shaped else plain
    return build(coeffs, a_blocks, a_list, a_count, b_blocks, b_list, b_count)


def solution(mesh):
    in_specs = (
        P("alpha", "beta"),
        P(None, "alpha", None, None),
        P(),
        P(),
        P(None, "beta", None, None),
        P(),
        P(),
    )
    out_specs = P("alpha", "beta")
    return jax.shard_map(
        on_device, mesh=mesh, in_specs=in_specs, out_specs=out_specs, check_vma=False
    )
```

```python
import functools

import jax
import jax.numpy as jnp
from jax import lax
from jax.experimental import pallas as pl
from jax.experimental.pallas import tpu as pltpu
from jax.sharding import PartitionSpec as P

FROM_A = 1
FROM_B = 2
PAIR = 2
LAG = 3
CORES = 2
VMEM_LIMIT = 60 * 1024 * 1024
KERNEL_LIMIT = 40 * 1024 * 1024
MESH = pl.DeviceIdType.MESH


def sigma_kernel(geometry, a_lists_hbm, a_counts_hbm, b_lists_hbm, b_counts_hbm, c_hbm, a_hbm, b_hbm, out_ref, last_ref, last_b_ref, a_lists, a_counts, b_lists, b_counts, a_vec, b_vec, cbuf, abuf, bbuf, picks, column, across, chosen,
                 straight, tail, adense, bdense, acc, small, table_sem, local_sem, beta_send, beta_recv, column_recv, up_send, down_send, across_send, across_recv,
                 straight_send, tail_recv, aside_send):
    na, nb, ops, slots, blk, row_blocks, col_blocks = geometry
    levels = na // PAIR
    rows = row_blocks * blk
    wide = FROM_B * blk
    a = lax.axis_index("alpha")
    c = lax.axis_index("beta")
    z = a // PAIR
    x = a % PAIR
    partner = a + 1 - 2 * x

    barrier = pltpu.get_barrier_semaphore()
    for j in range(1, nb):
        pl.semaphore_signal(barrier, inc=1, device_id={"beta": c ^ j}, device_id_type=MESH)
    pl.semaphore_signal(barrier, inc=1, device_id={"alpha": partner}, device_id_type=MESH)

    @pl.when(z < levels - 1)
    def _():
        pl.semaphore_signal(barrier, inc=1, device_id={"alpha": a + PAIR}, device_id_type=MESH)

    @pl.when(z > 0)
    def _():
        pl.semaphore_signal(barrier, inc=1, device_id={"alpha": a - PAIR}, device_id_type=MESH)

    tables = [(b_lists_hbm, b_vec), (a_lists_hbm, a_vec), (a_lists_hbm, a_lists), (a_counts_hbm, a_counts), (b_lists_hbm, b_lists), (b_counts_hbm, b_counts)]
    copies_t = [pltpu.make_async_copy(source, target, table_sem.at[n]) for n, (source, target) in enumerate(tables)]
    copies_c = [pltpu.make_async_copy(c_hbm.at[:, b * blk:(b + 1) * blk], cbuf.at[b], local_sem.at[2 + b]) for b in range(col_blocks)]
    copy_a = pltpu.make_async_copy(a_hbm, abuf, local_sem.at[0])
    copy_b = pltpu.make_async_copy(b_hbm, bbuf, local_sem.at[1])
    for copy in copies_t + copies_c:
        copy.start()
    copy_a.start()
    copy_b.start()
    copies_t[0].wait()

    lists = b_vec[...]
    lane = lax.broadcasted_iota(jnp.int32, (1, nb * col_blocks), 1)

    def extremes(receiver, owner):
        local = lists - owner * col_blocks
        hit = (local >= 0) & (local < col_blocks)
        rows_here = (lane >= receiver * col_blocks) & (lane < (receiver + 1) * col_blocks)
        low = jnp.min(jnp.min(jnp.where(hit, local, col_blocks), axis=0), axis=0, keepdims=True)
        high = jnp.max(jnp.max(jnp.where(hit, local, 0), axis=0), axis=0, keepdims=True)
        low = jnp.min(jnp.where(rows_here, low, col_blocks))
        high = jnp.max(jnp.where(rows_here, high, 0))
        return jnp.where(low < col_blocks, low, 0), high

    spans = [extremes(c ^ j, c) for j in range(nb)]
    for copy in copies_c:
        copy.wait()
    for j in range(nb):
        for u, block in enumerate(spans[j]):
            piece = cbuf[block]
            if j == 0:
                column[z, 0, :, u * blk:(u + 1) * blk] = piece
            else:
                picks[j - 1, :, u * blk:(u + 1) * blk] = piece

    neighbours = nb + jnp.where(z < levels - 1, 1, 0) + jnp.where(z > 0, 1, 0)
    pl.semaphore_wait(barrier, neighbours)

    def beta_copy(j):
        return pltpu.make_async_remote_copy(
            src_ref=picks.at[j - 1], dst_ref=column.at[z, j], send_sem=beta_send.at[j - 1], recv_sem=beta_recv.at[j - 1],
            device_id={"beta": c ^ j}, device_id_type=MESH)

    def up_copy(lev, j):
        return pltpu.make_async_remote_copy(
            src_ref=column.at[lev, j], dst_ref=column.at[lev, j], send_sem=up_send.at[lev, j], recv_sem=column_recv.at[lev, j],
            device_id={"alpha": a + PAIR}, device_id_type=MESH)

    def down_copy(lev, j):
        return pltpu.make_async_remote_copy(
            src_ref=column.at[lev, j], dst_ref=column.at[lev, j], send_sem=down_send.at[lev, j], recv_sem=column_recv.at[lev, j],
            device_id={"alpha": a - PAIR}, device_id_type=MESH)

    def across_copy(lev, j):
        return pltpu.make_async_remote_copy(
            src_ref=chosen.at[lev, j], dst_ref=across.at[lev, j], send_sem=across_send.at[lev, j], recv_sem=across_recv.at[lev, j],
            device_id={"alpha": partner}, device_id_type=MESH)

    def one_hot(value, place):
        gap = value - place
        return (1 - jnp.minimum(jnp.maximum(gap, -gap), 1)).astype(jnp.float32)

    def at_most(slot, count):
        return jnp.minimum(jnp.maximum(count - slot, 0), 1)

    def selected(lev, j, pick):
        total = jnp.zeros((blk, wide), jnp.float32)
        for i in range(row_blocks):
            total += column[lev, j, i * blk:(i + 1) * blk, :].astype(jnp.float32) * one_hot(pick, i)
        return total.astype(jnp.bfloat16)

    def offer(lev, j):
        chosen[lev, j] = selected(lev, j, small[levels + lev])
        across_copy(lev, j).start()

    def own_relays(j):
        @pl.when(z < levels - 1)
        def _():
            up_copy(z, j).start()

        @pl.when(z > 0)
        def _():
            down_copy(z, j).start()

    own_relays(0)
    for j in range(1, nb):
        beta_copy(j).start()
    for copy in copies_t[1:]:
        copy.wait()
    rows_list = a_vec[...]
    row_lane = lax.broadcasted_iota(jnp.int32, (1, na * row_blocks), 1)

    def row_pick(receiver, owner):
        local = rows_list - owner * row_blocks
        hit = (local >= 0) & (local < row_blocks)
        rows_here = (row_lane >= receiver * row_blocks) & (row_lane < (receiver + 1) * row_blocks)
        high = jnp.max(jnp.max(jnp.where(hit, local, 0), axis=0), axis=0, keepdims=True)
        return jnp.max(jnp.where(rows_here, high, 0))

    for lev in range(levels):
        small[lev] = row_pick(a, lev * PAIR + x)
        small[levels + lev] = row_pick(partner, lev * PAIR + x)
    for owner in range(nb):
        small[2 * levels + owner] = extremes(c, owner)[0]
    far = jnp.where(z == levels - 2, levels - 1, 0)
    opposite = levels - 1 - far
    for side in range(PAIR):
        small[2 * levels + nb + side] = row_pick(far * PAIR + (x + side) % PAIR, opposite * PAIR + x)
    out_ref[...] = jnp.zeros_like(out_ref)

    offer(z, 0)

    def dense(load, codes, groups, per_group, put):
        def group(g, carry):
            totals = [jnp.zeros((blk, blk), jnp.float32) for _ in range(per_group)]
            for s in range(slots):
                value = load(s)
                for p in range(per_group):
                    totals[p] += value * jnp.where(codes[s] == g * per_group + p, 1.0, 0.0)
            for p in range(per_group):
                put(g, p, totals[p])
            return carry

        lax.fori_loop(0, groups, group, 0)

    def build_a(piece):
        k = piece // row_blocks
        i = piece % row_blocks
        codes = []
        for s in range(slots):
            entry = a_lists[s, k, a * row_blocks + i]
            owner = lax.div(entry, row_blocks)
            upper = owner - 2 * lax.div(owner, 2)
            place = owner - upper + jnp.maximum(upper - x, x - upper)
            codes.append((place + 1) * at_most(s, a_counts[k, a * row_blocks + i]) - 1)

        def load(s):
            return abuf[k, s, pl.ds(i * blk, blk), :].astype(jnp.float32)

        def put(g, p, total):
            at = pl.ds(k * rows + i * blk, blk)
            high = total.astype(jnp.bfloat16)
            adense[g, at, p * blk:(p + 1) * blk] = high
            adense[g, at, (PAIR + p) * blk:(PAIR + p + 1) * blk] = (total - high.astype(jnp.float32)).astype(jnp.bfloat16)

        dense(load, codes, levels, PAIR, put)

    def build_b(piece):
        k = piece // col_blocks
        r = piece % col_blocks
        codes = []
        for s in range(slots):
            entry = b_lists[s, k, c * col_blocks + r]
            owner = lax.div(entry, col_blocks)
            gap = entry - owner * col_blocks - small[2 * levels + owner]
            place = (owner ^ c) * FROM_B + jnp.minimum(jnp.maximum(gap, -gap), 1)
            codes.append((place + 1) * at_most(s, b_counts[k, c * col_blocks + r]) - 1)

        def load(s):
            return bbuf[k, s, pl.ds(r * blk, blk), :].astype(jnp.float32)

        def put(g, p, total):
            bdense[g, k, pl.ds(r * blk, blk), p * blk:(p + 1) * blk] = total.astype(jnp.bfloat16)

        dense(load, codes, nb, FROM_B, put)

    a_pieces = ops * row_blocks
    pieces = ops * col_blocks

    def build_some(first, count):
        def one(n, carry):
            @pl.when(n < pieces)
            def _():
                build_b(n)
            return carry

        lax.fori_loop(first, first + count, one, 0)

    def beta_wait(j):
        pltpu.make_async_remote_copy(
            src_ref=picks.at[j - 1], dst_ref=column.at[z, j], send_sem=beta_send.at[j - 1], recv_sem=beta_recv.at[j - 1],
            device_id={"beta": c ^ j}, device_id_type=MESH).wait_recv()

    copy_a.wait()

    def one_a(n, carry):
        build_a(n)
        return carry

    lax.fori_loop(0, a_pieces // 2, one_a, 0)
    built = 0
    for j in range(1, nb):
        beta_wait(j)
        own_relays(j)
        offer(z, j)
        if j == 1:
            lax.fori_loop(a_pieces // 2, a_pieces, one_a, 0)
            copy_b.wait()
        if j < nb - 1:
            build_some(built, 2 * j)
            built += 2 * j

    def product(lev, j, mine):
        across_copy(lev, j).wait_recv()
        other = across[lev, j]
        value = jnp.concatenate([mine, other, mine, other], axis=0)
        return jnp.dot(adense[lev], value, preferred_element_type=jnp.float32)

    def combine(lev, j):
        acc[j] += product(lev, j, selected(lev, j, small[lev]))

    tile = min(2, col_blocks) * blk

    def finish(j):
        inters = [acc[j, k * rows:(k + 1) * rows, :].astype(jnp.bfloat16) for k in range(ops)]

        def columns(n, carry):
            here = pl.ds(pl.multiple_of(n * tile, tile), tile)
            total = out_ref[:, here]
            for k in range(ops):
                total += lax.dot_general(inters[k], bdense[j, k, here, :], (((1,), (1,)), ((), ())),
                                         preferred_element_type=jnp.float32)
            out_ref[:, here] = total
            return carry

        lax.fori_loop(0, col_blocks * blk // tile, columns, 0)

    def straight_copy(j):
        return pltpu.make_async_remote_copy(
            src_ref=straight.at[0, j], dst_ref=tail.at[j], send_sem=straight_send.at[0, j], recv_sem=tail_recv.at[j],
            device_id={"alpha": far * PAIR + x}, device_id_type=MESH)

    def diagonal_copy(j):
        return pltpu.make_async_remote_copy(
            src_ref=straight.at[1, j], dst_ref=across.at[opposite, j], send_sem=straight_send.at[1, j], recv_sem=across_recv.at[opposite, j],
            device_id={"alpha": far * PAIR + 1 - x}, device_id_type=MESH)

    lightened = (z == 1) & (c == 0)
    forwards = (z == 1) & (c == CORES)
    beside = jnp.where(c < CORES, c + CORES, jnp.where(c < 2 * CORES, c - CORES, c))

    def aside_copy():
        return pltpu.make_async_remote_copy(
            src_ref=straight.at[1 - x, 0], dst_ref=tail.at[0], send_sem=aside_send.at[0], recv_sem=tail_recv.at[0],
            device_id={"beta": beside}, device_id_type=MESH)

    def forward_crossing():
        return pltpu.make_async_remote_copy(
            src_ref=tail.at[0], dst_ref=across.at[levels - 1, 0], send_sem=aside_send.at[1], recv_sem=across_recv.at[levels - 1, 0],
            device_id={"alpha": a - 1, "beta": beside}, device_id_type=MESH)

    def forward_direct():
        return pltpu.make_async_remote_copy(
            src_ref=tail.at[0], dst_ref=tail.at[0], send_sem=aside_send.at[1], recv_sem=tail_recv.at[0],
            device_id={"alpha": a - PAIR, "beta": beside}, device_id_type=MESH)

    def arrive(lev, j, below):
        pltpu.make_async_remote_copy(
            src_ref=column.at[lev, j], dst_ref=column.at[lev, j], send_sem=up_send.at[lev, j], recv_sem=column_recv.at[lev, j],
            device_id={"alpha": partner}, device_id_type=MESH).wait_recv()
        last = (z == levels - 2) & (lev == 0) if below else (z == 1) & (lev == levels - 1)

        @pl.when(last)
        def _():
            straight[1, j] = selected(lev, j, small[2 * levels + nb + 1])
            straight[0, j] = selected(lev, j, small[2 * levels + nb])
            if below:
                diagonal_copy(j).start()
                straight_copy(j).start()
            else:
                ahead = (c < CORES) & (x == 0)
                behind = (c < CORES) & (x == 1)
                previous = jnp.maximum(j - 1, 0)
                kept = (j > 1) | ((j == 1) & jnp.logical_not(lightened))

                @pl.when(lightened & (j == 0))
                def _():
                    aside_copy().start()

                @pl.when(ahead)
                def _():
                    straight_copy(j).start()

                    @pl.when(kept)
                    def _():
                        diagonal_copy(previous).start()

                    @pl.when(j == nb - 1)
                    def _():
                        diagonal_copy(j).start()

                @pl.when(jnp.logical_not(ahead))
                def _():
                    diagonal_copy(j).start()

                @pl.when(behind & kept)
                def _():
                    straight_copy(previous).start()

                @pl.when(jnp.logical_not(ahead) & (jnp.logical_not(behind) | (j == nb - 1)))
                def _():
                    straight_copy(j).start()

        if below:
            @pl.when((z < levels - 1) & jnp.logical_not(last))
            def _():
                up_copy(lev, j).start()
        else:
            @pl.when((z > 0) & jnp.logical_not(last))
            def _():
                down_copy(lev, j).start()

        offer(lev, j)

    relayed = (levels - 2) * nb
    at_end = (z == 0) | (z == levels - 1)

    def step(i, carry, final=False):
        j = i % nb
        distance = i // nb + 1

        @pl.when((i == relayed - nb + 1) & forwards)
        def _():
            aside_copy().wait_recv()

            @pl.when(x == 0)
            def _():
                forward_crossing().start()

            @pl.when(x == 1)
            def _():
                forward_direct().start()

        @pl.when((i < relayed) & (z - distance >= 0))
        def _():
            arrive(z - distance, j, True)

        @pl.when((i < relayed) & (z + distance < levels))
        def _():
            arrive(z + distance, j, False)

        own = jnp.maximum(i - 1, 0) % nb

        @pl.when((i > 0) & (i <= nb))
        def _():
            acc[own] = product(z, own, selected(z, own, small[z]))

        before = jnp.maximum(i - LAG, 0)
        j_before = before % nb
        distance_before = before // nb + 1

        @pl.when((i >= LAG) & (i < relayed + LAG) & (z - distance_before >= 0))
        def _():
            combine(z - distance_before, j_before)

        @pl.when((i >= LAG) & (i < relayed + LAG) & (z + distance_before < levels))
        def _():
            combine(z + distance_before, j_before)

        build_some(built + 2 * i, 2)


        early = i - (relayed + LAG - nb)

        @pl.when((early >= 0) & (early < nb - 1) & jnp.logical_not(at_end))
        def _():
            finish(early)

        @pl.when(i >= relayed)
        def _():
            @pl.when(at_end)
            def _():
                pltpu.make_async_remote_copy(
                    src_ref=straight.at[0, j], dst_ref=tail.at[j], send_sem=straight_send.at[0, j], recv_sem=tail_recv.at[j],
                    device_id={"alpha": partner}, device_id_type=MESH).wait_recv()
                lev = levels - 1 - z
                total = acc[j] + product(lev, j, tail[j])
                if final:
                    for k in range(ops):
                        last_ref[k] = total[k * rows:(k + 1) * rows].astype(jnp.bfloat16)
                else:
                    acc[j] = total

            if final:
                @pl.when(jnp.logical_not(at_end))
                def _():
                    for k in range(ops):
                        last_ref[k] = acc[j, k * rows:(k + 1) * rows, :].astype(jnp.bfloat16)
            else:
                @pl.when(at_end)
                def _():
                    finish(j)

        return carry

    lax.fori_loop(0, relayed + nb - 1, step, 0)

    def drain(n, carry):
        lev = n // nb
        j = n % nb
        up_last = (z == levels - 2) & (lev == 0)
        down_last = (z == 1) & (lev == levels - 1)

        @pl.when((lev <= z) & (z < levels - 1) & jnp.logical_not(up_last))
        def _():
            up_copy(lev, j).wait_send()

        @pl.when((lev >= z) & (z > 0) & jnp.logical_not(down_last))
        def _():
            down_copy(lev, j).wait_send()

        @pl.when(up_last | down_last)
        def _():
            turned = lightened & (j == 0)

            @pl.when(turned)
            def _():
                aside_copy().wait_send()

            @pl.when(jnp.logical_not(turned & (x == 1)))
            def _():
                straight_copy(j).wait_send()

            @pl.when(jnp.logical_not(turned & (x == 0)))
            def _():
                diagonal_copy(j).wait_send()

            @pl.when(forwards & (j == 0))
            def _():
                forward_direct().wait_send()

        @pl.when(jnp.logical_not(at_end & (lev == levels - 1 - z)))
        def _():
            across_copy(lev, j).wait_send()

        return carry

    def drain_all():
        for j in range(1, nb):
            beta_copy(j).wait_send()
        lax.fori_loop(0, levels * nb, drain, 0)

    @pl.when(at_end)
    def _():
        drain_all()

    last_b_ref[...] = bdense[nb - 1]
    step(relayed + nb - 1, 0, True)

    @pl.when(jnp.logical_not(at_end))
    def _():
        drain_all()


def close_kernel(tile, part, last, last_b, out_hbm, staged, sems):
    copies = []
    for n in range(part.shape[1] // tile):
        here = slice(n * tile, (n + 1) * tile)
        staged[n] = part[:, here] + sum(lax.dot_general(last[k], last_b[k, here, :], (((1,), (1,)), ((), ())), preferred_element_type=jnp.float32) for k in range(last.shape[0]))
        copies.append(pltpu.make_async_copy(staged.at[n], out_hbm.at[:, here], sems.at[n]))
        copies[-1].start()
    for copy in copies:
        copy.wait()


def scratch_of(geometry, dtype):
    na, nb, ops, slots, blk, row_blocks, col_blocks = geometry
    levels = na // PAIR
    rows, cols, wide = row_blocks * blk, col_blocks * blk, FROM_B * blk
    return [
        ((col_blocks, rows, blk), dtype),
        ((ops, slots, rows, blk), dtype),
        ((ops, slots, cols, blk), dtype),
        ((nb - 1, rows, wide), dtype),
        ((levels, nb, rows, wide), dtype),
        ((levels, nb, blk, wide), dtype),
        ((levels, nb, blk, wide), dtype),
        ((PAIR, nb, blk, wide), dtype),
        ((nb, blk, wide), dtype),
        ((levels, ops * rows, 2 * PAIR * blk), dtype),
        ((nb, ops, cols, wide), dtype),
        ((nb, ops * rows, wide), jnp.float32),
    ]


def scratch_bytes(geometry):
    total = 0
    for shape, dtype in scratch_of(geometry, jnp.bfloat16):
        size = jnp.dtype(dtype).itemsize
        for extent in shape:
            size *= extent
        total += size
    return total


def fused(geometry, coeffs, a_blocks, a_list, a_count, b_blocks, b_list, b_count):
    na, nb, ops, slots, blk, row_blocks, col_blocks = geometry
    levels = na // PAIR
    a_lists = jnp.transpose(a_list, (2, 0, 1))
    b_lists = jnp.transpose(b_list, (2, 0, 1))
    rows, cols = row_blocks * blk, col_blocks * blk
    dma = pltpu.SemaphoreType.DMA
    vmem = pl.BlockSpec(memory_space=pltpu.VMEM)
    held = pl.pallas_call(
        functools.partial(sigma_kernel, geometry),
        out_shape=(pltpu.VMEM((rows, cols), jnp.float32), pltpu.VMEM((ops, rows, FROM_B * blk), coeffs.dtype), pltpu.VMEM((ops, cols, FROM_B * blk), coeffs.dtype)),
        in_specs=[pl.BlockSpec(memory_space=pltpu.HBM)] * 7,
        out_specs=(vmem, vmem, vmem),
        scratch_shapes=[
            pltpu.SMEM(a_lists.shape, jnp.int32), pltpu.SMEM(a_count.shape, jnp.int32), pltpu.SMEM(b_lists.shape, jnp.int32),
            pltpu.SMEM(b_count.shape, jnp.int32), pltpu.VMEM(a_lists.shape, jnp.int32), pltpu.VMEM(b_lists.shape, jnp.int32),
        ] + [pltpu.VMEM(shape, dtype) for shape, dtype in scratch_of(geometry, coeffs.dtype)] + [
            pltpu.SMEM((2 * levels + nb + PAIR,), jnp.int32),
            dma((6,)), dma((2 + col_blocks,)), dma((nb - 1,)), dma((nb - 1,)), dma((levels, nb)), dma((levels, nb)), dma((levels, nb)),
            dma((levels, nb)), dma((levels, nb)), dma((PAIR, nb)), dma((nb,)), dma((2,)),
        ],
        compiler_params=pltpu.CompilerParams(collective_id=0, has_side_effects=True, vmem_limit_bytes=KERNEL_LIMIT),
        name="sigma_build",
    )(*[pltpu.with_memory_space_constraint(v, pltpu.HBM) for v in (a_lists, a_count, b_lists, b_count, coeffs, jnp.transpose(a_blocks, (0, 2, 1, 3)), jnp.transpose(b_blocks, (0, 2, 1, 3)))])
    tile = cols // 2
    return pl.pallas_call(
        functools.partial(close_kernel, tile),
        out_shape=jax.ShapeDtypeStruct((rows, cols), jnp.float32),
        in_specs=[vmem, vmem, vmem],
        out_specs=pl.BlockSpec(memory_space=pltpu.HBM),
        scratch_shapes=[pltpu.VMEM((cols // tile, rows, tile), jnp.float32), dma((cols // tile,))],
        compiler_params=pltpu.CompilerParams(vmem_limit_bytes=8 * 1024 * 1024),
        name="close_sigma",
    )(*held)


def arrange(entries, owners, per_owner, capacity):
    operators, total, list_slots = entries.shape
    flattened = entries.reshape(operators, owners, per_owner * list_slots)
    matches = flattened[..., None] == jnp.arange(total, dtype=jnp.int32)
    present = jnp.any(matches, axis=(0, 2)).reshape(owners, owners, per_owner).astype(jnp.int32)
    ranking = jnp.cumsum(present, axis=2)
    position = jnp.arange(capacity, dtype=jnp.int32) + 1
    chosen_bits = (present[..., None] == 1) & (ranking[..., None] == position)
    local_ids = jnp.arange(per_owner, dtype=jnp.int32)[None, None, :, None]
    wanted = jnp.sum(local_ids * chosen_bits.astype(jnp.int32), axis=2)
    return (wanted, ranking)


def locate(entries, ranking_here, per_owner, capacity):
    owner = entries // per_owner
    local_id = entries % per_owner
    return owner * capacity + ranking_here[owner, local_id] - 1


def pick_columns(pool_piece, index_piece):
    return pool_piece[:, index_piece]


def plain(coeffs, a_blocks, a_list, a_count, b_blocks, b_list, b_count):
    operators, local_rows, list_slots, block_size = a_blocks.shape
    local_cols = coeffs.shape[1]
    row_blocks = local_rows // block_size
    col_blocks = local_cols // block_size
    row_capacity = FROM_A
    col_capacity = FROM_B
    alpha_size = lax.axis_size("alpha")
    beta_size = lax.axis_size("beta")
    alpha_here = lax.axis_index("alpha")
    beta_here = lax.axis_index("beta")
    slot_ids = jnp.arange(list_slots, dtype=jnp.int32)
    alpha_mine = lax.dynamic_slice_in_dim(a_list, alpha_here * row_blocks, row_blocks, 1)
    alpha_counts = lax.dynamic_slice_in_dim(a_count, alpha_here * row_blocks, row_blocks, 1)
    alpha_valid = slot_ids < alpha_counts[..., None]
    alpha_kept = jnp.where(
        alpha_valid[:, :, None, :, None],
        a_blocks.reshape(operators, row_blocks, block_size, list_slots, block_size),
        jnp.zeros((), jnp.bfloat16),
    )
    wanted, ranking = arrange(a_list, alpha_size, row_blocks, row_capacity)
    outgoing = coeffs.reshape(row_blocks, block_size, local_cols)[wanted[:, alpha_here, :]]
    incoming = lax.all_to_all(outgoing, "alpha", split_axis=0, concat_axis=0, tiled=True)
    source_index = locate(alpha_mine, ranking[alpha_here], row_blocks, row_capacity)
    chosen = incoming.reshape(alpha_size * row_capacity, block_size, local_cols)[source_index]
    inter = jnp.einsum("kbrsi,kbsic->kbrc", alpha_kept, chosen, preferred_element_type=jnp.float32)
    inter = inter.astype(jnp.bfloat16).reshape(operators, local_rows, col_blocks, block_size)
    wanted_cols, ranking_cols = arrange(b_list, beta_size, col_blocks, col_capacity)
    outgoing_cols = inter[:, :, wanted_cols[:, beta_here, :], :]
    incoming_cols = lax.all_to_all(outgoing_cols, "beta", split_axis=2, concat_axis=2, tiled=True)
    beta_mine = lax.dynamic_slice_in_dim(b_list, beta_here * col_blocks, col_blocks, 1)
    beta_counts = lax.dynamic_slice_in_dim(b_count, beta_here * col_blocks, col_blocks, 1)
    beta_valid = slot_ids < beta_counts[..., None]
    beta_kept = jnp.where(
        beta_valid[:, :, None, :, None],
        b_blocks.reshape(operators, col_blocks, block_size, list_slots, block_size),
        jnp.zeros((), jnp.bfloat16),
    )
    source_cols = locate(beta_mine, ranking_cols[beta_here], col_blocks, col_capacity)
    pooled = incoming_cols.reshape(operators, local_rows, beta_size * col_capacity, block_size)
    picked = jax.vmap(pick_columns)(pooled, source_cols)
    sigma = jnp.einsum("kabsj,kbrsj->abr", picked, beta_kept, preferred_element_type=jnp.float32)
    return sigma.reshape(local_rows, local_cols)


def on_device(coeffs, a_blocks, a_list, a_count, b_blocks, b_list, b_count):
    operators, local_rows, list_slots, block_size = a_blocks.shape
    na, nb = lax.axis_size("alpha"), lax.axis_size("beta")
    geometry = (na, nb, operators, list_slots, block_size, local_rows // block_size, coeffs.shape[1] // block_size)
    fits = scratch_bytes(geometry) < KERNEL_LIMIT * 3 // 4
    shaped = FROM_A == 1 and FROM_B == 2 and na % PAIR == 0 and na > 3 * PAIR and nb & (nb - 1) == 0 and nb >= 2 * CORES
    build = functools.partial(fused, geometry) if fits and shaped else plain
    return build(coeffs, a_blocks, a_list, a_count, b_blocks, b_list, b_count)


def solution(mesh):
    in_specs = (
        P("alpha", "beta"),
        P(None, "alpha", None, None),
        P(),
        P(),
        P(None, "beta", None, None),
        P(),
        P(),
    )
    out_specs = P("alpha", "beta")
    return jax.shard_map(
        on_device, mesh=mesh, in_specs=in_specs, out_specs=out_specs, check_vma=False
    )
```

```python
import functools

import jax
import jax.numpy as jnp
from jax import lax
from jax.experimental import pallas as pl
from jax.experimental.pallas import tpu as pltpu
from jax.sharding import PartitionSpec as P

FROM_A = 1
FROM_B = 2
PAIR = 2
CORES = 2
LAG = 3
VMEM_LIMIT = 60 * 1024 * 1024
KERNEL_LIMIT = 40 * 1024 * 1024
MESH = pl.DeviceIdType.MESH


def sigma_kernel(geometry, a_lists_hbm, a_counts_hbm, b_lists_hbm, b_counts_hbm, c_hbm, a_hbm, b_hbm, out_ref, last_ref, last_b_ref, a_lists, a_counts, b_lists, b_counts, a_vec, b_vec, cbuf, abuf, bbuf, picks, column, across, chosen,
                 straight, tail, adense, bdense, acc, small, table_sem, local_sem, beta_send, beta_recv, column_recv, up_send, down_send, across_send, across_recv,
                 straight_send, tail_recv):
    na, nb, ops, slots, blk, row_blocks, col_blocks = geometry
    levels = na // PAIR
    rows = row_blocks * blk
    wide = FROM_B * blk
    a = lax.axis_index("alpha")
    c = lax.axis_index("beta")
    z = a // PAIR
    x = a % PAIR
    partner = a + 1 - 2 * x

    barrier = pltpu.get_barrier_semaphore()
    for j in range(1, nb):
        pl.semaphore_signal(barrier, inc=1, device_id={"beta": c ^ j}, device_id_type=MESH)
    pl.semaphore_signal(barrier, inc=1, device_id={"alpha": partner}, device_id_type=MESH)

    @pl.when(z < levels - 1)
    def _():
        pl.semaphore_signal(barrier, inc=1, device_id={"alpha": a + PAIR}, device_id_type=MESH)

    @pl.when(z > 0)
    def _():
        pl.semaphore_signal(barrier, inc=1, device_id={"alpha": a - PAIR}, device_id_type=MESH)

    tables = [(b_lists_hbm, b_vec), (a_lists_hbm, a_vec), (a_lists_hbm, a_lists), (a_counts_hbm, a_counts), (b_lists_hbm, b_lists), (b_counts_hbm, b_counts)]
    copies_t = [pltpu.make_async_copy(source, target, table_sem.at[n]) for n, (source, target) in enumerate(tables)]
    copies_c = [pltpu.make_async_copy(c_hbm.at[:, b * blk:(b + 1) * blk], cbuf.at[b], local_sem.at[2 + b]) for b in range(col_blocks)]
    copy_a = pltpu.make_async_copy(a_hbm, abuf, local_sem.at[0])
    copy_b = pltpu.make_async_copy(b_hbm, bbuf, local_sem.at[1])
    for copy in copies_t + copies_c:
        copy.start()
    copy_a.start()
    copy_b.start()
    copies_t[0].wait()

    lists = b_vec[...]
    lane = lax.broadcasted_iota(jnp.int32, (1, nb * col_blocks), 1)

    def extremes(receiver, owner):
        local = lists - owner * col_blocks
        hit = (local >= 0) & (local < col_blocks)
        rows_here = (lane >= receiver * col_blocks) & (lane < (receiver + 1) * col_blocks)
        low = jnp.min(jnp.min(jnp.where(hit, local, col_blocks), axis=0), axis=0, keepdims=True)
        high = jnp.max(jnp.max(jnp.where(hit, local, 0), axis=0), axis=0, keepdims=True)
        low = jnp.min(jnp.where(rows_here, low, col_blocks))
        high = jnp.max(jnp.where(rows_here, high, 0))
        return jnp.where(low < col_blocks, low, 0), high

    spans = [extremes(c ^ j, c) for j in range(nb)]
    for copy in copies_c:
        copy.wait()
    for j in range(nb):
        for u, block in enumerate(spans[j]):
            piece = cbuf[block]
            if j == 0:
                column[z, 0, :, u * blk:(u + 1) * blk] = piece
            else:
                picks[j - 1, :, u * blk:(u + 1) * blk] = piece

    neighbours = nb + jnp.where(z < levels - 1, 1, 0) + jnp.where(z > 0, 1, 0)
    pl.semaphore_wait(barrier, neighbours)

    def beta_copy(j):
        return pltpu.make_async_remote_copy(
            src_ref=picks.at[j - 1], dst_ref=column.at[z, j], send_sem=beta_send.at[j - 1], recv_sem=beta_recv.at[j - 1],
            device_id={"beta": c ^ j}, device_id_type=MESH)

    def up_copy(lev, j):
        return pltpu.make_async_remote_copy(
            src_ref=column.at[lev, j], dst_ref=column.at[lev, j], send_sem=up_send.at[lev, j], recv_sem=column_recv.at[lev, j],
            device_id={"alpha": a + PAIR}, device_id_type=MESH)

    def down_copy(lev, j):
        return pltpu.make_async_remote_copy(
            src_ref=column.at[lev, j], dst_ref=column.at[lev, j], send_sem=down_send.at[lev, j], recv_sem=column_recv.at[lev, j],
            device_id={"alpha": a - PAIR}, device_id_type=MESH)

    def across_copy(lev, j):
        return pltpu.make_async_remote_copy(
            src_ref=chosen.at[lev, j], dst_ref=across.at[lev, j], send_sem=across_send.at[lev, j], recv_sem=across_recv.at[lev, j],
            device_id={"alpha": partner}, device_id_type=MESH)

    def one_hot(value, place):
        gap = value - place
        return (1 - jnp.minimum(jnp.maximum(gap, -gap), 1)).astype(jnp.float32)

    def at_most(slot, count):
        return jnp.minimum(jnp.maximum(count - slot, 0), 1)

    def selected(lev, j, pick):
        total = jnp.zeros((blk, wide), jnp.float32)
        for i in range(row_blocks):
            total += column[lev, j, i * blk:(i + 1) * blk, :].astype(jnp.float32) * one_hot(pick, i)
        return total.astype(jnp.bfloat16)

    def offer(lev, j):
        chosen[lev, j] = selected(lev, j, small[levels + lev])
        across_copy(lev, j).start()

    def own_relays(j):
        @pl.when(z < levels - 1)
        def _():
            up_copy(z, j).start()

        @pl.when(z > 0)
        def _():
            down_copy(z, j).start()

    own_relays(0)
    for j in range(1, nb):
        beta_copy(j).start()
    for copy in copies_t[1:]:
        copy.wait()
    rows_list = a_vec[...]
    row_lane = lax.broadcasted_iota(jnp.int32, (1, na * row_blocks), 1)

    def row_pick(receiver, owner):
        local = rows_list - owner * row_blocks
        hit = (local >= 0) & (local < row_blocks)
        rows_here = (row_lane >= receiver * row_blocks) & (row_lane < (receiver + 1) * row_blocks)
        high = jnp.max(jnp.max(jnp.where(hit, local, 0), axis=0), axis=0, keepdims=True)
        return jnp.max(jnp.where(rows_here, high, 0))

    for lev in range(levels):
        small[lev] = row_pick(a, lev * PAIR + x)
        small[levels + lev] = row_pick(partner, lev * PAIR + x)
    for owner in range(nb):
        small[2 * levels + owner] = extremes(c, owner)[0]
    far = jnp.where(z == levels - 2, levels - 1, 0)
    opposite = levels - 1 - far
    for side in range(PAIR):
        small[2 * levels + nb + side] = row_pick(far * PAIR + (x + side) % PAIR, opposite * PAIR + x)
    out_ref[...] = jnp.zeros_like(out_ref)

    offer(z, 0)

    def dense(load, codes, groups, per_group, put):
        def group(g, carry):
            totals = [jnp.zeros((blk, blk), jnp.float32) for _ in range(per_group)]
            for s in range(slots):
                value = load(s)
                for p in range(per_group):
                    totals[p] += value * jnp.where(codes[s] == g * per_group + p, 1.0, 0.0)
            for p in range(per_group):
                put(g, p, totals[p])
            return carry

        lax.fori_loop(0, groups, group, 0)

    def build_a(piece):
        k = piece // row_blocks
        i = piece % row_blocks
        codes = []
        for s in range(slots):
            entry = a_lists[s, k, a * row_blocks + i]
            owner = lax.div(entry, row_blocks)
            upper = owner - 2 * lax.div(owner, 2)
            place = owner - upper + jnp.maximum(upper - x, x - upper)
            codes.append((place + 1) * at_most(s, a_counts[k, a * row_blocks + i]) - 1)

        def load(s):
            return abuf[k, s, pl.ds(i * blk, blk), :].astype(jnp.float32)

        def put(g, p, total):
            at = pl.ds(k * rows + i * blk, blk)
            high = total.astype(jnp.bfloat16)
            adense[g, at, p * blk:(p + 1) * blk] = high
            adense[g, at, (PAIR + p) * blk:(PAIR + p + 1) * blk] = (total - high.astype(jnp.float32)).astype(jnp.bfloat16)

        dense(load, codes, levels, PAIR, put)

    def build_b(piece):
        k = piece // col_blocks
        r = piece % col_blocks
        codes = []
        for s in range(slots):
            entry = b_lists[s, k, c * col_blocks + r]
            owner = lax.div(entry, col_blocks)
            gap = entry - owner * col_blocks - small[2 * levels + owner]
            place = (owner ^ c) * FROM_B + jnp.minimum(jnp.maximum(gap, -gap), 1)
            codes.append((place + 1) * at_most(s, b_counts[k, c * col_blocks + r]) - 1)

        def load(s):
            return bbuf[k, s, pl.ds(r * blk, blk), :].astype(jnp.float32)

        def put(g, p, total):
            bdense[g, k, pl.ds(r * blk, blk), p * blk:(p + 1) * blk] = total.astype(jnp.bfloat16)

        dense(load, codes, nb, FROM_B, put)

    a_pieces = ops * row_blocks
    pieces = ops * col_blocks

    def build_some(first, count):
        def one(n, carry):
            @pl.when(n < pieces)
            def _():
                build_b(n)
            return carry

        lax.fori_loop(first, first + count, one, 0)

    def beta_wait(j):
        pltpu.make_async_remote_copy(
            src_ref=picks.at[j - 1], dst_ref=column.at[z, j], send_sem=beta_send.at[j - 1], recv_sem=beta_recv.at[j - 1],
            device_id={"beta": c ^ j}, device_id_type=MESH).wait_recv()

    copy_a.wait()

    def one_a(n, carry):
        build_a(n)
        return carry

    lax.fori_loop(0, a_pieces // 2, one_a, 0)
    built = 0
    for j in range(1, nb):
        beta_wait(j)
        own_relays(j)
        offer(z, j)
        if j == 1:
            lax.fori_loop(a_pieces // 2, a_pieces, one_a, 0)
            copy_b.wait()
        if j < nb - 1:
            build_some(built, 2 * j)
            built += 2 * j

    def product(lev, j, mine):
        across_copy(lev, j).wait_recv()
        other = across[lev, j]
        value = jnp.concatenate([mine, other, mine, other], axis=0)
        return jnp.dot(adense[lev], value, preferred_element_type=jnp.float32)

    def combine(lev, j):
        acc[j] += product(lev, j, selected(lev, j, small[lev]))

    tile = min(2, col_blocks) * blk

    def finish(j):
        inters = [acc[j, k * rows:(k + 1) * rows, :].astype(jnp.bfloat16) for k in range(ops)]

        def columns(n, carry):
            here = pl.ds(pl.multiple_of(n * tile, tile), tile)
            total = out_ref[:, here]
            for k in range(ops):
                total += lax.dot_general(inters[k], bdense[j, k, here, :], (((1,), (1,)), ((), ())),
                                         preferred_element_type=jnp.float32)
            out_ref[:, here] = total
            return carry

        lax.fori_loop(0, col_blocks * blk // tile, columns, 0)

    def straight_copy(j):
        return pltpu.make_async_remote_copy(
            src_ref=straight.at[0, j], dst_ref=tail.at[j], send_sem=straight_send.at[0, j], recv_sem=tail_recv.at[j],
            device_id={"alpha": far * PAIR + x}, device_id_type=MESH)

    def diagonal_copy(j):
        return pltpu.make_async_remote_copy(
            src_ref=straight.at[1, j], dst_ref=across.at[opposite, j], send_sem=straight_send.at[1, j], recv_sem=across_recv.at[opposite, j],
            device_id={"alpha": far * PAIR + 1 - x}, device_id_type=MESH)

    def arrive(lev, j, below):
        pltpu.make_async_remote_copy(
            src_ref=column.at[lev, j], dst_ref=column.at[lev, j], send_sem=up_send.at[lev, j], recv_sem=column_recv.at[lev, j],
            device_id={"alpha": partner}, device_id_type=MESH).wait_recv()
        last = (z == levels - 2) & (lev == 0) if below else (z == 1) & (lev == levels - 1)

        @pl.when(last)
        def _():
            straight[1, j] = selected(lev, j, small[2 * levels + nb + 1])
            straight[0, j] = selected(lev, j, small[2 * levels + nb])
            if below:
                diagonal_copy(j).start()
                straight_copy(j).start()
            else:
                ahead = (c < CORES) & (x == 0)
                behind = (c < CORES) & (x == 1)
                previous = jnp.maximum(j - 1, 0)

                @pl.when(ahead)
                def _():
                    straight_copy(j).start()

                    @pl.when(j > 0)
                    def _():
                        diagonal_copy(previous).start()

                    @pl.when(j == nb - 1)
                    def _():
                        diagonal_copy(j).start()

                @pl.when(jnp.logical_not(ahead))
                def _():
                    diagonal_copy(j).start()

                @pl.when(behind & (j > 0))
                def _():
                    straight_copy(previous).start()

                @pl.when(jnp.logical_not(ahead) & (jnp.logical_not(behind) | (j == nb - 1)))
                def _():
                    straight_copy(j).start()

        if below:
            @pl.when((z < levels - 1) & jnp.logical_not(last))
            def _():
                up_copy(lev, j).start()
        else:
            @pl.when((z > 0) & jnp.logical_not(last))
            def _():
                down_copy(lev, j).start()

        offer(lev, j)

    relayed = (levels - 2) * nb
    at_end = (z == 0) | (z == levels - 1)

    def step(i, carry, final=False):
        j = i % nb
        distance = i // nb + 1

        @pl.when((i < relayed) & (z - distance >= 0))
        def _():
            arrive(z - distance, j, True)

        @pl.when((i < relayed) & (z + distance < levels))
        def _():
            arrive(z + distance, j, False)

        own = jnp.maximum(i - 1, 0) % nb

        @pl.when((i > 0) & (i <= nb))
        def _():
            acc[own] = product(z, own, selected(z, own, small[z]))

        before = jnp.maximum(i - LAG, 0)
        j_before = before % nb
        distance_before = before // nb + 1

        @pl.when((i >= LAG) & (i < relayed + LAG) & (z - distance_before >= 0))
        def _():
            combine(z - distance_before, j_before)

        @pl.when((i >= LAG) & (i < relayed + LAG) & (z + distance_before < levels))
        def _():
            combine(z + distance_before, j_before)

        build_some(built + 2 * i, 2)

        early = i - (relayed + LAG - nb)

        @pl.when((early >= 0) & (early < nb - 1) & jnp.logical_not(at_end))
        def _():
            finish(early)

        @pl.when(i >= relayed)
        def _():
            @pl.when(at_end)
            def _():
                pltpu.make_async_remote_copy(
                    src_ref=straight.at[0, j], dst_ref=tail.at[j], send_sem=straight_send.at[0, j], recv_sem=tail_recv.at[j],
                    device_id={"alpha": partner}, device_id_type=MESH).wait_recv()
                lev = levels - 1 - z
                total = acc[j] + product(lev, j, tail[j])
                if final:
                    for k in range(ops):
                        last_ref[k] = total[k * rows:(k + 1) * rows].astype(jnp.bfloat16)
                else:
                    acc[j] = total

            if final:
                @pl.when(jnp.logical_not(at_end))
                def _():
                    for k in range(ops):
                        last_ref[k] = acc[j, k * rows:(k + 1) * rows, :].astype(jnp.bfloat16)
            else:
                @pl.when(at_end)
                def _():
                    finish(j)

        return carry

    lax.fori_loop(0, relayed + nb - 1, step, 0)

    def drain(n, carry):
        lev = n // nb
        j = n % nb
        up_last = (z == levels - 2) & (lev == 0)
        down_last = (z == 1) & (lev == levels - 1)

        @pl.when((lev <= z) & (z < levels - 1) & jnp.logical_not(up_last))
        def _():
            up_copy(lev, j).wait_send()

        @pl.when((lev >= z) & (z > 0) & jnp.logical_not(down_last))
        def _():
            down_copy(lev, j).wait_send()

        @pl.when(up_last | down_last)
        def _():
            straight_copy(j).wait_send()
            diagonal_copy(j).wait_send()

        @pl.when(jnp.logical_not(at_end & (lev == levels - 1 - z)))
        def _():
            across_copy(lev, j).wait_send()

        return carry

    def drain_all():
        for j in range(1, nb):
            beta_copy(j).wait_send()
        lax.fori_loop(0, levels * nb, drain, 0)

    @pl.when(at_end)
    def _():
        drain_all()

    last_b_ref[...] = bdense[nb - 1]
    step(relayed + nb - 1, 0, True)

    @pl.when(jnp.logical_not(at_end))
    def _():
        drain_all()


def close_kernel(tile, part, last, last_b, out_hbm, staged, sems):
    copies = []
    for n in range(part.shape[1] // tile):
        here = slice(n * tile, (n + 1) * tile)
        staged[n] = part[:, here] + sum(lax.dot_general(last[k], last_b[k, here, :], (((1,), (1,)), ((), ())), preferred_element_type=jnp.float32) for k in range(last.shape[0]))
        copies.append(pltpu.make_async_copy(staged.at[n], out_hbm.at[:, here], sems.at[n]))
        copies[-1].start()
    for copy in copies:
        copy.wait()


def scratch_of(geometry, dtype):
    na, nb, ops, slots, blk, row_blocks, col_blocks = geometry
    levels = na // PAIR
    rows, cols, wide = row_blocks * blk, col_blocks * blk, FROM_B * blk
    return [
        ((col_blocks, rows, blk), dtype),
        ((ops, slots, rows, blk), dtype),
        ((ops, slots, cols, blk), dtype),
        ((nb - 1, rows, wide), dtype),
        ((levels, nb, rows, wide), dtype),
        ((levels, nb, blk, wide), dtype),
        ((levels, nb, blk, wide), dtype),
        ((PAIR, nb, blk, wide), dtype),
        ((nb, blk, wide), dtype),
        ((levels, ops * rows, 2 * PAIR * blk), dtype),
        ((nb, ops, cols, wide), dtype),
        ((nb, ops * rows, wide), jnp.float32),
    ]


def scratch_bytes(geometry):
    total = 0
    for shape, dtype in scratch_of(geometry, jnp.bfloat16):
        size = jnp.dtype(dtype).itemsize
        for extent in shape:
            size *= extent
        total += size
    return total


def fused(geometry, coeffs, a_blocks, a_list, a_count, b_blocks, b_list, b_count):
    na, nb, ops, slots, blk, row_blocks, col_blocks = geometry
    levels = na // PAIR
    a_lists = jnp.transpose(a_list, (2, 0, 1))
    b_lists = jnp.transpose(b_list, (2, 0, 1))
    rows, cols = row_blocks * blk, col_blocks * blk
    dma = pltpu.SemaphoreType.DMA
    vmem = pl.BlockSpec(memory_space=pltpu.VMEM)
    held = pl.pallas_call(
        functools.partial(sigma_kernel, geometry),
        out_shape=(pltpu.VMEM((rows, cols), jnp.float32), pltpu.VMEM((ops, rows, FROM_B * blk), coeffs.dtype), pltpu.VMEM((ops, cols, FROM_B * blk), coeffs.dtype)),
        in_specs=[pl.BlockSpec(memory_space=pltpu.HBM)] * 7,
        out_specs=(vmem, vmem, vmem),
        scratch_shapes=[
            pltpu.SMEM(a_lists.shape, jnp.int32), pltpu.SMEM(a_count.shape, jnp.int32), pltpu.SMEM(b_lists.shape, jnp.int32),
            pltpu.SMEM(b_count.shape, jnp.int32), pltpu.VMEM(a_lists.shape, jnp.int32), pltpu.VMEM(b_lists.shape, jnp.int32),
        ] + [pltpu.VMEM(shape, dtype) for shape, dtype in scratch_of(geometry, coeffs.dtype)] + [
            pltpu.SMEM((2 * levels + nb + PAIR,), jnp.int32),
            dma((6,)), dma((2 + col_blocks,)), dma((nb - 1,)), dma((nb - 1,)), dma((levels, nb)), dma((levels, nb)), dma((levels, nb)),
            dma((levels, nb)), dma((levels, nb)), dma((PAIR, nb)), dma((nb,)),
        ],
        compiler_params=pltpu.CompilerParams(collective_id=0, has_side_effects=True, vmem_limit_bytes=KERNEL_LIMIT),
        name="sigma_build",
    )(*[pltpu.with_memory_space_constraint(v, pltpu.HBM) for v in (a_lists, a_count, b_lists, b_count, coeffs, jnp.transpose(a_blocks, (0, 2, 1, 3)), jnp.transpose(b_blocks, (0, 2, 1, 3)))])
    tile = cols // 2
    return pl.pallas_call(
        functools.partial(close_kernel, tile),
        out_shape=jax.ShapeDtypeStruct((rows, cols), jnp.float32),
        in_specs=[vmem, vmem, vmem],
        out_specs=pl.BlockSpec(memory_space=pltpu.HBM),
        scratch_shapes=[pltpu.VMEM((cols // tile, rows, tile), jnp.float32), dma((cols // tile,))],
        compiler_params=pltpu.CompilerParams(vmem_limit_bytes=8 * 1024 * 1024),
        name="close_sigma",
    )(*held)


def arrange(entries, owners, per_owner, capacity):
    operators, total, list_slots = entries.shape
    flattened = entries.reshape(operators, owners, per_owner * list_slots)
    matches = flattened[..., None] == jnp.arange(total, dtype=jnp.int32)
    present = jnp.any(matches, axis=(0, 2)).reshape(owners, owners, per_owner).astype(jnp.int32)
    ranking = jnp.cumsum(present, axis=2)
    position = jnp.arange(capacity, dtype=jnp.int32) + 1
    chosen_bits = (present[..., None] == 1) & (ranking[..., None] == position)
    local_ids = jnp.arange(per_owner, dtype=jnp.int32)[None, None, :, None]
    wanted = jnp.sum(local_ids * chosen_bits.astype(jnp.int32), axis=2)
    return (wanted, ranking)


def locate(entries, ranking_here, per_owner, capacity):
    owner = entries // per_owner
    local_id = entries % per_owner
    return owner * capacity + ranking_here[owner, local_id] - 1


def pick_columns(pool_piece, index_piece):
    return pool_piece[:, index_piece]


def plain(coeffs, a_blocks, a_list, a_count, b_blocks, b_list, b_count):
    operators, local_rows, list_slots, block_size = a_blocks.shape
    local_cols = coeffs.shape[1]
    row_blocks = local_rows // block_size
    col_blocks = local_cols // block_size
    row_capacity = FROM_A
    col_capacity = FROM_B
    alpha_size = lax.axis_size("alpha")
    beta_size = lax.axis_size("beta")
    alpha_here = lax.axis_index("alpha")
    beta_here = lax.axis_index("beta")
    slot_ids = jnp.arange(list_slots, dtype=jnp.int32)
    alpha_mine = lax.dynamic_slice_in_dim(a_list, alpha_here * row_blocks, row_blocks, 1)
    alpha_counts = lax.dynamic_slice_in_dim(a_count, alpha_here * row_blocks, row_blocks, 1)
    alpha_valid = slot_ids < alpha_counts[..., None]
    alpha_kept = jnp.where(
        alpha_valid[:, :, None, :, None],
        a_blocks.reshape(operators, row_blocks, block_size, list_slots, block_size),
        jnp.zeros((), jnp.bfloat16),
    )
    wanted, ranking = arrange(a_list, alpha_size, row_blocks, row_capacity)
    outgoing = coeffs.reshape(row_blocks, block_size, local_cols)[wanted[:, alpha_here, :]]
    incoming = lax.all_to_all(outgoing, "alpha", split_axis=0, concat_axis=0, tiled=True)
    source_index = locate(alpha_mine, ranking[alpha_here], row_blocks, row_capacity)
    chosen = incoming.reshape(alpha_size * row_capacity, block_size, local_cols)[source_index]
    inter = jnp.einsum("kbrsi,kbsic->kbrc", alpha_kept, chosen, preferred_element_type=jnp.float32)
    inter = inter.astype(jnp.bfloat16).reshape(operators, local_rows, col_blocks, block_size)
    wanted_cols, ranking_cols = arrange(b_list, beta_size, col_blocks, col_capacity)
    outgoing_cols = inter[:, :, wanted_cols[:, beta_here, :], :]
    incoming_cols = lax.all_to_all(outgoing_cols, "beta", split_axis=2, concat_axis=2, tiled=True)
    beta_mine = lax.dynamic_slice_in_dim(b_list, beta_here * col_blocks, col_blocks, 1)
    beta_counts = lax.dynamic_slice_in_dim(b_count, beta_here * col_blocks, col_blocks, 1)
    beta_valid = slot_ids < beta_counts[..., None]
    beta_kept = jnp.where(
        beta_valid[:, :, None, :, None],
        b_blocks.reshape(operators, col_blocks, block_size, list_slots, block_size),
        jnp.zeros((), jnp.bfloat16),
    )
    source_cols = locate(beta_mine, ranking_cols[beta_here], col_blocks, col_capacity)
    pooled = incoming_cols.reshape(operators, local_rows, beta_size * col_capacity, block_size)
    picked = jax.vmap(pick_columns)(pooled, source_cols)
    sigma = jnp.einsum("kabsj,kbrsj->abr", picked, beta_kept, preferred_element_type=jnp.float32)
    return sigma.reshape(local_rows, local_cols)


def on_device(coeffs, a_blocks, a_list, a_count, b_blocks, b_list, b_count):
    operators, local_rows, list_slots, block_size = a_blocks.shape
    na, nb = lax.axis_size("alpha"), lax.axis_size("beta")
    geometry = (na, nb, operators, list_slots, block_size, local_rows // block_size, coeffs.shape[1] // block_size)
    fits = scratch_bytes(geometry) < KERNEL_LIMIT * 3 // 4
    shaped = FROM_A == 1 and FROM_B == 2 and na % PAIR == 0 and na > 3 * PAIR and nb & (nb - 1) == 0 and nb > 1
    build = functools.partial(fused, geometry) if fits and shaped else plain
    return build(coeffs, a_blocks, a_list, a_count, b_blocks, b_list, b_count)


def solution(mesh):
    in_specs = (
        P("alpha", "beta"),
        P(None, "alpha", None, None),
        P(),
        P(),
        P(None, "beta", None, None),
        P(),
        P(),
    )
    out_specs = P("alpha", "beta")
    return jax.shard_map(
        on_device, mesh=mesh, in_specs=in_specs, out_specs=out_specs, check_vma=False
    )
```

```python
import functools

import jax
import jax.numpy as jnp
from jax import lax
from jax.experimental import pallas as pl
from jax.experimental.pallas import tpu as pltpu
from jax.sharding import PartitionSpec as P

FROM_A = 1
FROM_B = 2
PAIR = 2
LAG = 2
CORES = 2
VMEM_LIMIT = 60 * 1024 * 1024
KERNEL_LIMIT = 40 * 1024 * 1024
MESH = pl.DeviceIdType.MESH


def sigma_kernel(geometry, a_lists_hbm, a_counts_hbm, b_lists_hbm, b_counts_hbm, c_hbm, a_hbm, b_hbm, out_ref, last_ref, last_b_ref, a_lists, a_counts, b_lists, b_counts, a_vec, b_vec, cbuf, abuf, bbuf, picks, column, across, chosen,
                 straight, tail, adense, bdense, acc, small, table_sem, local_sem, beta_send, beta_recv, column_recv, up_send, down_send, across_send, across_recv,
                 straight_send, tail_recv, aside_send):
    na, nb, ops, slots, blk, row_blocks, col_blocks = geometry
    levels = na // PAIR
    rows = row_blocks * blk
    wide = FROM_B * blk
    a = lax.axis_index("alpha")
    c = lax.axis_index("beta")
    z = a // PAIR
    x = a % PAIR
    partner = a + 1 - 2 * x

    barrier = pltpu.get_barrier_semaphore()
    for j in range(1, nb):
        pl.semaphore_signal(barrier, inc=1, device_id={"beta": c ^ j}, device_id_type=MESH)
    pl.semaphore_signal(barrier, inc=1, device_id={"alpha": partner}, device_id_type=MESH)

    @pl.when(z < levels - 1)
    def _():
        pl.semaphore_signal(barrier, inc=1, device_id={"alpha": a + PAIR}, device_id_type=MESH)

    @pl.when(z > 0)
    def _():
        pl.semaphore_signal(barrier, inc=1, device_id={"alpha": a - PAIR}, device_id_type=MESH)

    tables = [(b_lists_hbm, b_vec), (a_lists_hbm, a_vec), (a_lists_hbm, a_lists), (a_counts_hbm, a_counts), (b_lists_hbm, b_lists), (b_counts_hbm, b_counts)]
    copies_t = [pltpu.make_async_copy(source, target, table_sem.at[n]) for n, (source, target) in enumerate(tables)]
    copies_c = [pltpu.make_async_copy(c_hbm.at[:, b * blk:(b + 1) * blk], cbuf.at[b], local_sem.at[2 + b]) for b in range(col_blocks)]
    copy_a = pltpu.make_async_copy(a_hbm, abuf, local_sem.at[0])
    copy_b = pltpu.make_async_copy(b_hbm, bbuf, local_sem.at[1])
    for copy in copies_t + copies_c:
        copy.start()
    copy_a.start()
    copy_b.start()
    copies_t[0].wait()

    lists = b_vec[...]
    lane = lax.broadcasted_iota(jnp.int32, (1, nb * col_blocks), 1)

    def extremes(receiver, owner):
        local = lists - owner * col_blocks
        hit = (local >= 0) & (local < col_blocks)
        rows_here = (lane >= receiver * col_blocks) & (lane < (receiver + 1) * col_blocks)
        low = jnp.min(jnp.min(jnp.where(hit, local, col_blocks), axis=0), axis=0, keepdims=True)
        high = jnp.max(jnp.max(jnp.where(hit, local, 0), axis=0), axis=0, keepdims=True)
        low = jnp.min(jnp.where(rows_here, low, col_blocks))
        high = jnp.max(jnp.where(rows_here, high, 0))
        return jnp.where(low < col_blocks, low, 0), high

    spans = [extremes(c ^ j, c) for j in range(nb)]
    for copy in copies_c:
        copy.wait()
    for j in range(nb):
        for u, block in enumerate(spans[j]):
            piece = cbuf[block]
            if j == 0:
                column[z, 0, :, u * blk:(u + 1) * blk] = piece
            else:
                picks[j - 1, :, u * blk:(u + 1) * blk] = piece

    neighbours = nb + jnp.where(z < levels - 1, 1, 0) + jnp.where(z > 0, 1, 0)
    pl.semaphore_wait(barrier, neighbours)

    def beta_copy(j):
        return pltpu.make_async_remote_copy(
            src_ref=picks.at[j - 1], dst_ref=column.at[z, j], send_sem=beta_send.at[j - 1], recv_sem=beta_recv.at[j - 1],
            device_id={"beta": c ^ j}, device_id_type=MESH)

    def up_copy(lev, j):
        return pltpu.make_async_remote_copy(
            src_ref=column.at[lev, j], dst_ref=column.at[lev, j], send_sem=up_send.at[lev, j], recv_sem=column_recv.at[lev, j],
            device_id={"alpha": a + PAIR}, device_id_type=MESH)

    def down_copy(lev, j):
        return pltpu.make_async_remote_copy(
            src_ref=column.at[lev, j], dst_ref=column.at[lev, j], send_sem=down_send.at[lev, j], recv_sem=column_recv.at[lev, j],
            device_id={"alpha": a - PAIR}, device_id_type=MESH)

    def across_copy(lev, j):
        return pltpu.make_async_remote_copy(
            src_ref=chosen.at[lev, j], dst_ref=across.at[lev, j], send_sem=across_send.at[lev, j], recv_sem=across_recv.at[lev, j],
            device_id={"alpha": partner}, device_id_type=MESH)

    def one_hot(value, place):
        gap = value - place
        return (1 - jnp.minimum(jnp.maximum(gap, -gap), 1)).astype(jnp.float32)

    def at_most(slot, count):
        return jnp.minimum(jnp.maximum(count - slot, 0), 1)

    def selected(lev, j, pick):
        total = jnp.zeros((blk, wide), jnp.float32)
        for i in range(row_blocks):
            total += column[lev, j, i * blk:(i + 1) * blk, :].astype(jnp.float32) * one_hot(pick, i)
        return total.astype(jnp.bfloat16)

    def offer(lev, j):
        chosen[lev, j] = selected(lev, j, small[levels + lev])
        across_copy(lev, j).start()

    def own_relays(j):
        @pl.when(z < levels - 1)
        def _():
            up_copy(z, j).start()

        @pl.when(z > 0)
        def _():
            down_copy(z, j).start()

    own_relays(0)
    for j in range(1, nb):
        beta_copy(j).start()
    for copy in copies_t[1:]:
        copy.wait()
    rows_list = a_vec[...]
    row_lane = lax.broadcasted_iota(jnp.int32, (1, na * row_blocks), 1)

    def row_pick(receiver, owner):
        local = rows_list - owner * row_blocks
        hit = (local >= 0) & (local < row_blocks)
        rows_here = (row_lane >= receiver * row_blocks) & (row_lane < (receiver + 1) * row_blocks)
        high = jnp.max(jnp.max(jnp.where(hit, local, 0), axis=0), axis=0, keepdims=True)
        return jnp.max(jnp.where(rows_here, high, 0))

    for lev in range(levels):
        small[lev] = row_pick(a, lev * PAIR + x)
        small[levels + lev] = row_pick(partner, lev * PAIR + x)
    for owner in range(nb):
        small[2 * levels + owner] = extremes(c, owner)[0]
    far = jnp.where(z == levels - 2, levels - 1, 0)
    opposite = levels - 1 - far
    for side in range(PAIR):
        small[2 * levels + nb + side] = row_pick(far * PAIR + (x + side) % PAIR, opposite * PAIR + x)
    out_ref[...] = jnp.zeros_like(out_ref)

    offer(z, 0)

    def dense(load, codes, groups, per_group, put):
        def group(g, carry):
            totals = [jnp.zeros((blk, blk), jnp.float32) for _ in range(per_group)]
            for s in range(slots):
                value = load(s)
                for p in range(per_group):
                    totals[p] += value * jnp.where(codes[s] == g * per_group + p, 1.0, 0.0)
            for p in range(per_group):
                put(g, p, totals[p])
            return carry

        lax.fori_loop(0, groups, group, 0)

    def build_a(piece):
        k = piece // row_blocks
        i = piece % row_blocks
        codes = []
        for s in range(slots):
            entry = a_lists[s, k, a * row_blocks + i]
            owner = lax.div(entry, row_blocks)
            upper = owner - 2 * lax.div(owner, 2)
            place = owner - upper + jnp.maximum(upper - x, x - upper)
            codes.append((place + 1) * at_most(s, a_counts[k, a * row_blocks + i]) - 1)

        def load(s):
            return abuf[k, s, pl.ds(i * blk, blk), :].astype(jnp.float32)

        def put(g, p, total):
            at = pl.ds(k * rows + i * blk, blk)
            high = total.astype(jnp.bfloat16)
            adense[g, at, p * blk:(p + 1) * blk] = high
            adense[g, at, (PAIR + p) * blk:(PAIR + p + 1) * blk] = (total - high.astype(jnp.float32)).astype(jnp.bfloat16)

        dense(load, codes, levels, PAIR, put)

    def build_b(piece):
        k = piece // col_blocks
        r = piece % col_blocks
        codes = []
        for s in range(slots):
            entry = b_lists[s, k, c * col_blocks + r]
            owner = lax.div(entry, col_blocks)
            gap = entry - owner * col_blocks - small[2 * levels + owner]
            place = (owner ^ c) * FROM_B + jnp.minimum(jnp.maximum(gap, -gap), 1)
            codes.append((place + 1) * at_most(s, b_counts[k, c * col_blocks + r]) - 1)

        def load(s):
            return bbuf[k, s, pl.ds(r * blk, blk), :].astype(jnp.float32)

        def put(g, p, total):
            bdense[g, k, pl.ds(r * blk, blk), p * blk:(p + 1) * blk] = total.astype(jnp.bfloat16)

        dense(load, codes, nb, FROM_B, put)

    a_pieces = ops * row_blocks
    pieces = ops * col_blocks

    def build_some(first, count):
        def one(n, carry):
            @pl.when(n < pieces)
            def _():
                build_b(n)
            return carry

        lax.fori_loop(first, first + count, one, 0)

    def beta_wait(j):
        pltpu.make_async_remote_copy(
            src_ref=picks.at[j - 1], dst_ref=column.at[z, j], send_sem=beta_send.at[j - 1], recv_sem=beta_recv.at[j - 1],
            device_id={"beta": c ^ j}, device_id_type=MESH).wait_recv()

    copy_a.wait()

    def one_a(n, carry):
        build_a(n)
        return carry

    lax.fori_loop(0, a_pieces // 2, one_a, 0)
    built = 0
    for j in range(1, nb):
        beta_wait(j)
        own_relays(j)
        offer(z, j)
        if j == 1:
            lax.fori_loop(a_pieces // 2, a_pieces, one_a, 0)
            copy_b.wait()
        if j < nb - 1:
            build_some(built, 2 * j)
            built += 2 * j

    def product(lev, j, mine):
        across_copy(lev, j).wait_recv()
        other = across[lev, j]
        value = jnp.concatenate([mine, other, mine, other], axis=0)
        return jnp.dot(adense[lev], value, preferred_element_type=jnp.float32)

    def combine(lev, j):
        acc[j] += product(lev, j, selected(lev, j, small[lev]))

    tile = min(2, col_blocks) * blk

    def finish(j):
        inters = [acc[j, k * rows:(k + 1) * rows, :].astype(jnp.bfloat16) for k in range(ops)]

        def columns(n, carry):
            here = pl.ds(pl.multiple_of(n * tile, tile), tile)
            total = out_ref[:, here]
            for k in range(ops):
                total += lax.dot_general(inters[k], bdense[j, k, here, :], (((1,), (1,)), ((), ())),
                                         preferred_element_type=jnp.float32)
            out_ref[:, here] = total
            return carry

        lax.fori_loop(0, col_blocks * blk // tile, columns, 0)

    def straight_copy(j):
        return pltpu.make_async_remote_copy(
            src_ref=straight.at[0, j], dst_ref=tail.at[j], send_sem=straight_send.at[0, j], recv_sem=tail_recv.at[j],
            device_id={"alpha": far * PAIR + x}, device_id_type=MESH)

    def diagonal_copy(j):
        return pltpu.make_async_remote_copy(
            src_ref=straight.at[1, j], dst_ref=across.at[opposite, j], send_sem=straight_send.at[1, j], recv_sem=across_recv.at[opposite, j],
            device_id={"alpha": far * PAIR + 1 - x}, device_id_type=MESH)

    lightened = (z == 1) & (c == 0)
    forwards = (z == 1) & (c == CORES)
    beside = jnp.where(c < CORES, c + CORES, jnp.where(c < 2 * CORES, c - CORES, c))

    def aside_copy():
        return pltpu.make_async_remote_copy(
            src_ref=straight.at[1 - x, 0], dst_ref=tail.at[0], send_sem=aside_send.at[0], recv_sem=tail_recv.at[0],
            device_id={"beta": beside}, device_id_type=MESH)

    def forward_crossing():
        return pltpu.make_async_remote_copy(
            src_ref=tail.at[0], dst_ref=across.at[levels - 1, 0], send_sem=aside_send.at[1], recv_sem=across_recv.at[levels - 1, 0],
            device_id={"alpha": a - 1, "beta": beside}, device_id_type=MESH)

    def forward_direct():
        return pltpu.make_async_remote_copy(
            src_ref=tail.at[0], dst_ref=tail.at[0], send_sem=aside_send.at[1], recv_sem=tail_recv.at[0],
            device_id={"alpha": a - PAIR, "beta": beside}, device_id_type=MESH)

    def arrive(lev, j, below):
        pltpu.make_async_remote_copy(
            src_ref=column.at[lev, j], dst_ref=column.at[lev, j], send_sem=up_send.at[lev, j], recv_sem=column_recv.at[lev, j],
            device_id={"alpha": partner}, device_id_type=MESH).wait_recv()
        last = (z == levels - 2) & (lev == 0) if below else (z == 1) & (lev == levels - 1)

        @pl.when(last)
        def _():
            straight[1, j] = selected(lev, j, small[2 * levels + nb + 1])
            straight[0, j] = selected(lev, j, small[2 * levels + nb])
            if below:
                diagonal_copy(j).start()
                straight_copy(j).start()
            else:
                ahead = (c < CORES) & (x == 0)
                behind = (c < CORES) & (x == 1)
                previous = jnp.maximum(j - 1, 0)
                kept = (j > 1) | ((j == 1) & jnp.logical_not(lightened))

                @pl.when(lightened & (j == 0))
                def _():
                    aside_copy().start()

                @pl.when(ahead)
                def _():
                    straight_copy(j).start()

                    @pl.when(kept)
                    def _():
                        diagonal_copy(previous).start()

                    @pl.when(j == nb - 1)
                    def _():
                        diagonal_copy(j).start()

                @pl.when(jnp.logical_not(ahead))
                def _():
                    diagonal_copy(j).start()

                @pl.when(behind & kept)
                def _():
                    straight_copy(previous).start()

                @pl.when(jnp.logical_not(ahead) & (jnp.logical_not(behind) | (j == nb - 1)))
                def _():
                    straight_copy(j).start()

        if below:
            @pl.when((z < levels - 1) & jnp.logical_not(last))
            def _():
                up_copy(lev, j).start()
        else:
            @pl.when((z > 0) & jnp.logical_not(last))
            def _():
                down_copy(lev, j).start()

        offer(lev, j)

    relayed = (levels - 2) * nb
    at_end = (z == 0) | (z == levels - 1)

    def step(i, carry, final=False):
        j = i % nb
        distance = i // nb + 1

        @pl.when((i == relayed - nb + 1) & forwards)
        def _():
            aside_copy().wait_recv()

            @pl.when(x == 0)
            def _():
                forward_crossing().start()

            @pl.when(x == 1)
            def _():
                forward_direct().start()

        @pl.when((i < relayed) & (z - distance >= 0))
        def _():
            arrive(z - distance, j, True)

        @pl.when((i < relayed) & (z + distance < levels))
        def _():
            arrive(z + distance, j, False)

        own = jnp.maximum(i - 1, 0) % nb

        @pl.when((i > 0) & (i <= nb))
        def _():
            acc[own] = product(z, own, selected(z, own, small[z]))

        before = jnp.maximum(i - LAG, 0)
        j_before = before % nb
        distance_before = before // nb + 1

        @pl.when((i >= LAG) & (i < relayed + LAG) & (z - distance_before >= 0))
        def _():
            combine(z - distance_before, j_before)

        @pl.when((i >= LAG) & (i < relayed + LAG) & (z + distance_before < levels))
        def _():
            combine(z + distance_before, j_before)

        build_some(built + 2 * i, 2)


        early = i - (relayed + LAG - nb)

        @pl.when((early >= 0) & (early < nb - 1) & jnp.logical_not(at_end))
        def _():
            finish(early)

        @pl.when(i >= relayed)
        def _():
            @pl.when(at_end)
            def _():
                pltpu.make_async_remote_copy(
                    src_ref=straight.at[0, j], dst_ref=tail.at[j], send_sem=straight_send.at[0, j], recv_sem=tail_recv.at[j],
                    device_id={"alpha": partner}, device_id_type=MESH).wait_recv()
                lev = levels - 1 - z
                total = acc[j] + product(lev, j, tail[j])
                if final:
                    for k in range(ops):
                        last_ref[k] = total[k * rows:(k + 1) * rows].astype(jnp.bfloat16)
                else:
                    acc[j] = total

            if final:
                @pl.when(jnp.logical_not(at_end))
                def _():
                    for k in range(ops):
                        last_ref[k] = acc[j, k * rows:(k + 1) * rows, :].astype(jnp.bfloat16)
            else:
                @pl.when(at_end)
                def _():
                    finish(j)

        return carry

    lax.fori_loop(0, relayed + nb - 1, step, 0)

    def drain(n, carry):
        lev = n // nb
        j = n % nb
        up_last = (z == levels - 2) & (lev == 0)
        down_last = (z == 1) & (lev == levels - 1)

        @pl.when((lev <= z) & (z < levels - 1) & jnp.logical_not(up_last))
        def _():
            up_copy(lev, j).wait_send()

        @pl.when((lev >= z) & (z > 0) & jnp.logical_not(down_last))
        def _():
            down_copy(lev, j).wait_send()

        @pl.when(up_last | down_last)
        def _():
            turned = lightened & (j == 0)

            @pl.when(turned)
            def _():
                aside_copy().wait_send()

            @pl.when(jnp.logical_not(turned & (x == 1)))
            def _():
                straight_copy(j).wait_send()

            @pl.when(jnp.logical_not(turned & (x == 0)))
            def _():
                diagonal_copy(j).wait_send()

            @pl.when(forwards & (j == 0))
            def _():
                forward_direct().wait_send()

        @pl.when(jnp.logical_not(at_end & (lev == levels - 1 - z)))
        def _():
            across_copy(lev, j).wait_send()

        return carry

    def drain_all():
        for j in range(1, nb):
            beta_copy(j).wait_send()
        lax.fori_loop(0, levels * nb, drain, 0)

    @pl.when(at_end)
    def _():
        drain_all()

    last_b_ref[...] = bdense[nb - 1]
    step(relayed + nb - 1, 0, True)

    @pl.when(jnp.logical_not(at_end))
    def _():
        drain_all()


def close_kernel(tile, part, last, last_b, out_hbm, staged, sems):
    copies = []
    for n in range(part.shape[1] // tile):
        here = slice(n * tile, (n + 1) * tile)
        staged[n] = part[:, here] + sum(lax.dot_general(last[k], last_b[k, here, :], (((1,), (1,)), ((), ())), preferred_element_type=jnp.float32) for k in range(last.shape[0]))
        copies.append(pltpu.make_async_copy(staged.at[n], out_hbm.at[:, here], sems.at[n]))
        copies[-1].start()
    for copy in copies:
        copy.wait()


def scratch_of(geometry, dtype):
    na, nb, ops, slots, blk, row_blocks, col_blocks = geometry
    levels = na // PAIR
    rows, cols, wide = row_blocks * blk, col_blocks * blk, FROM_B * blk
    return [
        ((col_blocks, rows, blk), dtype),
        ((ops, slots, rows, blk), dtype),
        ((ops, slots, cols, blk), dtype),
        ((nb - 1, rows, wide), dtype),
        ((levels, nb, rows, wide), dtype),
        ((levels, nb, blk, wide), dtype),
        ((levels, nb, blk, wide), dtype),
        ((PAIR, nb, blk, wide), dtype),
        ((nb, blk, wide), dtype),
        ((levels, ops * rows, 2 * PAIR * blk), dtype),
        ((nb, ops, cols, wide), dtype),
        ((nb, ops * rows, wide), jnp.float32),
    ]


def scratch_bytes(geometry):
    total = 0
    for shape, dtype in scratch_of(geometry, jnp.bfloat16):
        size = jnp.dtype(dtype).itemsize
        for extent in shape:
            size *= extent
        total += size
    return total


def fused(geometry, coeffs, a_blocks, a_list, a_count, b_blocks, b_list, b_count):
    na, nb, ops, slots, blk, row_blocks, col_blocks = geometry
    levels = na // PAIR
    a_lists = jnp.transpose(a_list, (2, 0, 1))
    b_lists = jnp.transpose(b_list, (2, 0, 1))
    rows, cols = row_blocks * blk, col_blocks * blk
    dma = pltpu.SemaphoreType.DMA
    vmem = pl.BlockSpec(memory_space=pltpu.VMEM)
    held = pl.pallas_call(
        functools.partial(sigma_kernel, geometry),
        out_shape=(pltpu.VMEM((rows, cols), jnp.float32), pltpu.VMEM((ops, rows, FROM_B * blk), coeffs.dtype), pltpu.VMEM((ops, cols, FROM_B * blk), coeffs.dtype)),
        in_specs=[pl.BlockSpec(memory_space=pltpu.HBM)] * 7,
        out_specs=(vmem, vmem, vmem),
        scratch_shapes=[
            pltpu.SMEM(a_lists.shape, jnp.int32), pltpu.SMEM(a_count.shape, jnp.int32), pltpu.SMEM(b_lists.shape, jnp.int32),
            pltpu.SMEM(b_count.shape, jnp.int32), pltpu.VMEM(a_lists.shape, jnp.int32), pltpu.VMEM(b_lists.shape, jnp.int32),
        ] + [pltpu.VMEM(shape, dtype) for shape, dtype in scratch_of(geometry, coeffs.dtype)] + [
            pltpu.SMEM((2 * levels + nb + PAIR,), jnp.int32),
            dma((6,)), dma((2 + col_blocks,)), dma((nb - 1,)), dma((nb - 1,)), dma((levels, nb)), dma((levels, nb)), dma((levels, nb)),
            dma((levels, nb)), dma((levels, nb)), dma((PAIR, nb)), dma((nb,)), dma((2,)),
        ],
        compiler_params=pltpu.CompilerParams(collective_id=0, has_side_effects=True, vmem_limit_bytes=KERNEL_LIMIT),
        name="sigma_build",
    )(*[pltpu.with_memory_space_constraint(v, pltpu.HBM) for v in (a_lists, a_count, b_lists, b_count, coeffs, jnp.transpose(a_blocks, (0, 2, 1, 3)), jnp.transpose(b_blocks, (0, 2, 1, 3)))])
    tile = cols // 2
    return pl.pallas_call(
        functools.partial(close_kernel, tile),
        out_shape=jax.ShapeDtypeStruct((rows, cols), jnp.float32),
        in_specs=[vmem, vmem, vmem],
        out_specs=pl.BlockSpec(memory_space=pltpu.HBM),
        scratch_shapes=[pltpu.VMEM((cols // tile, rows, tile), jnp.float32), dma((cols // tile,))],
        compiler_params=pltpu.CompilerParams(vmem_limit_bytes=8 * 1024 * 1024),
        name="close_sigma",
    )(*held)


def arrange(entries, owners, per_owner, capacity):
    operators, total, list_slots = entries.shape
    flattened = entries.reshape(operators, owners, per_owner * list_slots)
    matches = flattened[..., None] == jnp.arange(total, dtype=jnp.int32)
    present = jnp.any(matches, axis=(0, 2)).reshape(owners, owners, per_owner).astype(jnp.int32)
    ranking = jnp.cumsum(present, axis=2)
    position = jnp.arange(capacity, dtype=jnp.int32) + 1
    chosen_bits = (present[..., None] == 1) & (ranking[..., None] == position)
    local_ids = jnp.arange(per_owner, dtype=jnp.int32)[None, None, :, None]
    wanted = jnp.sum(local_ids * chosen_bits.astype(jnp.int32), axis=2)
    return (wanted, ranking)


def locate(entries, ranking_here, per_owner, capacity):
    owner = entries // per_owner
    local_id = entries % per_owner
    return owner * capacity + ranking_here[owner, local_id] - 1


def pick_columns(pool_piece, index_piece):
    return pool_piece[:, index_piece]


def plain(coeffs, a_blocks, a_list, a_count, b_blocks, b_list, b_count):
    operators, local_rows, list_slots, block_size = a_blocks.shape
    local_cols = coeffs.shape[1]
    row_blocks = local_rows // block_size
    col_blocks = local_cols // block_size
    row_capacity = FROM_A
    col_capacity = FROM_B
    alpha_size = lax.axis_size("alpha")
    beta_size = lax.axis_size("beta")
    alpha_here = lax.axis_index("alpha")
    beta_here = lax.axis_index("beta")
    slot_ids = jnp.arange(list_slots, dtype=jnp.int32)
    alpha_mine = lax.dynamic_slice_in_dim(a_list, alpha_here * row_blocks, row_blocks, 1)
    alpha_counts = lax.dynamic_slice_in_dim(a_count, alpha_here * row_blocks, row_blocks, 1)
    alpha_valid = slot_ids < alpha_counts[..., None]
    alpha_kept = jnp.where(
        alpha_valid[:, :, None, :, None],
        a_blocks.reshape(operators, row_blocks, block_size, list_slots, block_size),
        jnp.zeros((), jnp.bfloat16),
    )
    wanted, ranking = arrange(a_list, alpha_size, row_blocks, row_capacity)
    outgoing = coeffs.reshape(row_blocks, block_size, local_cols)[wanted[:, alpha_here, :]]
    incoming = lax.all_to_all(outgoing, "alpha", split_axis=0, concat_axis=0, tiled=True)
    source_index = locate(alpha_mine, ranking[alpha_here], row_blocks, row_capacity)
    chosen = incoming.reshape(alpha_size * row_capacity, block_size, local_cols)[source_index]
    inter = jnp.einsum("kbrsi,kbsic->kbrc", alpha_kept, chosen, preferred_element_type=jnp.float32)
    inter = inter.astype(jnp.bfloat16).reshape(operators, local_rows, col_blocks, block_size)
    wanted_cols, ranking_cols = arrange(b_list, beta_size, col_blocks, col_capacity)
    outgoing_cols = inter[:, :, wanted_cols[:, beta_here, :], :]
    incoming_cols = lax.all_to_all(outgoing_cols, "beta", split_axis=2, concat_axis=2, tiled=True)
    beta_mine = lax.dynamic_slice_in_dim(b_list, beta_here * col_blocks, col_blocks, 1)
    beta_counts = lax.dynamic_slice_in_dim(b_count, beta_here * col_blocks, col_blocks, 1)
    beta_valid = slot_ids < beta_counts[..., None]
    beta_kept = jnp.where(
        beta_valid[:, :, None, :, None],
        b_blocks.reshape(operators, col_blocks, block_size, list_slots, block_size),
        jnp.zeros((), jnp.bfloat16),
    )
    source_cols = locate(beta_mine, ranking_cols[beta_here], col_blocks, col_capacity)
    pooled = incoming_cols.reshape(operators, local_rows, beta_size * col_capacity, block_size)
    picked = jax.vmap(pick_columns)(pooled, source_cols)
    sigma = jnp.einsum("kabsj,kbrsj->abr", picked, beta_kept, preferred_element_type=jnp.float32)
    return sigma.reshape(local_rows, local_cols)


def on_device(coeffs, a_blocks, a_list, a_count, b_blocks, b_list, b_count):
    operators, local_rows, list_slots, block_size = a_blocks.shape
    na, nb = lax.axis_size("alpha"), lax.axis_size("beta")
    geometry = (na, nb, operators, list_slots, block_size, local_rows // block_size, coeffs.shape[1] // block_size)
    fits = scratch_bytes(geometry) < KERNEL_LIMIT * 3 // 4
    shaped = FROM_A == 1 and FROM_B == 2 and na % PAIR == 0 and na > 3 * PAIR and nb & (nb - 1) == 0 and nb >= 2 * CORES
    build = functools.partial(fused, geometry) if fits and shaped else plain
    return build(coeffs, a_blocks, a_list, a_count, b_blocks, b_list, b_count)


def solution(mesh):
    in_specs = (
        P("alpha", "beta"),
        P(None, "alpha", None, None),
        P(),
        P(),
        P(None, "beta", None, None),
        P(),
        P(),
    )
    out_specs = P("alpha", "beta")
    return jax.shard_map(
        on_device, mesh=mesh, in_specs=in_specs, out_specs=out_specs, check_vma=False
    )
```
